32 devices in a mesh: dp: 16 (over z, y, x), mp: 2 (over core).
Axes of the slice: x: 2, y: 2, z: 4, core: 2. Of those that a mesh axis runs over, the one named last changes fastest.
Arguments:
- tokens: bfloat16 [32768, 768], P(('dp', 'mp')), may hold values from -6 to 6
- out_grad: bfloat16 [32768, 768], P(('dp', 'mp')), may hold values from -6 to 6
- image_lengths: int32 [16, 69], P('dp'), may hold values from 0 to 98, as said below
- group_of_block: int32 [16], P('dp'), may hold values from 0 to 2, as said below
- norm_gains: float32 [2, 768], replicated, may hold values from 0.5 to 1.5
- row_biases: float32 [4, 768], replicated, may hold values from -1.5 to 1.5
- w_qkv: bfloat16 [3, 768, 768], P(None, None, 'mp'), may hold values from -0.21875 to 0.21875
- qv_bias: float32 [2, 768], P(None, 'mp'), may hold values from -1.5 to 1.5
- w_out: bfloat16 [768, 768], P('mp'), may hold values from -0.875 to 0.875
- w_fc1: bfloat16 [768, 3072], P(None, 'mp'), may hold values from -0.21875 to 0.21875
- b_fc1: float32 [3072], P('mp'), may hold values from -1.5 to 1.5
- w_fc2: bfloat16 [3072, 768], P('mp'), may hold values from -0.109375 to 0.109375
Outputs:
- output: bfloat16 [32768, 768], P(('dp', 'mp'))
- tokens_grad: float32 [32768, 768], P(('dp', 'mp'))
- norm_gains_grad: float32 [2, 768], replicated
- row_biases_grad: float32 [4, 768], replicated
- w_qkv_grad: float32 [3, 768, 768], P(None, None, 'mp')
- qv_bias_grad: float32 [2, 768], P(None, 'mp')
- w_out_grad: float32 [768, 768], P('mp')
- w_fc1_grad: float32 [768, 3072], P(None, 'mp')
- b_fc1_grad: float32 [3072], P('mp')
- w_fc2_grad: float32 [3072, 768], P('mp')
The draws below stay inside these ranges and needn't reach their ends.
Inputs may be any that keep to these rules, and one draw needn't show every extreme that they name: `image_lengths`: row b lists the patch counts of the images packed in block b from the first slot on; each image has 30 to 98 patches, slots after the last image hold 0, the counts of a row sum to at most 2048 and the rest of the block is padding; every block has an image of 98 patches. `group_of_block`: entry b is the dataset group of block b; it never falls along the blocks, and each of the 3 groups holds at least one block.
All inputs are finite; a program needn't handle non-finite values.
Results may differ from the reference program's by a relative error of at most 0.015.
Values may be sent and summed in bfloat16 or wider, within the bound.
No kernel may reach another device: no remote copies, remote signals or barrier semaphores. Data moves between devices by JAX's collectives and lax.ppermute only.
A program may use at most 256 MiB of HBM per device.

```python
import jax
import jax.numpy as jnp
from jax import lax

D = 768
HEADS = 12
HEAD_DIM = 64
FF = 3072
ROWS = 2048
GROUPS = 3
LEN_NORM = 64
SLOTS = 69
TOKENS = 32768
N_DP = 16


def draw_image_lengths(key, part):
    first_key, second_key = jax.random.split(key)
    counts = jax.random.randint(first_key, (N_DP, SLOTS), 30, 99)
    longest = jax.random.randint(second_key, (N_DP, 1), 0, 2)
    slot_ids = jnp.arange(SLOTS, dtype=jnp.int32)[None, :]
    counts = jnp.where(slot_ids == longest, 98, counts)
    image_ends = jnp.cumsum(counts, axis=1)
    return jnp.where(image_ends <= ROWS, counts, 0).astype(jnp.int32)


def draw_group_of_block(key, part):
    first_key, second_key = jax.random.split(key)
    middle = N_DP // 2
    cut_one = jax.random.randint(first_key, (), 1, middle)
    cut_two = jax.random.randint(second_key, (), middle + 1, N_DP)
    position = jnp.arange(N_DP, dtype=jnp.int32)
    return ((position >= cut_one).astype(jnp.int32) + (position >= cut_two).astype(jnp.int32)).astype(jnp.int32)


def steps_of(stream_key, extent, cuts, low, largest):
    factor_of, own = 1.0, jax.random.fold_in(stream_key, 6)
    for axis_at, shards_of in cuts:
        heights = jnp.exp(jax.random.uniform(jax.random.fold_in(own, axis_at), (shards_of,), jnp.float32, low / len(cuts), largest / len(cuts)))
        factor_of = factor_of * jnp.repeat(heights, extent[axis_at] // shards_of).reshape([-1 if axis == axis_at else 1 for axis in range(len(extent))])
    return factor_of


def noise(stream_key, extent, scale, reach, cuts=(), held_as=jnp.bfloat16):
    array = scale * jax.random.normal(stream_key, extent, jnp.float32)
    if cuts:
        array = array * steps_of(stream_key, extent, cuts, -0.22, 0.18)
    return jnp.clip(array, -reach, reach).astype(held_as)


def setup_inputs(seed: int = 0) -> dict:
    streams_of = jax.random.split(jax.random.key(seed), 13)
    tokens = noise(streams_of[0], (TOKENS, D), 1.0, 6.0, ((0, 32),))
    out_grad = noise(streams_of[1], (TOKENS, D), 1.0, 6.0, ((0, 32),))
    image_lengths = draw_image_lengths(jax.random.fold_in(streams_of[12], 71), 0)
    group_of_block = draw_group_of_block(jax.random.fold_in(streams_of[12], 71), 0)
    norm_gains = jnp.clip(1.0 + 0.1 * jax.random.normal(streams_of[4], (2, D), jnp.float32), 0.5, 1.5)
    row_biases = noise(streams_of[5], (4, D), 0.3, 1.5, (), jnp.float32)
    w_qkv = noise(streams_of[6], (3, D, D), D ** -0.5, 0.21875, ((2, 2),))
    qv_bias = noise(streams_of[7], (2, D), 0.3, 1.5, ((1, 2),), jnp.float32)
    w_out = noise(streams_of[8], (D, D), (D // 16) ** -0.5, 0.875, ((0, 2),))
    w_fc1 = noise(streams_of[9], (D, FF), D ** -0.5, 0.21875, ((1, 2),))
    b_fc1 = noise(streams_of[10], (FF,), 0.3, 1.5, ((0, 2),), jnp.float32)
    w_fc2 = noise(streams_of[11], (FF, D), FF ** -0.5, 0.109375, ((0, 2),))
    return dict(tokens=tokens, out_grad=out_grad, image_lengths=image_lengths, group_of_block=group_of_block, norm_gains=norm_gains, row_biases=row_biases, w_qkv=w_qkv, qv_bias=qv_bias, w_out=w_out, w_fc1=w_fc1, b_fc1=b_fc1, w_fc2=w_fc2)


@jax.custom_vjp
def low(v):
    return lax.optimization_barrier(v.astype(jnp.bfloat16)).astype(jnp.float32)

@jax.custom_vjp
def low_back(v):
    return v

def low_keep(v):
    return (low(v), None)

def low_pass(kept, grad):
    return (grad,)

def back_keep(v):
    return (v, None)

def back_low(kept, grad):
    return (low(grad),)
low.defvjp(low_keep, low_pass)
low_back.defvjp(back_keep, back_low)

def layer_norm(values, gain_vec, shift_vec):
    center = values - lax.optimization_barrier(jnp.mean(values, axis=-1, keepdims=True))
    spread = lax.optimization_barrier(jnp.mean(center * center, axis=-1, keepdims=True))
    return center * lax.rsqrt(spread + 1e-06) * gain_vec + shift_vec

def gelu_tanh(values):
    return 0.5 * values * (1.0 + jnp.tanh(0.7978845608028654 * (values + 0.044715 * values * values * values)))

def image_rows(lengths, row_count):
    image_ends = jnp.cumsum(lengths)
    position = jnp.arange(row_count, dtype=jnp.int32)
    segment = lax.optimization_barrier(jnp.sum((position[:, None] >= image_ends[None, :]).astype(jnp.int32), axis=1))
    slot_ids = jnp.arange(lengths.shape[0], dtype=jnp.int32)
    row_length = lax.optimization_barrier(jnp.sum(jnp.where(segment[:, None] == slot_ids[None, :], lengths[None, :], 0), axis=1))
    return (segment, row_length)

def attend(queries, keys_all, values_all, segment):
    row_count, head_count, head_dim = queries.shape
    block_rows = min(512, row_count)
    score_scale = head_dim ** (-0.5)

    def one_block(pieces):
        query_block, segment_block = pieces
        scores = jnp.einsum('qhd,khd->hqk', query_block, keys_all, precision=lax.Precision.HIGHEST) * score_scale
        scores = low_back(scores)
        scores = jnp.where((segment_block[:, None] == segment[None, :])[None], scores, -1000000000.0)
        top_score = lax.optimization_barrier(jnp.max(scores, axis=-1, keepdims=True))
        exponent = jnp.exp(scores - top_score)
        weights = low(exponent / lax.optimization_barrier(jnp.sum(exponent, axis=-1, keepdims=True)))
        return jnp.einsum('hqk,khd->qhd', weights, values_all, precision=lax.Precision.HIGHEST)
    blocks = (queries.reshape(row_count // block_rows, block_rows, head_count, head_dim), segment.reshape(row_count // block_rows, block_rows))
    return lax.map(jax.checkpoint(one_block), blocks).reshape(row_count, head_count * head_dim)

def forward_block(tokens_f, segment, norm_gains, row_biases, w_qkv, qv_bias, w_out, w_fc1, b_fc1, w_fc2):
    normed = low(layer_norm(tokens_f, norm_gains[0], row_biases[0]))
    projected = jnp.einsum('rd,tde->tre', normed, w_qkv, precision=lax.Precision.HIGHEST)
    bias_three = jnp.stack([qv_bias[0], jnp.zeros_like(qv_bias[0]), qv_bias[1]])
    projected = low_back(low(projected + bias_three[:, None, :]))
    row_count = tokens_f.shape[0]
    shaped = projected.reshape(3, row_count, HEADS, HEAD_DIM)
    context = attend(shaped[0], shaped[1], shaped[2], segment)
    context = low_back(low(context))
    hidden_one = tokens_f + low_back(jnp.dot(context, w_out, precision=lax.Precision.HIGHEST)) + row_biases[2]
    normed_two = low(layer_norm(hidden_one, norm_gains[1], row_biases[1]))
    before = low_back(jnp.dot(normed_two, w_fc1, precision=lax.Precision.HIGHEST) + b_fc1)
    activated = low(gelu_tanh(before))
    return hidden_one + low_back(jnp.dot(activated, w_fc2, precision=lax.Precision.HIGHEST)) + row_biases[3]

def reference(tokens, out_grad, image_lengths, group_of_block, norm_gains, row_biases, w_qkv, qv_bias, w_out, w_fc1, b_fc1, w_fc2):
    segment, row_length = jax.vmap(lambda lengths: image_rows(lengths, ROWS))(image_lengths)
    images = lax.optimization_barrier(jnp.sum((image_lengths > 0).astype(jnp.float32), axis=1))
    member = (group_of_block[:, None] == jnp.arange(GROUPS, dtype=jnp.int32)[None, :]).astype(jnp.float32)
    group_images = lax.optimization_barrier(jnp.sum(images[:, None] * member, axis=0))
    group_roots = jnp.sqrt(group_images)
    factor = jnp.sum(group_images) / (group_roots * jnp.sum(group_roots))
    block_factor = lax.optimization_barrier(jnp.sum(member * factor[None, :], axis=1))
    live_rows = (row_length > 0).astype(jnp.float32)
    weight_row = block_factor[:, None] * LEN_NORM * live_rows / jnp.maximum(row_length, 1).astype(jnp.float32)
    cotangent = out_grad.astype(jnp.float32).reshape(N_DP, ROWS, D) * weight_row[:, :, None]
    params = (norm_gains, row_biases, w_qkv.astype(jnp.float32), qv_bias, w_out.astype(jnp.float32), w_fc1.astype(jnp.float32), b_fc1, w_fc2.astype(jnp.float32))

    def forward(inputs, weights):

        def one_pack(pieces):
            return forward_block(pieces[0], pieces[1], *weights)
        return lax.map(jax.checkpoint(one_pack), (inputs, segment))
    output, pullback = jax.vjp(forward, tokens.astype(jnp.float32).reshape(N_DP, ROWS, D), params)
    input_grad, weight_grads = pullback(cotangent)
    return (output.reshape(TOKENS, D).astype(jnp.bfloat16), input_grad.reshape(TOKENS, D), weight_grads[0], weight_grads[1], weight_grads[2], weight_grads[3], weight_grads[4], weight_grads[5], weight_grads[6], weight_grads[7])
```

```python
import functools

import jax
import jax.numpy as jnp
from jax import lax
from jax.experimental import pallas as pl
from jax.experimental.pallas import tpu as pltpu
from jax.sharding import PartitionSpec as P

TILE = 128
MASKED = -3e38
F32 = jnp.float32
BF16 = jnp.bfloat16

def pick_heads(block):
    lane = lax.broadcasted_iota(jnp.int32, block.shape, 1)
    zero = jnp.zeros_like(block)
    return jnp.concatenate([jnp.where(lane < 64, block, zero), jnp.where(lane < 64, zero, block)], axis=0)

def join_heads(both):
    half = both.shape[1] // 2
    row = lax.broadcasted_iota(jnp.int32, (both.shape[0], half), 0)
    return jnp.where(row < 64, both[:, :half], both[:, half:]).T

def window(tiles, i):
    return [pl.multiple_of(lax.rem(i + step, tiles) * TILE, TILE) for step in (tiles - 1, 0, 1)]

def bias_of(starts, seg_col_ref, seg_row):
    keys = jnp.concatenate([seg_col_ref[pl.ds(s, TILE), :] for s in starts], axis=0)
    bias = jnp.where(keys == seg_row, 0.0, MASKED).astype(F32)
    return jnp.concatenate([bias, bias], axis=1)

def rows_of(ref, starts, cols):
    return jnp.concatenate([ref[pl.ds(s, TILE), cols] for s in starts], axis=0)


HEAD_DIM = 64
GROUPS = 3
LEN_NORM = 64
EPS = 1e-06
GELU_C = 0.7978845608028654
VMEM = pl.BlockSpec(memory_space=pltpu.VMEM)
SMEM = pl.BlockSpec(memory_space=pltpu.SMEM)
ANY = pl.BlockSpec(memory_space=pl.ANY)


def dot(a, b):
    return jnp.dot(a, b, preferred_element_type=F32)


def dot_nt(a, b):
    return lax.dot_general(a, b, (((1,), (1,)), ((), ())), preferred_element_type=F32)


def dot_tn(a, b):
    return lax.dot_general(a, b, (((0,), (0,)), ((), ())), preferred_element_type=F32)


def shape_of(shape, dtype):
    return jax.ShapeDtypeStruct(shape, dtype)


def nbytes(a):
    size = a.dtype.itemsize
    for n in a.shape:
        size *= n
    return size


COST_SHARE = 4


class Order:
    token = None
    after = ()


def call(body, args, outs, flops=0, scratch=(), limit=12, scalars=0, places=None, out_places=None):
    outs = list(outs)
    waits = [a for a in (Order.token, *Order.after) if a is not None]
    Order.after = ()
    places = [SMEM] * scalars + [VMEM] * (len(args) - scalars) if places is None else places
    n_in, n_wait, n_out = len(args), len(waits), len(outs)

    def tied(*refs):
        token_ref = refs[n_in + n_wait + n_out]
        token_ref[...] = jnp.zeros_like(token_ref)
        body(*refs[:n_in], *refs[n_in + n_wait : n_in + n_wait + n_out], *refs[n_in + n_wait + n_out + 1 :])

    *results, Order.token = pl.pallas_call(
        tied,
        in_specs=list(places) + [ANY] * n_wait,
        out_specs=(list(out_places) if out_places else [VMEM] * n_out) + [VMEM],
        out_shape=outs + [shape_of((8, 128), F32)],
        scratch_shapes=list(scratch),
        compiler_params=pltpu.CompilerParams(vmem_limit_bytes=limit << 20),
        cost_estimate=pl.CostEstimate(flops=1, bytes_accessed=sum(nbytes(a) for a in [*args, *outs]) // COST_SHARE, transcendentals=0),
    )(*args, *waits)
    return results


def after(*arrays):
    Order.after = arrays


def norm_parts(values):
    center = values - jnp.mean(values, axis=-1, keepdims=True)
    rstd = lax.rsqrt(jnp.mean(center * center, axis=-1, keepdims=True) + EPS)
    return center * rstd, rstd


def norm_back(grad, unit, rstd, gain):
    scaled = grad * gain
    return rstd * (
        scaled
        - jnp.mean(scaled, axis=-1, keepdims=True)
        - unit * jnp.mean(scaled * unit, axis=-1, keepdims=True)
    )


def fold(a):
    return jnp.sum(a.astype(F32), axis=0, keepdims=True)


def prep_body(core_ref, group_ref, lengths_ref, grad_ref, col_ref, row_ref, len_ref, count_ref, low_ref):
    ext, own = col_ref.shape[0], len_ref.shape[0]
    slots = lengths_ref.shape[1]
    pad = jnp.zeros((1, 128 - slots), F32)
    lengths = jnp.concatenate([lengths_ref[...].astype(F32), pad], axis=1)
    before = lax.broadcasted_iota(jnp.int32, (128, 128), 0) <= lax.broadcasted_iota(jnp.int32, (128, 128), 1)
    ends = dot(jnp.broadcast_to(lengths, (8, 128)).astype(BF16), jnp.where(before, 1.0, 0.0).astype(BF16))[0:1]
    lane = lax.broadcasted_iota(jnp.int32, (1, 128), 1)
    ends = jnp.where(lane < slots, ends, 1e9)
    row = lax.broadcasted_iota(jnp.int32, (ext, 1), 0)
    core = core_ref[0]
    edge = jnp.where(core == 0, 0, -own - (ext - own))
    position = row + jnp.where(row < own, core * own, edge + core * own)
    past = jnp.where(position.astype(F32) >= ends, 1.0, 0.0)
    segment = jnp.sum(past, axis=1, keepdims=True)
    col_ref[...] = segment
    row_ref[...] = dot_nt(jnp.ones((8, 128), BF16), past.astype(BF16))[0:1]
    hit = jnp.where(segment[:own] == lane.astype(F32), lengths, 0.0)
    length = jnp.sum(hit, axis=1, keepdims=True)
    weight = jnp.where(length > 0, LEN_NORM / jnp.maximum(length, 1.0), 0.0)
    len_ref[...] = weight
    low_ref[...] = (grad_ref[...].astype(F32) * weight).astype(BF16)
    images = jnp.sum(jnp.where(lengths > 0, 1.0, 0.0), axis=1, keepdims=True)
    count_ref[...] = jnp.zeros_like(count_ref)
    count_ref[0:1, 0:128] = jnp.where(lane == group_ref[0], images, 0.0)


def prep_call(core, group, lengths, out_grad):
    own, width = out_grad.shape
    ext = own + TILE
    return call(
        prep_body,
        (core, group, lengths, out_grad),
        [
            shape_of((ext, 1), F32),
            shape_of((1, ext), F32),
            shape_of((own, 1), F32),
            shape_of((16, width), F32),
            shape_of((own, width), BF16),
        ],
        scalars=2,
    )


def factor_body(group_ref, counts_ref, factor_ref):
    lane = lax.broadcasted_iota(jnp.int32, (1, 128), 1)
    counts = jnp.where(lane < GROUPS, fold(counts_ref[:, :128]) * 0.5, 0.0)
    roots = jnp.sqrt(counts)
    all_images = jnp.sum(counts, axis=1, keepdims=True)
    all_roots = jnp.sum(roots, axis=1, keepdims=True)
    root = jnp.sum(jnp.where(lane == group_ref[0], roots, 0.0), axis=1, keepdims=True)
    factor_ref[...] = jnp.broadcast_to(all_images / (root * all_roots), factor_ref.shape)


def factor_call(group, counts):
    return call(factor_body, (group, counts), [shape_of((8, 128), F32)], scalars=1)[0]


def qkv_body(tokens_ref, halo_ref, gains_ref, biases_ref, w_ref, w2_ref, b_ref, b2_ref, normed_ref, out_ref):
    own, width = tokens_ref.shape
    ext = normed_ref.shape[0]
    for r, ref in [(r, tokens_ref) for r in range(0, own, 256)] + [(own, halo_ref)]:
        n = min(256, ext - r)
        at = 0 if ref is halo_ref else r
        unit, _ = norm_parts(ref[at : at + n, :].astype(F32))
        normed = (unit * gains_ref[0:1, :] + biases_ref[0:1, :]).astype(BF16)
        normed_ref[r : r + n, :] = normed
        for t in range(3):
            weights = jnp.concatenate([w_ref[t], w2_ref[t]], axis=1)
            part = dot(normed, weights)
            if t != 1:
                row = t // 2
                part = part + jnp.concatenate([b_ref[row : row + 1, :], b2_ref[row : row + 1, :]], axis=1)
            out_ref[r : r + n, t * width : (t + 1) * width] = part.astype(BF16)


def qkv_call(tokens, halo, gains, biases, w, w2, b, b2):
    own, width = tokens.shape
    ext = own + halo.shape[0]
    return call(
        qkv_body,
        (tokens, halo, gains, biases, w, w2, b, b2),
        [shape_of((ext, width), BF16), shape_of((ext, 3 * width), BF16)],
        6 * ext * width * width,
    )


def out_norm_body(ctx_ref, tok_ref, w_ref, w2_ref, gains_ref, biases_ref, hid_ref, norm_ref):
    weights = jnp.concatenate([w_ref[...], w2_ref[...]], axis=0)
    own = tok_ref.shape[0]
    product = lambda r: dot(ctx_ref[r : r + 256, :], weights)
    ready = product(0)
    for r in range(0, own, 256):
        later = product(r + 256) if r + 256 < own else None
        rows = slice(r, r + 256)
        hidden = tok_ref[rows, :].astype(F32) + ready + biases_ref[2:3, :]
        hid_ref[rows, :] = hidden
        unit, _ = norm_parts(hidden)
        norm_ref[rows, :] = (unit * gains_ref[1:2, :] + biases_ref[1:2, :]).astype(BF16)
        ready = later


def out_norm_call(ctx, tokens, w, w2, gains, biases):
    rows, width = tokens.shape
    return call(
        out_norm_body,
        (ctx, tokens, w, w2, gains, biases),
        [shape_of((rows, width), F32), shape_of((rows, width), BF16)],
        2 * rows * width * width,
    )


def ffn_body(x_ref, g_ref, w_ref, w2_ref, b_ref, b2_ref, v_ref, v2_ref, act_ref, gb_ref, sum_ref, *, step=256, cols=256):
    half = w_ref.shape[1]
    sum_ref[...] = jnp.zeros_like(sum_ref)

    def products(rows, j):
        up, bias, down, at = (w_ref, b_ref, v_ref, j) if j < half else (w2_ref, b2_ref, v2_ref, j - half)
        v = dot(x_ref[rows, :], up[:, at : at + cols]) + bias[:, at : at + cols]
        return v, dot_nt(g_ref[rows, :], down[at : at + cols, :])

    def finish(rows, j, v, grad):
        u = v * v
        gate = 0.5 * jnp.tanh(v * (GELU_C + (GELU_C * 0.044715) * u)) + 0.5
        act = v * gate
        act_ref[rows, j : j + cols] = act.astype(BF16)
        slope = gate + act * (1.0 - gate) * (2 * GELU_C + (GELU_C * 6 * 0.044715) * u)
        low = (grad * slope).astype(BF16)
        gb_ref[rows, j : j + cols] = low
        sum_ref[:, j : j + cols] += fold(low)

    def one(i, _):
        rows = pl.ds(pl.multiple_of(i * step, step), step)
        ready = products(rows, 0)
        for j in range(0, 2 * half, cols):
            later = products(rows, j + cols) if j + cols < 2 * half else None
            finish(rows, j, *ready)
            ready = later
        return 0

    lax.fori_loop(0, x_ref.shape[0] // step, one, 0)


def ffn_call(x, g, w, w2, b, b2, v, v2, step=256, cols=256):
    rows, width = x.shape
    hidden = 2 * w.shape[1]
    return call(
        functools.partial(ffn_body, step=step, cols=cols),
        (x, g, w, w2, b, b2, v, v2),
        [shape_of((rows, hidden), BF16), shape_of((rows, hidden), BF16), shape_of((1, hidden), F32)],
        4 * rows * width * hidden,
        limit=12,
    )


def fc2_grad_body(act_ref, low_ref, own_ref, other_ref):
    half = own_ref.shape[0]
    for r in range(0, half, 256):
        other_ref[r : r + 256, :] = dot_tn(act_ref[:, half + r : half + r + 256], low_ref[...]).astype(BF16)
    for r in range(0, half, 256):
        own_ref[r : r + 256, :] = dot_tn(act_ref[:, r : r + 256], low_ref[...])


def fc1_grad_body(x_ref, gb_ref, own_ref, other_ref):
    half = own_ref.shape[1]
    for r in range(0, x_ref.shape[1], 256):
        left = x_ref[:, r : r + 256]
        other_ref[r : r + 256, :] = dot_tn(left, gb_ref[:, half:]).astype(BF16)
        own_ref[r : r + 256, :] = dot_tn(left, gb_ref[:, :half])


def early_grad_body(ctx_ref, low_ref, norm_ref, ga_ref, own_ref, other_ref):
    half = own_ref.shape[1]
    own = low_ref.shape[0]
    for h in range(2):
        cols, at = slice(h * half, (h + 1) * half), 2 * h * half
        other_ref[at : at + half, :] = dot_tn(ctx_ref[:, half:], low_ref[:, cols]).astype(BF16)
        own_ref[at : at + half, :] = dot_tn(ctx_ref[:, :half], low_ref[:, cols])
        both = dot_tn(norm_ref[:own, cols], ga_ref[...])
        own_ref[at + half : at + 2 * half, :] = both[:, :half]
        other_ref[at + half : at + 2 * half, :] = both[:, half:].astype(BF16)


def late_grad_body(norm_ref, gb_ref, own_ref, other_ref):
    own, width = gb_ref.shape[0], own_ref.shape[1]
    for r in range(0, own_ref.shape[0], 256):
        both = dot_tn(norm_ref[:own, r : r + 256], gb_ref[...])
        own_ref[r : r + 256, :] = both[:, :width]
        other_ref[r : r + 256, :] = both[:, width:].astype(BF16)


def grad_call(body, shape, flops, *args):
    return call(body, args, [shape_of(shape, F32), shape_of(shape, BF16)], flops)


def grad_hidden_body(gb_ref, w_ref, w2_ref, hid_ref, og_ref, wr_ref, gains_ref, gh_ref, low_ref, sums_ref):
    half = w_ref.shape[1]

    def product(r):
        rows = slice(r, r + 256)
        return dot_nt(gb_ref[rows, :half], w_ref[...]) + dot_nt(gb_ref[rows, half:], w2_ref[...])

    own = hid_ref.shape[0]
    ready, sums = product(0), [0.0] * 4
    for r in range(0, own, 256):
        later = product(r + 256) if r + 256 < own else None
        rows, grad = slice(r, r + 256), ready
        unit, rstd = norm_parts(hid_ref[rows, :])
        cot = og_ref[rows, :].astype(F32) * wr_ref[rows, :]
        hidden = norm_back(grad, unit, rstd, gains_ref[1:2, :]) + cot
        gh_ref[rows, :] = hidden
        low_ref[rows, :] = hidden.astype(BF16)
        sums = [a + fold(b) for a, b in zip(sums, (grad * unit, grad, hidden, cot))]
        ready = later
    for row, a in enumerate(sums):
        sums_ref[row : row + 1, :] = a


def grad_hidden_call(gb, w, w2, hidden, out_grad, weight_col, gains):
    rows, width = hidden.shape
    return call(
        grad_hidden_body,
        (gb, w, w2, hidden, out_grad, weight_col, gains),
        [shape_of((rows, width), F32), shape_of((rows, width), BF16), shape_of((8, width), F32)],
        2 * rows * width * gb.shape[1],
    )


def gctx_body(x_ref, h_ref, w_ref, w2_ref, out_ref):
    own = x_ref.shape[0]
    for r in range(0, own, 256):
        weights = jnp.concatenate([w_ref[...], w2_ref[...]], axis=0)
        out_ref[r : r + 256, :] = dot_nt(x_ref[r : r + 256, :], weights).astype(BF16)
    weights = jnp.concatenate([w_ref[...], w2_ref[...]], axis=0)
    out_ref[own:, :] = dot_nt(h_ref[...], weights).astype(BF16)


def gctx_call(x, h, w, w2):
    rows, width = x.shape
    ext = rows + h.shape[0]
    return call(
        gctx_body,
        (x, h, w, w2),
        [shape_of((ext, width), BF16)],
        2 * ext * width * width,
    )[0]


def grad_tokens_body(ga_ref, gb_ref, w_ref, w2_ref, tok_ref, gh_ref, gains_ref, two_ref, fc1_ref, factor_ref, out_ref, sums_ref):
    factor = factor_ref[0:1, 0:1]
    width = tok_ref.shape[1]
    half = w_ref.shape[2]
    sums_ref[...] = jnp.zeros_like(sums_ref)
    sums_ref[2:6, :] = two_ref[0:4, :]
    for r in range(4):
        sums_ref[9 + r : 10 + r, :] = fc1_ref[:, r * width : (r + 1) * width]

    def product(r):
        grad = jnp.zeros((256, width), F32)
        for ref, lo, hi in ((ga_ref, 0, TILE), (gb_ref, TILE, half)):
            weights = [w[t, :, lo:hi] for w in (w_ref, w2_ref) for t in range(3)]
            grad = grad + dot_nt(ref[r : r + 256, :], jnp.concatenate(weights, axis=1))
        return grad

    own = tok_ref.shape[0]
    ready, sums = product(0), [0.0] * 5
    for r in range(0, own, 256):
        later = product(r + 256) if r + 256 < own else None
        rows, grad = slice(r, r + 256), ready
        unit, rstd = norm_parts(tok_ref[rows, :].astype(F32))
        out_ref[rows, :] = (norm_back(grad, unit, rstd, gains_ref[0:1, :]) + gh_ref[rows, :]) * factor
        terms = (grad * unit, grad, ga_ref[rows, :], gb_ref[rows, :width], gb_ref[rows, width:])
        sums = [a + fold(b) for a, b in zip(sums, terms)]
        ready = later
    for row, a in zip((0, 1, 6, 7, 8), sums):
        sums_ref[row : row + 1, :] = a
    sums_ref[...] = sums_ref[...] * factor


def grad_tokens_call(ga, gb, w, w2, tokens, grad_hidden, gains, two, fc1, factor):
    rows, width = tokens.shape
    return call(
        grad_tokens_body,
        (ga, gb, w, w2, tokens, grad_hidden, gains, two, fc1, factor),
        [shape_of((rows, width), F32), shape_of((16, width), F32)],
        6 * rows * width * width,
    )


def vectors_body(core_ref, all_ref, gains_ref, shifts_ref, qv_ref, fc1_ref):
    blocks = all_ref.shape[0] // 32
    width = all_ref.shape[1]
    half = qv_ref.shape[1]
    total = all_ref[0:32, :]
    for b in range(1, blocks):
        total = total + all_ref[32 * b : 32 * (b + 1), :]
    mine = jnp.where(core_ref[0] == 0, total[:16], total[16:])
    peer = jnp.where(core_ref[0] == 0, total[16:], total[:16])
    both = mine + peer
    gains_ref[0:1, :] = both[0:1]
    gains_ref[1:2, :] = both[2:3]
    shifts_ref[0:1, :] = both[1:2]
    shifts_ref[1:4, :] = both[3:6]
    small = mine[6:7, :half] + peer[6:7, half:]
    large = mine[7:8] + peer[8:9]
    for row, t in ((0, 0), (1, 2)):
        qv_ref[row : row + 1, :TILE] = small[:, t * TILE : (t + 1) * TILE]
        qv_ref[row : row + 1, TILE:] = large[:, t * 2 * TILE : (t + 1) * 2 * TILE]
    for r in range(2):
        fc1_ref[:, r * width : (r + 1) * width] = mine[9 + r : 10 + r] + peer[11 + r : 12 + r]


def vectors_call(core, everything, half, hidden_half):
    width = everything.shape[1]
    return call(
        vectors_body,
        (core, everything),
        [shape_of((2, width), F32), shape_of((4, width), F32), shape_of((2, half), F32), shape_of((1, hidden_half), F32)],
        scalars=1,
    )


def output_body(a_ref, w_ref, w2_ref, hid_ref, biases_ref, out_ref):
    half = w_ref.shape[0]
    for r in range(0, hid_ref.shape[0], 256):
        rows = slice(r, r + 256)
        mlp = dot(a_ref[rows, :half], w_ref[...]) + dot(a_ref[rows, half:], w2_ref[...])
        out_ref[rows, :] = (hid_ref[rows, :] + mlp + biases_ref[3:4, :]).astype(BF16)


def output_call(a, w, w2, hidden, biases):
    rows, width = hidden.shape
    return call(
        output_body,
        (a, w, w2, hidden, biases),
        [shape_of((rows, width), BF16)],
        2 * rows * width * a.shape[1],
    )[0]


def attn_fwd_body(
    place_ref,
    qkv_ref,
    seg_col_ref,
    seg_row_ref,
    normed_ref,
    other_ref,
    gains_ref,
    biases_ref,
    w_ref,
    w2_ref,
    b_ref,
    b2_ref,
    out_ref,
    far_ref,
    wide_ref,
    keys_ref,
    values_ref,
    weight_ref,
    sem,
    *,
    tiles,
    scale,
):
    own, width = out_ref.shape

    pairs = width // TILE
    lane = lax.broadcasted_iota(jnp.int32, (TILE, TILE), 1)

    def one(i, _):
        starts = window(tiles, i)
        here = pl.ds(starts[1], TILE)
        bias = bias_of(starts, seg_col_ref, seg_row_ref[:, here])
        cols = lambda t, p: slice(t * width + p * TILE, t * width + (p + 1) * TILE)
        scores, probs = {}, {}
        for step in range(pairs + 2):
            if step < pairs:
                queries = pick_heads(qkv_ref[here, cols(0, step)] * jnp.asarray(scale, BF16))
                scores[step] = dot_nt(rows_of(qkv_ref, starts, cols(1, step)), queries) + bias
            p = step - 1
            if 0 <= p < pairs:
                expo = jnp.exp(scores[p] - jnp.max(scores[p], axis=0, keepdims=True))
                probs[p] = (expo * (1.0 / jnp.sum(expo, axis=0, keepdims=True))).astype(BF16)
            p = step - 2
            if 0 <= p < pairs:
                both = dot_tn(probs[p], rows_of(qkv_ref, starts, cols(2, p)))
                out_ref[here, cols(0, p)] = jnp.where(lane < HEAD_DIM, both[:TILE], both[TILE:]).astype(BF16)
        return 0

    lax.fori_loop(0, own // TILE, one, 0)
    total_rows, first_row = place_ref[0], place_ref[1]

    @pl.when(total_rows < 2 * own - TILE)
    def _():
        load = pltpu.make_async_copy(other_ref, far_ref, sem)
        load.start()
        load.wait()

        @pl.loop(0, own // TILE)
        def _(i):
            rows = pl.ds(pl.multiple_of(i * TILE, TILE), TILE)
            unit, _ = norm_parts(far_ref[rows, :].astype(F32))
            far_ref[rows, :] = (unit * gains_ref[0:1, :] + biases_ref[0:1, :]).astype(BF16)

        key_row = lax.broadcasted_iota(jnp.int32, (2 * own, 1), 0) + first_row
        key_row = jnp.where(key_row >= 2 * own, key_row - 2 * own, key_row)
        wide_ref[...] = jnp.where(key_row >= total_rows, 0.0, MASKED)
        for side, (wide, bias_ref) in enumerate(((w_ref, b_ref), (w2_ref, b2_ref))):
            half = wide.shape[2]

            @pl.loop(0, half // TILE)
            def _(p):
                at = pl.multiple_of(p * TILE, TILE)
                base = pl.multiple_of(side * half + p * TILE, TILE)
                for t, ref in ((1, keys_ref), (2, values_ref)):
                    load = pltpu.make_async_copy(wide.at[t, :, pl.ds(at, TILE)], weight_ref, sem)
                    load.start()
                    load.wait()
                    ref[:own, :] = qkv_ref[:own, pl.ds(pl.multiple_of(t * width + base, TILE), TILE)]
                    part = dot(far_ref[...], weight_ref[...])
                    if t == 2:
                        part = part + bias_ref[1:2, pl.ds(at, TILE)]
                    ref[own:, :] = part.astype(BF16)

                @pl.loop(0, own // TILE)
                def _(i):
                    rows = pl.ds(pl.multiple_of(i * TILE, TILE), TILE)
                    queries = pick_heads(qkv_ref[rows, pl.ds(base, TILE)] * jnp.asarray(scale, BF16))
                    scores = dot_nt(keys_ref[...], queries) + wide_ref[...]
                    top = jnp.max(scores, axis=0, keepdims=True)
                    expo = jnp.exp(scores - top)
                    probs = (expo * (1.0 / jnp.sum(expo, axis=0, keepdims=True))).astype(BF16)
                    full = join_heads(dot_tn(values_ref[...], probs)).astype(BF16)
                    row = lax.broadcasted_iota(jnp.int32, (TILE, TILE), 0) + i * TILE + first_row
                    out_ref[rows, pl.ds(base, TILE)] = jnp.where(row >= total_rows, full, out_ref[rows, pl.ds(base, TILE)])


def attn_fwd(place, qkv, seg_col, seg_row, normed, other, gains, biases, w, w2, b, b2, scale):
    own, width = other.shape
    ext = qkv.shape[0]
    return call(
        functools.partial(attn_fwd_body, tiles=ext // TILE, scale=scale),
        (place, qkv, seg_col, seg_row, normed, other, gains, biases, w, w2, b, b2),
        [shape_of((own, width), BF16)],
        40 * own * 3 * TILE * width,
        scratch=[
            pltpu.VMEM((own, width), BF16),
            pltpu.VMEM((2 * own, 1), F32),
            pltpu.VMEM((2 * own, TILE), BF16),
            pltpu.VMEM((2 * own, TILE), BF16),
            pltpu.VMEM((width, TILE), BF16),
            pltpu.SemaphoreType.DMA(()),
        ],
        limit=8,
        places=[SMEM, VMEM, VMEM, VMEM, ANY, ANY, VMEM, VMEM, ANY, ANY, VMEM, VMEM],
    )[0]


def attn_bwd_body(qkv_ref, g_ref, seg_col_ref, seg_row_ref, out_ref, dq_ref, dk_ref, dv_ref, *, tiles, scale, pairs, turns):
    own, width = out_ref.shape[0], qkv_ref.shape[1] // 3
    dk_ref[...] = jnp.zeros_like(dk_ref)
    dv_ref[...] = jnp.zeros_like(dv_ref)

    def load(starts, here, p):
        cols = lambda t: slice(t * width + p * TILE, t * width + (p + 1) * TILE)
        queries = pick_heads(qkv_ref[here, cols(0)] * jnp.asarray(scale, BF16))
        keys, values = rows_of(qkv_ref, starts, cols(1)), rows_of(qkv_ref, starts, cols(2))
        return queries, keys, values, pick_heads(g_ref[here, cols(0)])

    def products(arrays, bias):
        queries, keys, values, grads = arrays
        return dot_nt(keys, queries) + bias, dot_nt(values, grads)

    def softmax_back(scores, grad_probs):
        expo = jnp.exp(scores - jnp.max(scores, axis=0, keepdims=True))
        probs = expo * (1.0 / jnp.sum(expo, axis=0, keepdims=True))
        mean = jnp.sum(probs * grad_probs, axis=0, keepdims=True)
        return probs.astype(BF16), (probs * (grad_probs - mean)).astype(BF16)

    def finish(starts, here, at, arrays, probs, grad_scores):
        queries, keys, _, grads = arrays
        cols = slice(at * TILE, (at + 1) * TILE)
        dv, dk = dot(probs, grads), dot(grad_scores, queries)
        for k, s in enumerate(starts):
            part = slice(k * TILE, (k + 1) * TILE)
            dk_ref[pl.ds(s, TILE), cols] += dk[part]
            dv_ref[pl.ds(s, TILE), cols] += dv[part]
        dq_ref[here, cols] = (join_heads(dot_tn(keys, grad_scores)) * scale).astype(BF16)

    def one(i, _):
        work = []
        for turn in range(turns):
            starts = window(tiles, i * turns + turn)
            here = pl.ds(starts[1], TILE)
            bias = bias_of(starts, seg_col_ref, seg_row_ref[:, here])
            work += [(starts, here, bias, at, p) for at, p in enumerate(pairs)]
        first, second = {}, {}
        for step in range(len(work) + 2):
            if step < len(work):
                starts, here, bias, at, p = work[step]
                first[step] = products(load(starts, here, p), bias)
            if 0 <= step - 1 < len(work):
                second[step - 1] = softmax_back(*first.pop(step - 1))
            if 0 <= step - 2 < len(work):
                starts, here, bias, at, p = work[step - 2]
                finish(starts, here, at, load(starts, here, p), *second.pop(step - 2))
        return 0

    lax.fori_loop(0, tiles // turns, one, 0)
    half = len(pairs) * TILE // 2
    for side in range(2):
        cols = slice(side * half, (side + 1) * half)
        base = side * 3 * half
        out_ref[:, base : base + half] = dq_ref[:own, cols]
        out_ref[:, base + half : base + 2 * half] = dk_ref[:own, cols].astype(BF16)
        out_ref[:, base + 2 * half : base + 3 * half] = dv_ref[:own, cols].astype(BF16)


def attn_bwd(qkv, g, seg_col, seg_row, own, scale, pairs, turns):
    ext = g.shape[0]
    cols = len(pairs) * TILE
    return call(
        functools.partial(attn_bwd_body, tiles=ext // TILE, scale=scale, pairs=pairs, turns=turns),
        (qkv, g, seg_col, seg_row),
        [shape_of((own, 3 * cols), BF16)],
        100 * own * 3 * TILE * cols,
        scratch=[pltpu.VMEM((ext, cols), BF16), pltpu.VMEM((ext, cols), F32), pltpu.VMEM((ext, cols), F32)],
        limit=14,
    )[0]


def half_of(side_ref, flip):
    return 1 - side_ref[0] if flip else side_ref[0]


def first_split_body(side_ref, kept_ref, got_ref, factor_ref, send_ref, keep_ref):
    half = keep_ref.shape[0]
    factor = factor_ref[0:1, 0:1]
    total = lambda at: (kept_ref[pl.ds(at, half), :] + got_ref[pl.ds(at, half), :].astype(F32)) * factor
    send_ref[...] = total(pl.multiple_of((1 - side_ref[0]) * half, 16)).astype(BF16)
    keep_ref[...] = total(pl.multiple_of(side_ref[0] * half, 16))


def first_split(side, kept, got, factor):
    half, cols = kept.shape[0] // 2, kept.shape[1]
    return call(
        first_split_body,
        (side, kept, got, factor),
        [shape_of((half, cols), BF16), shape_of((half, cols), F32)],
        scalars=1,
    )


def first_add_body(kept_ref, got_ref, factor_ref, out_ref):
    out_ref[...] = ((kept_ref[...] + got_ref[...].astype(F32)) * factor_ref[0:1, 0:1]).astype(BF16)


def first_add(kept, got, factor):
    return call(first_add_body, (kept, got, factor), [shape_of(kept.shape, BF16)])[0]


def split_two_body(side_ref, kept_ref, got_ref, send_ref, keep_ref):
    half = keep_ref.shape[0]
    total = lambda at: kept_ref[pl.ds(at, half), :] + got_ref[pl.ds(at, half), :].astype(F32)
    send_ref[...] = total(pl.multiple_of((1 - side_ref[0]) * half, 16)).astype(BF16)
    keep_ref[...] = total(pl.multiple_of(side_ref[0] * half, 16))


def split_two(side, kept, got):
    half, cols = kept.shape[0] // 2, kept.shape[1]
    return call(
        split_two_body,
        (side, kept, got),
        [shape_of((half, cols), BF16), shape_of((half, cols), F32)],
        scalars=1,
    )


def add_body(kept_ref, got_ref, out_ref):
    out_ref[...] = (kept_ref[...] + got_ref[...].astype(F32)).astype(BF16)


def add_two(kept, got):
    return call(add_body, (kept, got), [shape_of(kept.shape, BF16)])[0]


def join_body(side_ref, own_ref, got_ref, out_ref):
    half = own_ref.shape[0]
    out_ref[pl.ds(pl.multiple_of(side_ref[0] * half, 16), half), :] = own_ref[...]
    out_ref[pl.ds(pl.multiple_of((1 - side_ref[0]) * half, 16), half), :] = got_ref[...]


def join_two(side, own, got):
    half, cols = own.shape
    return call(join_body, (side, own, got), [shape_of((2 * half, cols), BF16)], scalars=1)[0]


def last_body(side_ref, own_ref, got_ref, token_ref, out_ref, done_ref):
    out_ref[side_ref[0]] = own_ref[...].astype(F32)
    out_ref[1 - side_ref[0]] = got_ref[...].astype(F32)
    done_ref[...] = jnp.zeros_like(done_ref)


def last_rows(side, own, got, steps=3):
    rows, cols = own.shape
    n = rows // steps
    out, Order.token = pl.pallas_call(
        last_body,
        grid_spec=pltpu.PrefetchScalarGridSpec(
            num_scalar_prefetch=1,
            grid=(steps,),
            in_specs=[pl.BlockSpec((n, cols), lambda i, s: (i, 0))] * 2 + [ANY],
            out_specs=[
                pl.BlockSpec((2, n, cols), lambda i, s: (0, i, 0)),
                pl.BlockSpec((8, 128), lambda i, s: (0, 0)),
            ],
        ),
        out_shape=[shape_of((2, rows, cols), F32), shape_of((8, 128), F32)],
        compiler_params=pltpu.CompilerParams(vmem_limit_bytes=12 << 20),
        cost_estimate=pl.CostEstimate(flops=1, bytes_accessed=1, transcendentals=0),
    )(side, own, got, Order.token)
    return out.reshape(2 * rows, cols)


def last_qkv_body(side_ref, a0_ref, a1_ref, b0_ref, b1_ref, wout_ref, wqkv_ref):
    half = wout_ref.shape[0]
    for flip, a_ref, b_ref in ((False, a0_ref, b0_ref), (True, a1_ref, b1_ref)):
        part = pl.ds(pl.multiple_of(half_of(side_ref, flip) * half, 128), half)
        wout_ref[:, part] = a_ref[:half, :].astype(F32)
        for t in range(3):
            wqkv_ref[t, part, :TILE] = a_ref[half:, t * TILE : (t + 1) * TILE].astype(F32)
            wqkv_ref[t, part, TILE:] = b_ref[:, t * 2 * TILE : (t + 1) * 2 * TILE].astype(F32)


def last_qkv(side, a0, a1, b0, b1):
    half = a0.shape[1]
    return call(
        last_qkv_body,
        (side, a0, a1, b0, b1),
        [shape_of((half, 2 * half), F32), shape_of((3, 2 * half, half), F32)],
        scalars=1,
    )


def swap(x):
    return lax.ppermute(x, "mp", [(0, 1), (1, 0)])


def exchange(x, bits, n):
    pairs = [(2 * d + m, 2 * (d ^ bits[m]) + m) for d in range(n) for m in range(2)]
    return lax.ppermute(x, ("dp", "mp"), pairs)


def sum_any(part):
    n = lax.axis_size("dp")
    shape = part.shape
    part = part.reshape(-1, shape[-1])
    if n & (n - 1) or part.shape[0] % n:
        return lax.psum(part, "dp").reshape(shape)
    d = lax.axis_index("dp")
    bits = [1 << k for k in range(n.bit_length() - 1)]
    for bit in bits:
        half = part.shape[0] // 2
        side = lax.rem(d // bit, 2)
        sent = lax.dynamic_slice_in_dim(part, (1 - side) * half, half).astype(BF16)
        kept = lax.dynamic_slice_in_dim(part, side * half, half)
        part = kept + exchange(sent, (bit, bit), n).astype(F32)
    total = part.astype(BF16)
    for bit in reversed(bits):
        side = lax.rem(d // bit, 2)
        got = exchange(total, (bit, bit), n)
        total = jnp.concatenate([jnp.where(side == 0, total, got), jnp.where(side == 0, got, total)], axis=0)
    return total.astype(F32).reshape(shape)


STAGES = ((1, 2), (2, 1), (4, 4), (8, 8))


class Bucket:
    def __init__(self, sides, sent, kept):
        self.sides, self.at, self.kept = sides, 0, kept
        self.got = exchange(sent, STAGES[0], 16)

    def step(self):
        self.at += 1
        if self.at < 4:
            sent, self.kept = split_two(self.sides[self.at], self.kept, self.got)
            self.got = exchange(sent, STAGES[self.at], 16)
        elif self.at == 4:
            self.kept = add_two(self.kept, self.got)
            self.got = exchange(self.kept, STAGES[3], 16)
        else:
            stage = 8 - self.at
            self.kept = join_two(self.sides[stage], self.kept, self.got)
            self.got = exchange(self.kept, STAGES[stage - 1], 16)


def local(
    tokens,
    out_grad,
    image_lengths,
    group_of_block,
    norm_gains,
    row_biases,
    w_qkv,
    qv_bias,
    w_out,
    w_fc1,
    b_fc1,
    w_fc2,
):
    own, width = tokens.shape
    half = w_qkv.shape[2]
    hidden_half = w_fc1.shape[1]
    row_count = own * 2
    n = lax.axis_size("dp")
    d, m = lax.axis_index("dp"), lax.axis_index("mp")
    scale = HEAD_DIM ** (-0.5)
    Order.token, Order.after = None, ()

    edge = lax.dynamic_slice_in_dim(tokens, (1 - m) * (own - TILE), TILE)
    w_qkv2 = swap(w_qkv)
    halo = swap(edge)
    qv_bias2 = swap(qv_bias)
    tokens_other = swap(tokens)
    w_out2 = swap(w_out)
    b_fc12 = swap(b_fc1[None, :])
    w_fc12 = swap(w_fc1)
    w_fc22 = swap(w_fc2)

    core = m.astype(jnp.int32).reshape(1)
    place = jnp.stack([jnp.sum(image_lengths), (m * own).astype(jnp.int32)])
    seg_col, seg_row, weight_col, counts, out_low = prep_call(core, group_of_block, image_lengths, out_grad)
    counts = lax.all_gather(counts, ("dp", "mp"), axis=0, tiled=True)

    normed, qkv = qkv_call(tokens, halo, norm_gains, row_biases, w_qkv, w_qkv2, qv_bias, qv_bias2)
    context = attn_fwd(
        place, qkv, seg_col, seg_row, normed, tokens_other, norm_gains, row_biases, w_qkv, w_qkv2, qv_bias, qv_bias2, scale
    )
    hidden_one, normed_two = out_norm_call(context, tokens, w_out, w_out2, norm_gains, row_biases)
    act, gb, fc1_sums = ffn_call(normed_two, out_low, w_fc1, w_fc12, b_fc1[None, :], b_fc12, w_fc2, w_fc22)
    fc2_own, fc2_got = grad_call(
        fc2_grad_body, (hidden_half, width), 4 * own * hidden_half * width, act, out_low
    )
    fc2_got = swap(fc2_got)
    fc1_own, fc1_got = grad_call(
        fc1_grad_body, (width, hidden_half), 4 * own * hidden_half * width, normed_two, gb
    )
    fc1_got = swap(fc1_got)
    fast = n == 16
    if fast:
        both = lambda a, b: lax.rem(d // jnp.where(m == 0, a, b), 2).astype(jnp.int32)
        sides = jnp.stack([both(a, b) for a, b in STAGES])
        sides = [sides[k : k + 1] for k in range(4)]
    begin = lambda kept, got: Bucket(sides, *first_split(sides[0], kept, got, factor)) if fast else None
    step = lambda *buckets: [b.step() for b in buckets if fast]

    factor = factor_call(group_of_block, counts)
    fc2 = begin(fc2_own, fc2_got)
    grad_hidden, hidden_low, sums_two = grad_hidden_call(
        gb, w_fc1, w_fc12, hidden_one, out_grad, weight_col, norm_gains
    )
    edge_low = swap(lax.dynamic_slice_in_dim(hidden_low, (1 - m) * (own - TILE), TILE))
    fc1 = begin(fc1_own, fc1_got)
    step(fc2)
    grad_context = gctx_call(hidden_low, edge_low, w_out, w_out2)
    pairs = width // TILE
    attn_back = lambda which, turns: attn_bwd(qkv, grad_context, seg_col, seg_row, own, scale, which, turns)
    grad_a = attn_back((0, pairs // 2), 3)
    step(fc1, fc2)
    early_own, early_got = grad_call(
        early_grad_body, (2 * width, half), 8 * own * half * width, context, hidden_low, normed, grad_a
    )
    early_got = swap(early_got)
    grad_b = attn_back((*range(1, pairs // 2), *range(pairs // 2 + 1, pairs)), 1)
    step(fc1, fc2)
    early = begin(early_own, early_got)
    late_own, late_got = grad_call(late_grad_body, (width, width), 4 * own * width * width, normed, grad_b)
    late_got = swap(late_got)
    grad_input, vectors = grad_tokens_call(
        grad_a, grad_b, w_qkv, w_qkv2, tokens, grad_hidden, norm_gains, sums_two, fc1_sums, factor
    )
    vectors = lax.all_gather(vectors, ("dp", "mp"), axis=0, tiled=True)
    late = begin(late_own, late_got)
    step(fc2, fc1, early)
    output = output_call(act, w_fc2, w_fc22, hidden_one, row_biases)
    if fast:
        step(fc2, fc1, early, late)
        step(fc2, fc1, early, late)
        step(fc2, fc1, early, late)
        grad_fc2 = last_rows(sides[0], fc2.kept, fc2.got)
        step(fc1, late, early)
        grad_fc1 = last_rows(sides[0], fc1.kept, fc1.got)
        step(late, early)
        step(late, early)
        step(late)
        grad_out, grad_qkv = last_qkv(sides[0], early.kept, early.got, late.kept, late.got)
    else:
        total = lambda kept, got: (kept + got.astype(F32)) * factor[0, 0]
        grad_fc2 = sum_any(total(fc2_own, fc2_got))
        grad_fc1 = sum_any(total(fc1_own, fc1_got))
        first = total(early_own, early_got).reshape(4, half, half)
        second = total(late_own, late_got)
        grad_out = sum_any(jnp.concatenate([first[0], first[2]], axis=1))
        first = jnp.concatenate([first[1], first[3]])
        parts = [
            jnp.concatenate([first[:, t * TILE : (t + 1) * TILE], second[:, t * 2 * TILE : (t + 1) * 2 * TILE]], axis=1)
            for t in range(3)
        ]
        grad_qkv = sum_any(jnp.stack(parts))
    gains, shifts, grad_qv_bias, grad_b_fc1 = vectors_call(core, vectors, half, hidden_half)
    return (
        output,
        grad_input,
        gains,
        shifts,
        grad_qkv,
        grad_qv_bias,
        grad_out,
        grad_fc1,
        grad_b_fc1.reshape(hidden_half),
        grad_fc2,
    )


def solution(mesh):
    placed = (
        P(("dp", "mp"), None),
        P(("dp", "mp"), None),
        P("dp", None),
        P("dp"),
        P(),
        P(),
        P(None, None, "mp"),
        P(None, "mp"),
        P("mp", None),
        P(None, "mp"),
        P("mp"),
        P("mp", None),
    )
    return jax.shard_map(
        local,
        mesh=mesh,
        in_specs=placed,
        out_specs=(
            P(("dp", "mp"), None),
            P(("dp", "mp"), None),
            P(),
            P(),
            P(None, None, "mp"),
            P(None, "mp"),
            P("mp", None),
            P(None, "mp"),
            P("mp"),
            P("mp", None),
        ),
        check_vma=False,
    )
```

```python
import functools

import jax
import jax.numpy as jnp
from jax import lax
from jax.experimental import pallas as pl
from jax.experimental.pallas import tpu as pltpu
from jax.sharding import PartitionSpec as P

TILE = 128
MASKED = -3e38
F32 = jnp.float32
BF16 = jnp.bfloat16

def pick_heads(block):
    lane = lax.broadcasted_iota(jnp.int32, block.shape, 1)
    zero = jnp.zeros_like(block)
    return jnp.concatenate([jnp.where(lane < 64, block, zero), jnp.where(lane < 64, zero, block)], axis=0)

def join_heads(both):
    half = both.shape[1] // 2
    row = lax.broadcasted_iota(jnp.int32, (both.shape[0], half), 0)
    return jnp.where(row < 64, both[:, :half], both[:, half:]).T

def window(tiles, i):
    return [pl.multiple_of(lax.rem(i + step, tiles) * TILE, TILE) for step in (tiles - 1, 0, 1)]

def bias_of(starts, seg_col_ref, seg_row):
    keys = jnp.concatenate([seg_col_ref[pl.ds(s, TILE), :] for s in starts], axis=0)
    bias = jnp.where(keys == seg_row, 0.0, MASKED).astype(F32)
    return jnp.concatenate([bias, bias], axis=1)

def rows_of(ref, starts, cols):
    return jnp.concatenate([ref[pl.ds(s, TILE), cols] for s in starts], axis=0)


HEAD_DIM = 64
GROUPS = 3
LEN_NORM = 64
EPS = 1e-06
GELU_C = 0.7978845608028654
VMEM = pl.BlockSpec(memory_space=pltpu.VMEM)
SMEM = pl.BlockSpec(memory_space=pltpu.SMEM)
HBM = pl.BlockSpec(memory_space=pltpu.MemorySpace.HBM)
ANY = pl.BlockSpec(memory_space=pl.ANY)


def dot(a, b):
    return jnp.dot(a, b, preferred_element_type=F32)


def dot_nt(a, b):
    return lax.dot_general(a, b, (((1,), (1,)), ((), ())), preferred_element_type=F32)


def dot_tn(a, b):
    return lax.dot_general(a, b, (((0,), (0,)), ((), ())), preferred_element_type=F32)


def shape_of(shape, dtype):
    return jax.ShapeDtypeStruct(shape, dtype)


def nbytes(a):
    size = a.dtype.itemsize
    for n in a.shape:
        size *= n
    return size


class Order:
    token = None


CHUNK = 256
FLOPS_A_MICRO = 1_150_000_000


def in_hbm(x):
    return pltpu.with_memory_space_constraint(x, pltpu.MemorySpace.HBM)


def fused(steps, inputs, outs, temps=None, scalars=(), raw=(), chunked=(), limit=22, ahead=1, micros=10):
    temps = temps or {}
    waits = [a for a in (Order.token,) if a is not None]
    names = list(inputs)
    loaded = [k for k in names if k not in scalars and k not in raw]
    buffers = {k: inputs[k] for k in loaded} | outs | temps
    is_sem = lambda v: not isinstance(v, (jax.Array, jax.ShapeDtypeStruct))
    kinds = [v if is_sem(v) else pltpu.VMEM(v.shape, v.dtype) for v in buffers.values()]
    sem_of, count = {}, 0
    for k in (*loaded, *outs):
        sem_of[k] = count
        count += buffers[k].shape[0] // CHUNK if k in chunked else 1
    first = {k: min(n for n, (_, used) in enumerate(steps) if k in used) for k in loaded}
    last = {k: max(n for n, (_, used) in enumerate(steps) if k in used) for k in outs}

    def body(*refs):
        given = dict(zip(names, refs))
        results = dict(zip(outs, refs[len(names) + len(waits) :]))
        token_ref = refs[len(names) + len(waits) + len(outs)]
        rest = refs[len(names) + len(waits) + len(outs) + 1 :]
        held, sems = dict(zip(buffers, rest)), rest[len(buffers)]
        token_ref[...] = jnp.zeros_like(token_ref)
        place = {k: given[k] for k in (*scalars, *raw)} | held

        def pieces(k, source, target):
            if k not in chunked:
                return [pltpu.make_async_copy(source, target, sems.at[sem_of[k]])]
            rows = [pl.ds(r, CHUNK) for r in range(0, buffers[k].shape[0], CHUNK)]
            return [
                pltpu.make_async_copy(source.at[at], target.at[at], sems.at[sem_of[k] + n]) for n, at in enumerate(rows)
            ]

        loads = {k: pieces(k, given[k], held[k]) for k in loaded}
        stores = {k: pieces(k, held[k], results[k]) for k in outs}

        def start(n):
            mine = [loads[k] for k in loaded if first[k] == n]
            for copies in [c for c in mine if len(c) == 1]:
                copies[0].start()
            for n in range(max([len(c) for c in mine], default=0)):
                for copies in mine:
                    if 1 < len(copies) and n < len(copies):
                        copies[n].start()

        def ready(r, *which):
            for k in which or loaded:
                if k in chunked:
                    loads[k][r // CHUNK].wait()

        def done(r):
            for k in outs:
                if k in chunked:
                    stores[k][r // CHUNK].start()

        for n in range(ahead):
            start(n)
        for n, (fn, used) in enumerate(steps):
            start(n + ahead)
            code = getattr(fn, "__code__", None)
            piecewise = chunked and code is not None and "ready" in code.co_varnames
            hooks = dict(ready=ready, done=done) if piecewise else {}
            for k in loaded:
                if first[k] == n and k not in chunked:
                    loads[k][0].wait()
            fn(*(place[k] for k in used), **hooks)
            for k in outs:
                if last[k] == n and k not in chunked:
                    stores[k][0].start()
        for k in outs:
            for copy in stores[k]:
                copy.wait()

    size = sum(nbytes(v) for v in buffers.values() if not is_sem(v))
    pad = sum(nbytes(v) * 128 for v in buffers.values() if not is_sem(v) and v.shape[-1] == 1)
    kernel = pl.pallas_call(
        body,
        in_specs=[SMEM if k in scalars else HBM for k in names] + [ANY] * len(waits),
        out_specs=[HBM] * len(outs) + [VMEM],
        out_shape=[*(pltpu.MemorySpace.HBM(v.shape, v.dtype) for v in outs.values()), shape_of((8, 128), F32)],
        scratch_shapes=[*kinds, pltpu.SemaphoreType.DMA((count,))],
        compiler_params=pltpu.CompilerParams(vmem_limit_bytes=(limit << 20) + size + pad),
        cost_estimate=pl.CostEstimate(flops=micros * FLOPS_A_MICRO + 1, bytes_accessed=1, transcendentals=0),
    )
    operands = [v if k in scalars else in_hbm(v) for k, v in inputs.items()]
    *results, Order.token = kernel(*operands, *waits)
    return results


def stream(body, args, outs, scalars=0, limit=22, chunked=()):
    named = {f"in{n}": a for n, a in enumerate(args)}
    made = {f"out{n}": a for n, a in enumerate(outs)}
    every = [*named, *made]
    return fused(
        [(body, every)],
        named,
        made,
        scalars=every[:scalars],
        chunked=[every[n] for n in chunked],
        limit=limit,
    )


def call(body, args, outs, scalars=0, limit=22, micros=0):
    outs = list(outs)
    waits = [a for a in (Order.token,) if a is not None]
    n_in, n_wait, n_out = len(args), len(waits), len(outs)

    def tied(*refs):
        token_ref = refs[n_in + n_wait + n_out]
        token_ref[...] = jnp.zeros_like(token_ref)
        body(*refs[:n_in], *refs[n_in + n_wait : n_in + n_wait + n_out])

    *results, Order.token = pl.pallas_call(
        tied,
        in_specs=[SMEM] * scalars + [VMEM] * (n_in - scalars) + [ANY] * n_wait,
        out_specs=[VMEM] * (n_out + 1),
        out_shape=outs + [shape_of((8, 128), F32)],
        compiler_params=pltpu.CompilerParams(vmem_limit_bytes=limit << 20),
        cost_estimate=pl.CostEstimate(
            flops=micros * FLOPS_A_MICRO + 1, bytes_accessed=sum(nbytes(a) for a in [*args, *outs]) // 64, transcendentals=0
        ),
    )(*args, *waits)
    return results


def norm_parts(values):
    center = values - jnp.mean(values, axis=-1, keepdims=True)
    rstd = lax.rsqrt(jnp.mean(center * center, axis=-1, keepdims=True) + EPS)
    return center * rstd, rstd


def norm_back(grad, unit, rstd, gain):
    scaled = grad * gain
    return rstd * (
        scaled
        - jnp.mean(scaled, axis=-1, keepdims=True)
        - unit * jnp.mean(scaled * unit, axis=-1, keepdims=True)
    )


def fold(a):
    return jnp.sum(a.astype(F32), axis=0, keepdims=True)


def prep_body(core_ref, lengths_ref, grad_ref, col_ref, row_ref, len_ref, low_ref):
    ext, own = col_ref.shape[0], len_ref.shape[0]
    slots = lengths_ref.shape[1]
    pad = jnp.zeros((1, 128 - slots), F32)
    lengths = jnp.concatenate([lengths_ref[...].astype(F32), pad], axis=1)
    before = lax.broadcasted_iota(jnp.int32, (128, 128), 0) <= lax.broadcasted_iota(jnp.int32, (128, 128), 1)
    ends = dot(jnp.broadcast_to(lengths, (8, 128)).astype(BF16), jnp.where(before, 1.0, 0.0).astype(BF16))[0:1]
    lane = lax.broadcasted_iota(jnp.int32, (1, 128), 1)
    ends = jnp.where(lane < slots, ends, 1e9)
    row = lax.broadcasted_iota(jnp.int32, (ext, 1), 0)
    core = core_ref[0]
    edge = jnp.where(core == 0, 0, -own - (ext - own))
    position = row + jnp.where(row < own, core * own, edge + core * own)
    past = jnp.where(position.astype(F32) >= ends, 1.0, 0.0)
    segment = jnp.sum(past, axis=1, keepdims=True)
    col_ref[...] = segment
    row_ref[...] = dot_nt(jnp.ones((8, 128), BF16), past.astype(BF16))[0:1]
    hit = jnp.where(segment[:own] == lane.astype(F32), lengths, 0.0)
    length = jnp.sum(hit, axis=1, keepdims=True)
    weight = jnp.where(length > 0, LEN_NORM / jnp.maximum(length, 1.0), 0.0)
    len_ref[...] = weight
    low_ref[...] = (grad_ref[...].astype(F32) * weight).astype(BF16)


def factor_body(group_ref, counts_ref, factor_ref):
    lane = lax.broadcasted_iota(jnp.int32, (1, 128), 1)
    counts = jnp.where(lane < GROUPS, fold(counts_ref[:, :128]) * 0.5, 0.0)
    roots = jnp.sqrt(counts)
    all_images = jnp.sum(counts, axis=1, keepdims=True)
    all_roots = jnp.sum(roots, axis=1, keepdims=True)
    root = jnp.sum(jnp.where(lane == group_ref[0], roots, 0.0), axis=1, keepdims=True)
    factor_ref[...] = jnp.broadcast_to(all_images / (root * all_roots), factor_ref.shape)


def factor_call(group, counts):
    return call(factor_body, (group, counts), [shape_of((8, 128), F32)], scalars=1)[0]


def edge_body(core_ref, other_ref, halo_ref, sem):
    rows = pl.ds(pl.multiple_of(core_ref[0] * (other_ref.shape[0] - TILE), TILE), TILE)
    load = pltpu.make_async_copy(other_ref.at[rows], halo_ref, sem)
    load.start()
    load.wait()


def qkv_body(tokens_ref, halo_ref, gains_ref, biases_ref, w_ref, w2_ref, b_ref, b2_ref, normed_ref, out_ref):
    own, width = tokens_ref.shape
    ext = normed_ref.shape[0]
    for r, ref in [(r, tokens_ref) for r in range(0, own, 256)] + [(own, halo_ref)]:
        n = min(256, ext - r)
        at = 0 if ref is halo_ref else r
        unit, _ = norm_parts(ref[at : at + n, :].astype(F32))
        normed = (unit * gains_ref[0:1, :] + biases_ref[0:1, :]).astype(BF16)
        normed_ref[r : r + n, :] = normed
        for t in range(3):
            weights = jnp.concatenate([w_ref[t], w2_ref[t]], axis=1)
            part = dot(normed, weights)
            if t != 1:
                row = t // 2
                part = part + jnp.concatenate([b_ref[row : row + 1, :], b2_ref[row : row + 1, :]], axis=1)
            out_ref[r : r + n, t * width : (t + 1) * width] = part.astype(BF16)


def out_norm_body(ctx_ref, tok_ref, w_ref, w2_ref, gains_ref, biases_ref, hid_ref, norm_ref):
    weights = jnp.concatenate([w_ref[...], w2_ref[...]], axis=0)
    own = tok_ref.shape[0]
    product = lambda r: dot(ctx_ref[r : r + 256, :], weights)
    ready = product(0)
    for r in range(0, own, 256):
        later = product(r + 256) if r + 256 < own else None
        rows = slice(r, r + 256)
        hidden = tok_ref[rows, :].astype(F32) + ready + biases_ref[2:3, :]
        hid_ref[rows, :] = hidden
        unit, _ = norm_parts(hidden)
        norm_ref[rows, :] = (unit * gains_ref[1:2, :] + biases_ref[1:2, :]).astype(BF16)
        ready = later


def ffn_body(x_ref, g_ref, w_ref, b_ref, v_ref, act_ref, gb_ref, sum_ref, *, ready=None, done=None):
    cols = 256
    hidden = w_ref.shape[1]
    rows_all = x_ref.shape[0]

    def products(r, j):
        if ready and j == 0:
            ready(r, "x", "g")
        if ready and r == 0:
            ready(j, "v")
        rows = slice(r, r + 256)
        v = dot(x_ref[rows, :], w_ref[:, j : j + cols]) + b_ref[:, j : j + cols]
        return v, dot_nt(g_ref[rows, :], v_ref[j : j + cols, :])

    sums = {}
    work = [(r, j) for r in range(0, rows_all, 256) for j in range(0, hidden, cols)]
    now = products(*work[0])
    for n, (r, j) in enumerate(work):
        later = products(*work[n + 1]) if n + 1 < len(work) else None
        v, grad = now
        rows = slice(r, r + 256)
        u = v * v
        gate = 0.5 * jnp.tanh(v * (GELU_C + (GELU_C * 0.044715) * u)) + 0.5
        act = v * gate
        act_ref[rows, j : j + cols] = act.astype(BF16)
        slope = gate + act * (1.0 - gate) * (2 * GELU_C + (GELU_C * 6 * 0.044715) * u)
        low = (grad * slope).astype(BF16)
        gb_ref[rows, j : j + cols] = low
        sums[j] = fold(low) + sums.get(j, 0.0)
        now = later
    for j, total in sums.items():
        sum_ref[:, j : j + cols] = total


def fc2_grad_body(act_ref, low_ref, out_ref):
    for r in range(0, out_ref.shape[0], 256):
        out_ref[r : r + 256, :] = dot_tn(act_ref[:, r : r + 256], low_ref[...]).astype(BF16)


def fc1_grad_body(x_ref, gb_ref, out_ref):
    for r in range(0, out_ref.shape[0], 256):
        out_ref[r : r + 256, :] = dot_tn(x_ref[:, r : r + 256], gb_ref[...]).astype(BF16)


def early_grad_body(ctx_ref, low_ref, norm_ref, ga_ref, own_ref, other_ref):
    half = own_ref.shape[1]
    own = low_ref.shape[0]
    for h in range(2):
        cols, at = slice(h * half, (h + 1) * half), 2 * h * half
        other_ref[at : at + half, :] = dot_tn(ctx_ref[:, half:], low_ref[:, cols]).astype(BF16)
        own_ref[at : at + half, :] = dot_tn(ctx_ref[:, :half], low_ref[:, cols]).astype(BF16)
        both = dot_tn(norm_ref[:own, cols], ga_ref[...]).astype(BF16)
        own_ref[at + half : at + 2 * half, :] = both[:, :half]
        other_ref[at + half : at + 2 * half, :] = both[:, half:]


def late_grad_body(norm_ref, gb_ref, gc_ref, own_ref, other_ref):
    own, half = gb_ref.shape[0], gb_ref.shape[1] // 2
    for r in range(0, own_ref.shape[0], 256):
        for n, ref in enumerate((gb_ref, gc_ref)):
            both = dot_tn(norm_ref[:own, r : r + 256], ref[...]).astype(BF16)
            own_ref[r : r + 256, n * half : (n + 1) * half] = both[:, :half]
            other_ref[r : r + 256, n * half : (n + 1) * half] = both[:, half:]


def edge_copies(core_ref, sources, targets, sems):
    at = (1 - core_ref[0]) * (sources[0].shape[0] - TILE)
    rows = pl.ds(pl.multiple_of(at, TILE), TILE)
    return [pltpu.make_async_copy(a.at[rows], b, sems.at[n]) for n, (a, b) in enumerate(zip(sources, targets))]


def edge_load_body(core_ref, a_ref, b_ref, c_ref, d_ref, a2_ref, b2_ref, c2_ref, d2_ref, sems):
    for copy in edge_copies(core_ref, (a_ref, b_ref, c_ref, d_ref), (a2_ref, b2_ref, c2_ref, d2_ref), sems):
        copy.start()


def edge_grad_body(
    core_ref, a_ref, b_ref, c_ref, d_ref, a2_ref, hid_ref, og_ref, wr_ref, sems, gb_ref, w_ref, w2_ref, gains_ref, out_ref
):
    for copy in edge_copies(core_ref, (a_ref, b_ref, c_ref, d_ref), (a2_ref, hid_ref, og_ref, wr_ref), sems):
        copy.wait()
    rows = pl.ds(pl.multiple_of((1 - core_ref[0]) * (gb_ref.shape[0] - TILE), TILE), TILE)
    grad = dot_nt(gb_ref[rows, :], w_ref[...]) + dot_nt(a2_ref[...], w2_ref[...])
    unit, rstd = norm_parts(hid_ref[...])
    back = norm_back(grad, unit, rstd, gains_ref[1:2, :])
    out_ref[...] = (back + og_ref[...].astype(F32) * wr_ref[...]).astype(BF16)


def grad_hidden_body(gb_ref, gb2_ref, w_ref, w2_ref, hid_ref, og_ref, wr_ref, gains_ref, gh_ref, low_ref, sums_ref, *, ready, done):
    def product(r):
        ready(r)
        rows = slice(r, r + 256)
        return dot_nt(gb_ref[rows, :], w_ref[...]) + dot_nt(gb2_ref[rows, :], w2_ref[...])

    own = hid_ref.shape[0]
    now, sums = product(0), [0.0] * 4
    for r in range(0, own, 256):
        later = product(r + 256) if r + 256 < own else None
        rows, grad = slice(r, r + 256), now
        unit, rstd = norm_parts(hid_ref[rows, :])
        cot = og_ref[rows, :].astype(F32) * wr_ref[rows, :]
        hidden = norm_back(grad, unit, rstd, gains_ref[1:2, :]) + cot
        gh_ref[rows, :] = hidden
        low_ref[rows, :] = hidden.astype(BF16)
        done(r)
        sums = [a + fold(b) for a, b in zip(sums, (grad * unit, grad, hidden, cot))]
        now = later
    for row, a in enumerate(sums):
        sums_ref[row : row + 1, :] = a


def grad_hidden_call(gb, gb2, w, w2, hidden, out_grad, weight_col, gains):
    rows, width = hidden.shape
    return stream(
        grad_hidden_body,
        (gb, gb2, w, w2, hidden, out_grad, weight_col, gains),
        [shape_of((rows, width), F32), shape_of((rows, width), BF16), shape_of((8, width), F32)],
        chunked=(0, 1, 4, 5, 6, 8, 9),
    )


def gctx_body(x_ref, h_ref, w_ref, w2_ref, out_ref):
    own = x_ref.shape[0]
    for r in range(0, own, 256):
        weights = jnp.concatenate([w_ref[...], w2_ref[...]], axis=0)
        out_ref[r : r + 256, :] = dot_nt(x_ref[r : r + 256, :], weights).astype(BF16)
    weights = jnp.concatenate([w_ref[...], w2_ref[...]], axis=0)
    out_ref[own:, :] = dot_nt(h_ref[...], weights).astype(BF16)


def grad_tokens_body(
    ga_ref, gb_ref, gc_ref, w_ref, w2_ref, tok_ref, gh_ref, gains_ref, two_ref, s_ref, s2_ref, factor_ref, out_ref, sums_ref
):
    factor = factor_ref[0:1, 0:1]
    width = tok_ref.shape[1]
    sums_ref[...] = jnp.zeros_like(sums_ref)
    sums_ref[2:6, :] = two_ref[0:4, :]
    for n, ref in enumerate((s_ref, s2_ref)):
        for r in range(2):
            row = 9 + 2 * n + r
            sums_ref[row : row + 1, :] = ref[:, r * width : (r + 1) * width]
    groups = (ga_ref, gb_ref, gc_ref)

    def product(r):
        grad = jnp.zeros((256, width), F32)
        for n, ref in enumerate(groups):
            cols = slice(n * TILE, (n + 1) * TILE)
            weights = [w[t, :, cols] for w in (w_ref, w2_ref) for t in range(3)]
            grad = grad + dot_nt(ref[r : r + 256, :], jnp.concatenate(weights, axis=1))
        return grad

    own = tok_ref.shape[0]
    now, sums = product(0), [0.0] * 5
    for r in range(0, own, 256):
        later = product(r + 256) if r + 256 < own else None
        rows, grad = slice(r, r + 256), now
        unit, rstd = norm_parts(tok_ref[rows, :].astype(F32))
        out_ref[rows, :] = (norm_back(grad, unit, rstd, gains_ref[0:1, :]) + gh_ref[rows, :]) * factor
        terms = (grad * unit, grad, *(ref[rows, :] for ref in groups))
        sums = [a + fold(b) for a, b in zip(sums, terms)]
        now = later
    for row, a in zip((0, 1, 6, 7, 8), sums):
        sums_ref[row : row + 1, :] = a
    sums_ref[...] = sums_ref[...] * factor


def vectors_body(core_ref, all_ref, gains_ref, shifts_ref, qv_ref, fc1_ref):
    blocks = all_ref.shape[0] // 32
    width = all_ref.shape[1]
    half = qv_ref.shape[1]
    total = all_ref[0:32, :]
    for b in range(1, blocks):
        total = total + all_ref[32 * b : 32 * (b + 1), :]
    mine = jnp.where(core_ref[0] == 0, total[:16], total[16:])
    peer = jnp.where(core_ref[0] == 0, total[16:], total[:16])
    both = mine + peer
    gains_ref[0:1, :] = both[0:1]
    gains_ref[1:2, :] = both[2:3]
    shifts_ref[0:1, :] = both[1:2]
    shifts_ref[1:4, :] = both[3:6]
    for n in range(3):
        both = mine[6 + n : 7 + n, :half] + peer[6 + n : 7 + n, half:]
        for row, t in ((0, 0), (1, 2)):
            qv_ref[row : row + 1, n * TILE : (n + 1) * TILE] = both[:, t * TILE : (t + 1) * TILE]
    for r in range(2):
        fc1_ref[:, r * width : (r + 1) * width] = mine[9 + r : 10 + r] + peer[11 + r : 12 + r]


def vectors_call(core, everything, half, hidden_half):
    width = everything.shape[1]
    return call(
        vectors_body,
        (core, everything),
        [shape_of((2, width), F32), shape_of((4, width), F32), shape_of((2, half), F32), shape_of((1, hidden_half), F32)],
        scalars=1,
    )


def output_body(a_ref, a2_ref, w_ref, w2_ref, hid_ref, biases_ref, out_ref, *, ready, done):
    for r in range(0, hid_ref.shape[0], 256):
        ready(r)
        rows = slice(r, r + 256)
        mlp = dot(a_ref[rows, :], w_ref[...]) + dot(a2_ref[rows, :], w2_ref[...])
        out_ref[rows, :] = (hid_ref[rows, :] + mlp + biases_ref[3:4, :]).astype(BF16)
        done(r)


def output_call(a, a2, w, w2, hidden, biases):
    return stream(
        output_body, (a, a2, w, w2, hidden, biases), [shape_of(hidden.shape, BF16)], chunked=(0, 1, 4, 6)
    )[0]


SCALE = HEAD_DIM ** (-0.5)


def attn_fwd_body(
    core_ref,
    lengths_ref,
    qkv_ref,
    seg_col_ref,
    seg_row_ref,
    normed_ref,
    other_ref,
    gains_ref,
    biases_ref,
    w_ref,
    w2_ref,
    b_ref,
    b2_ref,
    out_ref,
    far_ref,
    wide_ref,
    keys_ref,
    values_ref,
    sem,
):
    own, width = out_ref.shape
    tiles = qkv_ref.shape[0] // TILE

    pairs = width // TILE
    lane = lax.broadcasted_iota(jnp.int32, (TILE, TILE), 1)

    def one(i, _):
        starts = window(tiles, i)
        here = pl.ds(starts[1], TILE)
        bias = bias_of(starts, seg_col_ref, seg_row_ref[:, here])
        cols = lambda t, p: slice(t * width + p * TILE, t * width + (p + 1) * TILE)
        scores, probs = {}, {}
        for step in range(pairs + 2):
            if step < pairs:
                queries = pick_heads(qkv_ref[here, cols(0, step)] * jnp.asarray(SCALE, BF16))
                scores[step] = dot_nt(rows_of(qkv_ref, starts, cols(1, step)), queries) + bias
            p = step - 1
            if 0 <= p < pairs:
                expo = jnp.exp(scores[p] - jnp.max(scores[p], axis=0, keepdims=True))
                probs[p] = (expo * (1.0 / jnp.sum(expo, axis=0, keepdims=True))).astype(BF16)
            p = step - 2
            if 0 <= p < pairs:
                both = dot_tn(probs[p], rows_of(qkv_ref, starts, cols(2, p)))
                out_ref[here, cols(0, p)] = jnp.where(lane < HEAD_DIM, both[:TILE], both[TILE:]).astype(BF16)
        return 0

    lax.fori_loop(0, own // TILE, one, 0)
    total_rows = lax.fori_loop(0, lengths_ref.shape[1], lambda j, n: n + lengths_ref[0, j], jnp.int32(0))
    first_row = core_ref[0] * own

    @pl.when(total_rows < 2 * own - TILE)
    def _():
        load = pltpu.make_async_copy(other_ref, far_ref, sem)
        load.start()
        load.wait()

        @pl.loop(0, own // TILE)
        def _(i):
            rows = pl.ds(pl.multiple_of(i * TILE, TILE), TILE)
            unit, _ = norm_parts(far_ref[rows, :].astype(F32))
            far_ref[rows, :] = (unit * gains_ref[0:1, :] + biases_ref[0:1, :]).astype(BF16)

        key_row = lax.broadcasted_iota(jnp.int32, (2 * own, 1), 0) + first_row
        key_row = jnp.where(key_row >= 2 * own, key_row - 2 * own, key_row)
        wide_ref[...] = jnp.where(key_row >= total_rows, 0.0, MASKED)
        for side, (wide, bias_ref) in enumerate(((w_ref, b_ref), (w2_ref, b2_ref))):
            half = wide.shape[2]

            @pl.loop(0, half // TILE)
            def _(p):
                at = pl.multiple_of(p * TILE, TILE)
                base = pl.multiple_of(side * half + p * TILE, TILE)
                for t, ref in ((1, keys_ref), (2, values_ref)):
                    ref[:own, :] = qkv_ref[:own, pl.ds(pl.multiple_of(t * width + base, TILE), TILE)]
                    part = dot(far_ref[...], wide[t, :, pl.ds(at, TILE)])
                    if t == 2:
                        part = part + bias_ref[1:2, pl.ds(at, TILE)]
                    ref[own:, :] = part.astype(BF16)

                @pl.loop(0, own // TILE)
                def _(i):
                    rows = pl.ds(pl.multiple_of(i * TILE, TILE), TILE)
                    queries = pick_heads(qkv_ref[rows, pl.ds(base, TILE)] * jnp.asarray(SCALE, BF16))
                    scores = dot_nt(keys_ref[...], queries) + wide_ref[...]
                    top = jnp.max(scores, axis=0, keepdims=True)
                    expo = jnp.exp(scores - top)
                    probs = (expo * (1.0 / jnp.sum(expo, axis=0, keepdims=True))).astype(BF16)
                    full = join_heads(dot_tn(values_ref[...], probs)).astype(BF16)
                    row = lax.broadcasted_iota(jnp.int32, (TILE, TILE), 0) + i * TILE + first_row
                    out_ref[rows, pl.ds(base, TILE)] = jnp.where(row >= total_rows, full, out_ref[rows, pl.ds(base, TILE)])


def attn_bwd_body(qkv_ref, g_ref, seg_col_ref, seg_row_ref, out_ref, dq_ref, dk_ref, dv_ref, *, pairs, turns):
    tiles = qkv_ref.shape[0] // TILE
    own, width = out_ref.shape[0], qkv_ref.shape[1] // 3
    dk_ref[...] = jnp.zeros_like(dk_ref)
    dv_ref[...] = jnp.zeros_like(dv_ref)

    def load(starts, here, p):
        cols = lambda t: slice(t * width + p * TILE, t * width + (p + 1) * TILE)
        queries = pick_heads(qkv_ref[here, cols(0)] * jnp.asarray(SCALE, BF16))
        keys, values = rows_of(qkv_ref, starts, cols(1)), rows_of(qkv_ref, starts, cols(2))
        return queries, keys, values, pick_heads(g_ref[here, cols(0)])

    def products(arrays, bias):
        queries, keys, values, grads = arrays
        return dot_nt(keys, queries) + bias, dot_nt(values, grads)

    def softmax_back(scores, grad_probs):
        expo = jnp.exp(scores - jnp.max(scores, axis=0, keepdims=True))
        probs = expo * (1.0 / jnp.sum(expo, axis=0, keepdims=True))
        mean = jnp.sum(probs * grad_probs, axis=0, keepdims=True)
        return probs.astype(BF16), (probs * (grad_probs - mean)).astype(BF16)

    def finish(starts, here, at, arrays, probs, grad_scores):
        queries, keys, _, grads = arrays
        cols = slice(at * TILE, (at + 1) * TILE)
        dv, dk = dot(probs, grads), dot(grad_scores, queries)
        for k, s in enumerate(starts):
            part = slice(k * TILE, (k + 1) * TILE)
            dk_ref[pl.ds(s, TILE), cols] += dk[part]
            dv_ref[pl.ds(s, TILE), cols] += dv[part]
        dq_ref[here, cols] = (join_heads(dot_tn(keys, grad_scores)) * SCALE).astype(BF16)

    def one(i, _):
        work = []
        for turn in range(turns):
            starts = window(tiles, i * turns + turn)
            here = pl.ds(starts[1], TILE)
            bias = bias_of(starts, seg_col_ref, seg_row_ref[:, here])
            work += [(starts, here, bias, at, p) for at, p in enumerate(pairs)]
        first, second = {}, {}
        for step in range(len(work) + 2):
            if step < len(work):
                starts, here, bias, at, p = work[step]
                first[step] = products(load(starts, here, p), bias)
            if 0 <= step - 1 < len(work):
                second[step - 1] = softmax_back(*first.pop(step - 1))
            if 0 <= step - 2 < len(work):
                starts, here, bias, at, p = work[step - 2]
                finish(starts, here, at, load(starts, here, p), *second.pop(step - 2))
        return 0

    lax.fori_loop(0, tiles // turns, one, 0)
    half = len(pairs) * TILE // 2
    for side in range(2):
        cols = slice(side * half, (side + 1) * half)
        base = side * 3 * half
        out_ref[:, base : base + half] = dq_ref[:own, cols]
        out_ref[:, base + half : base + 2 * half] = dk_ref[:own, cols].astype(BF16)
        out_ref[:, base + 2 * half : base + 3 * half] = dv_ref[:own, cols].astype(BF16)


def half_of(side_ref, flip):
    return 1 - side_ref[0] if flip else side_ref[0]


def first_split_body(side_ref, kept_ref, got_ref, factor_ref, send_ref, keep_ref):
    half = keep_ref.shape[0]
    factor = factor_ref[0:1, 0:1]
    total = lambda at: (kept_ref[pl.ds(at, half), :].astype(F32) + got_ref[pl.ds(at, half), :].astype(F32)) * factor
    send_ref[...] = total(pl.multiple_of((1 - side_ref[0]) * half, 16)).astype(BF16)
    keep_ref[...] = total(pl.multiple_of(side_ref[0] * half, 16)).astype(BF16)


def first_split(side, kept, got, factor):
    half, cols = kept.shape[0] // 2, kept.shape[1]
    return call(
        first_split_body,
        (side, kept, got, factor),
        [shape_of((half, cols), BF16)] * 2,
        scalars=1,
    )


def split_two_body(side_ref, kept_ref, got_ref, send_ref, keep_ref):
    half = keep_ref.shape[0]
    total = lambda at: kept_ref[pl.ds(at, half), :].astype(F32) + got_ref[pl.ds(at, half), :].astype(F32)
    send_ref[...] = total(pl.multiple_of((1 - side_ref[0]) * half, 16)).astype(BF16)
    keep_ref[...] = total(pl.multiple_of(side_ref[0] * half, 16)).astype(BF16)


def split_two(side, kept, got, micros=0):
    half, cols = kept.shape[0] // 2, kept.shape[1]
    return call(
        split_two_body,
        (side, kept, got),
        [shape_of((half, cols), BF16)] * 2,
        scalars=1,
        micros=micros,
    )


def add_body(kept_ref, got_ref, out_ref):
    out_ref[...] = (kept_ref[...].astype(F32) + got_ref[...].astype(F32)).astype(BF16)


def add_two(kept, got):
    return call(add_body, (kept, got), [shape_of(kept.shape, BF16)])[0]


def join_body(side_ref, own_ref, got_ref, out_ref):
    half = own_ref.shape[0]
    out_ref[pl.ds(pl.multiple_of(side_ref[0] * half, 16), half), :] = own_ref[...]
    out_ref[pl.ds(pl.multiple_of((1 - side_ref[0]) * half, 16), half), :] = got_ref[...]


def join_two(side, own, got):
    half, cols = own.shape
    return call(join_body, (side, own, got), [shape_of((2 * half, cols), BF16)], scalars=1)[0]


def last_body(side_ref, own_ref, got_ref, out_ref):
    half = own_ref.shape[0]
    for flip, ref in ((False, own_ref), (True, got_ref)):
        out_ref[pl.ds(pl.multiple_of(half_of(side_ref, flip) * half, 16), half), :] = ref[...].astype(F32)


def last_rows(side, own, got):
    rows, cols = own.shape
    return call(last_body, (side, own, got), [shape_of((2 * rows, cols), F32)], scalars=1)[0]


def last_qkv_body(side_ref, a0_ref, a1_ref, b0_ref, b1_ref, wout_ref, wqkv_ref):
    half = wout_ref.shape[0]
    for flip, a_ref, b_ref in ((False, a0_ref, b0_ref), (True, a1_ref, b1_ref)):
        part = pl.ds(pl.multiple_of(half_of(side_ref, flip) * half, 128), half)
        wout_ref[:, part] = a_ref[:half, :].astype(F32)
        for t in range(3):
            wqkv_ref[t, part, :TILE] = a_ref[half:, t * TILE : (t + 1) * TILE].astype(F32)
            for n in range(2):
                at = n * half + t * TILE
                wqkv_ref[t, part, (1 + n) * TILE : (2 + n) * TILE] = b_ref[:, at : at + TILE].astype(F32)


def last_qkv(side, a0, a1, b0, b1):
    half = a0.shape[1]
    return call(
        last_qkv_body,
        (side, a0, a1, b0, b1),
        [shape_of((half, 2 * half), F32), shape_of((3, 2 * half, half), F32)],
        scalars=1,
    )


def swap(x):
    return lax.ppermute(x, "mp", [(0, 1), (1, 0)])


def exchange(x, bits, n):
    pairs = [(2 * d + m, 2 * (d ^ bits[m]) + m) for d in range(n) for m in range(2)]
    return lax.ppermute(x, ("dp", "mp"), pairs)


def sum_any(part):
    n = lax.axis_size("dp")
    shape = part.shape
    part = part.reshape(-1, shape[-1])
    if n & (n - 1) or part.shape[0] % n:
        return lax.psum(part, "dp").reshape(shape)
    d = lax.axis_index("dp")
    bits = [1 << k for k in range(n.bit_length() - 1)]
    for bit in bits:
        half = part.shape[0] // 2
        side = lax.rem(d // bit, 2)
        sent = lax.dynamic_slice_in_dim(part, (1 - side) * half, half).astype(BF16)
        kept = lax.dynamic_slice_in_dim(part, side * half, half)
        part = kept + exchange(sent, (bit, bit), n).astype(F32)
    total = part.astype(BF16)
    for bit in reversed(bits):
        side = lax.rem(d // bit, 2)
        got = exchange(total, (bit, bit), n)
        total = jnp.concatenate([jnp.where(side == 0, total, got), jnp.where(side == 0, got, total)], axis=0)
    return total.astype(F32).reshape(shape)


STAGES = ((1, 2), (2, 1), (4, 4), (8, 8))


class Bucket:
    def __init__(self, sides, sent, kept):
        self.sides, self.at, self.kept = sides, 0, kept
        self.got = exchange(sent, STAGES[0], 16)

    def step(self, micros=0):
        self.at += 1
        if self.at < 4:
            sent, self.kept = split_two(self.sides[self.at], self.kept, self.got, micros)
            self.got = exchange(sent, STAGES[self.at], 16)
        elif self.at == 4:
            self.kept = add_two(self.kept, self.got)
            self.got = exchange(self.kept, STAGES[3], 16)
        else:
            stage = 8 - self.at
            self.kept = join_two(self.sides[stage], self.kept, self.got)
            self.got = exchange(self.kept, STAGES[stage - 1], 16)


def local(
    tokens,
    out_grad,
    image_lengths,
    group_of_block,
    norm_gains,
    row_biases,
    w_qkv,
    qv_bias,
    w_out,
    w_fc1,
    b_fc1,
    w_fc2,
):
    own, width = tokens.shape
    half = w_qkv.shape[2]
    hidden_half = w_fc1.shape[1]
    row_count = own * 2
    n = lax.axis_size("dp")
    d, m = lax.axis_index("dp"), lax.axis_index("mp")
    Order.token = None

    tokens_other = swap(tokens)
    w_qkv2 = swap(w_qkv)
    qv_bias2 = swap(qv_bias)
    late_swap = lambda x: swap(lax.optimization_barrier((x, w_qkv2))[0])
    w_out2 = late_swap(w_out)
    w_fc12 = late_swap(w_fc1)
    w_fc22 = late_swap(w_fc2)
    b_fc12 = late_swap(b_fc1[None, :])

    core = m.astype(jnp.int32).reshape(1)
    ext = own + TILE
    images = jnp.sum((image_lengths > 0).astype(F32))
    lane = lax.broadcasted_iota(jnp.int32, (16, width), 1)
    row = lax.broadcasted_iota(jnp.int32, (16, width), 0)
    counts = jnp.where((row == 0) & (lane == group_of_block[0]), images, 0.0)
    counts = lax.all_gather(counts, ("dp", "mp"), axis=0, tiled=True)

    seg_col, seg_row, weight_col, out_low, normed, qkv, context = fused(
        [
            (prep_body, ["core", "lens", "og", "col", "row", "weight", "low"]),
            (edge_body, ["core", "other", "halo", "sem"]),
            (qkv_body, ["tokens", "halo", "gains", "biases", "w", "w2", "b", "b2", "normed", "qkv"]),
            (
                attn_fwd_body,
                ["core", "lengths", "qkv", "col", "row", "normed", "other", "gains", "biases"]
                + ["w", "w2", "b", "b2", "context", "far", "wide", "keys", "values", "sem"],
            ),
        ],
        dict(
            core=core,
            lengths=image_lengths,
            lens=image_lengths,
            og=out_grad,
            tokens=tokens,
            gains=norm_gains,
            biases=row_biases,
            w=w_qkv,
            w2=w_qkv2,
            b=qv_bias,
            b2=qv_bias2,
            other=tokens_other,
        ),
        dict(
            col=shape_of((ext, 1), F32),
            row=shape_of((1, ext), F32),
            weight=shape_of((own, 1), F32),
            low=shape_of((own, width), BF16),
            normed=shape_of((ext, width), BF16),
            qkv=shape_of((ext, 3 * width), BF16),
            context=shape_of((own, width), BF16),
        ),
        dict(
            halo=shape_of((TILE, width), BF16),
            far=shape_of((own, width), BF16),
            wide=shape_of((row_count, 1), F32),
            keys=shape_of((row_count, TILE), BF16),
            values=shape_of((row_count, TILE), BF16),
            sem=pltpu.SemaphoreType.DMA,
        ),
        scalars=("core", "lengths"),
        raw=("other",),
        ahead=3,
    )
    half_shapes = dict(
        act=shape_of((own, hidden_half), BF16),
        gb=shape_of((own, hidden_half), BF16),
        sums=shape_of((1, hidden_half), F32),
        grad2=shape_of((hidden_half, width), BF16),
        grad1=shape_of((width, hidden_half), BF16),
    )
    half_steps = [
        (ffn_body, ["x", "g", "w", "b", "v", "act", "gb", "sums"]),
        (fc2_grad_body, ["act", "g", "grad2"]),
        (fc1_grad_body, ["x", "gb", "grad1"]),
    ]
    hidden_one, normed_two, act2, gb2, sums2, fc2_got, fc1_got = fused(
        [(out_norm_body, ["context", "tokens", "wo", "wo2", "gains", "biases", "hidden", "x"]), *half_steps],
        dict(
            context=context,
            tokens=tokens,
            wo=w_out,
            wo2=w_out2,
            gains=norm_gains,
            biases=row_biases,
            g=out_low,
            w=w_fc12,
            b=b_fc12,
            v=w_fc22,
        ),
        dict(hidden=shape_of((own, width), F32), x=shape_of((own, width), BF16), **half_shapes),
    )
    fc2_got = swap(fc2_got)
    fc1_got = swap(fc1_got)
    edge_names = ["core", "gb2", "hidden", "og", "weight", "gb2e", "hiddene", "oge", "weighte", "sems"]
    act, gb, sums, fc2_own, fc1_own, edge_low = fused(
        [
            half_steps[0],
            (edge_load_body, edge_names),
            *half_steps[1:],
            (edge_grad_body, [*edge_names, "gb", "w", "w2", "gains", "edge"]),
        ],
        dict(
            core=core,
            w=w_fc1,
            b=b_fc1[None, :],
            x=normed_two,
            g=out_low,
            v=w_fc2,
            w2=w_fc12,
            gains=norm_gains,
            gb2=gb2,
            hidden=hidden_one,
            og=out_grad,
            weight=weight_col,
        ),
        half_shapes | dict(edge=shape_of((TILE, width), BF16)),
        dict(
            gb2e=shape_of((TILE, hidden_half), BF16),
            hiddene=shape_of((TILE, width), F32),
            oge=shape_of((TILE, width), BF16),
            weighte=shape_of((TILE, 1), F32),
            sems=pltpu.SemaphoreType.DMA((4,)),
        ),
        scalars=("core",),
        raw=("gb2", "hidden", "og", "weight"),
        chunked=("x", "g", "v"),
    )
    edge_low = swap(edge_low)
    factor = factor_call(group_of_block, counts)
    fast = n == 16
    if fast:
        both = lambda a, b: lax.rem(d // jnp.where(m == 0, a, b), 2).astype(jnp.int32)
        sides = jnp.stack([both(a, b) for a, b in STAGES])
        sides = [sides[k : k + 1] for k in range(4)]
    begin = lambda kept, got: Bucket(sides, *first_split(sides[0], kept, got, factor)) if fast else None
    step = lambda *buckets: [b.step() for b in buckets if fast]
    fc2 = begin(fc2_own, fc2_got)
    fc1 = begin(fc1_own, fc1_got)

    grad_hidden, hidden_low, sums_two = grad_hidden_call(
        gb, gb2, w_fc1, w_fc12, hidden_one, out_grad, weight_col, norm_gains
    )
    pairs = width // TILE // 2
    attn_back = lambda n: functools.partial(attn_bwd_body, pairs=(n, pairs + n), turns=3)
    attn_temps = dict(
        dq=shape_of((ext, 2 * TILE), BF16), dk=shape_of((ext, 2 * TILE), F32), dv=shape_of((ext, 2 * TILE), F32)
    )
    group_shape = shape_of((own, width), BF16)
    grad_context, grad_a, early_own, early_got = fused(
        [
            (gctx_body, ["low", "edge", "wo", "wo2", "g"]),
            (attn_back(0), ["qkv", "g", "col", "row", "out", "dq", "dk", "dv"]),
            (early_grad_body, ["context", "low", "normed", "out", "own", "other"]),
        ],
        dict(
            low=hidden_low,
            edge=edge_low,
            wo=w_out,
            wo2=w_out2,
            qkv=qkv,
            col=seg_col,
            row=seg_row,
            context=context,
            normed=normed,
        ),
        dict(
            g=shape_of((ext, width), BF16),
            out=group_shape,
            own=shape_of((2 * width, half), BF16),
            other=shape_of((2 * width, half), BF16),
        ),
        attn_temps,
    )
    early_got = swap(early_got)
    step(fc2, fc1)
    (grad_b,) = fused(
        [(attn_back(1), ["qkv", "g", "col", "row", "out", "dq", "dk", "dv"])],
        dict(qkv=qkv, g=grad_context, col=seg_col, row=seg_row),
        dict(out=group_shape),
        attn_temps,
    )
    early = begin(early_own, early_got)
    step(fc2, fc1)
    grad_input, vectors, late_own, late_got = fused(
        [
            (attn_back(2), ["qkv", "g", "col", "row", "gc", "dq", "dk", "dv"]),
            (
                grad_tokens_body,
                ["ga", "gb", "gc", "w", "w2", "tokens", "gh", "gains", "two", "s", "s2", "factor", "out", "sums"],
            ),
            (late_grad_body, ["normed", "gb", "gc", "own", "other"]),
        ],
        dict(
            qkv=qkv,
            g=grad_context,
            col=seg_col,
            row=seg_row,
            ga=grad_a,
            gb=grad_b,
            w=w_qkv,
            w2=w_qkv2,
            tokens=tokens,
            gh=grad_hidden,
            gains=norm_gains,
            two=sums_two,
            s=sums,
            s2=sums2,
            factor=factor,
            normed=normed,
        ),
        dict(
            out=shape_of((own, width), F32),
            sums=shape_of((16, width), F32),
            own=shape_of((width, width), BF16),
            other=shape_of((width, width), BF16),
        ),
        dict(gc=group_shape, **attn_temps),
    )
    late_got = swap(late_got)
    vectors = lax.all_gather(vectors, ("dp", "mp"), axis=0, tiled=True)
    step(fc2, fc1)
    if fast:
        early.step(20)
    late = begin(late_own, late_got)
    output = output_call(act, act2, w_fc2, w_fc22, hidden_one, row_biases)
    step(fc2, fc1)
    if fast:
        step(late, early, fc2, fc1)
        step(late, early, fc2, fc1)
        step(late, early, fc2, fc1)
        step(late, early)
        grad_fc2 = last_rows(sides[0], fc2.kept, fc2.got)
        step(late, early)
        grad_fc1 = last_rows(sides[0], fc1.kept, fc1.got)
        step(late, early)
        step(late)
        grad_out, grad_qkv = last_qkv(sides[0], early.kept, early.got, late.kept, late.got)
    else:
        total = lambda kept, got: (kept.astype(F32) + got.astype(F32)) * factor[0, 0]
        grad_fc2 = sum_any(total(fc2_own, fc2_got))
        grad_fc1 = sum_any(total(fc1_own, fc1_got))
        first = total(early_own, early_got).reshape(4, half, half)
        second = total(late_own, late_got)
        grad_out = sum_any(jnp.concatenate([first[0], first[2]], axis=1))
        first = jnp.concatenate([first[1], first[3]])
        part = lambda a, at: a[:, at : at + TILE]
        parts = [
            jnp.concatenate([part(first, t * TILE), part(second, t * TILE), part(second, half + t * TILE)], axis=1)
            for t in range(3)
        ]
        grad_qkv = sum_any(jnp.stack(parts))
    gains, shifts, grad_qv_bias, grad_b_fc1 = vectors_call(core, vectors, half, hidden_half)
    return (
        output,
        grad_input,
        gains,
        shifts,
        grad_qkv,
        grad_qv_bias,
        grad_out,
        grad_fc1,
        grad_b_fc1.reshape(hidden_half),
        grad_fc2,
    )


def solution(mesh):
    placed = (
        P(("dp", "mp"), None),
        P(("dp", "mp"), None),
        P("dp", None),
        P("dp"),
        P(),
        P(),
        P(None, None, "mp"),
        P(None, "mp"),
        P("mp", None),
        P(None, "mp"),
        P("mp"),
        P("mp", None),
    )
    return jax.shard_map(
        local,
        mesh=mesh,
        in_specs=placed,
        out_specs=(
            P(("dp", "mp"), None),
            P(("dp", "mp"), None),
            P(),
            P(),
            P(None, None, "mp"),
            P(None, "mp"),
            P("mp", None),
            P(None, "mp"),
            P("mp"),
            P("mp", None),
        ),
        check_vma=False,
    )
```

```python
import functools

import jax
import jax.numpy as jnp
from jax import lax
from jax.experimental import pallas as pl
from jax.experimental.pallas import tpu as pltpu
from jax.sharding import PartitionSpec as P

TILE = 128
MASKED = -3e38
F32 = jnp.float32
BF16 = jnp.bfloat16

def pick_heads(block):
    lane = lax.broadcasted_iota(jnp.int32, block.shape, 1)
    zero = jnp.zeros_like(block)
    return jnp.concatenate([jnp.where(lane < 64, block, zero), jnp.where(lane < 64, zero, block)], axis=0)

def join_heads(both):
    half = both.shape[1] // 2
    row = lax.broadcasted_iota(jnp.int32, (both.shape[0], half), 0)
    return jnp.where(row < 64, both[:, :half], both[:, half:]).T

def window(tiles, i):
    return [pl.multiple_of(lax.rem(i + step, tiles) * TILE, TILE) for step in (tiles - 1, 0, 1)]

def bias_of(starts, seg_col_ref, seg_row):
    keys = jnp.concatenate([seg_col_ref[pl.ds(s, TILE), :] for s in starts], axis=0)
    bias = jnp.where(keys == seg_row, 0.0, MASKED).astype(F32)
    return jnp.concatenate([bias, bias], axis=1)

def rows_of(ref, starts, cols):
    return jnp.concatenate([ref[pl.ds(s, TILE), cols] for s in starts], axis=0)


HEAD_DIM = 64
GROUPS = 3
LEN_NORM = 64
EPS = 1e-06
GELU_C = 0.7978845608028654
VMEM = pl.BlockSpec(memory_space=pltpu.VMEM)
SMEM = pl.BlockSpec(memory_space=pltpu.SMEM)
HBM = pl.BlockSpec(memory_space=pltpu.MemorySpace.HBM)
ANY = pl.BlockSpec(memory_space=pl.ANY)


def dot(a, b):
    return jnp.dot(a, b, preferred_element_type=F32)


def dot_nt(a, b):
    return lax.dot_general(a, b, (((1,), (1,)), ((), ())), preferred_element_type=F32)


def dot_tn(a, b):
    return lax.dot_general(a, b, (((0,), (0,)), ((), ())), preferred_element_type=F32)


def shape_of(shape, dtype):
    return jax.ShapeDtypeStruct(shape, dtype)


def nbytes(a):
    size = a.dtype.itemsize
    for n in a.shape:
        size *= n
    return size


class Order:
    token = None


CHUNK = 256
FLOPS_A_MICRO = 1_150_000_000


def in_hbm(x):
    return pltpu.with_memory_space_constraint(x, pltpu.MemorySpace.HBM)


def fused(steps, inputs, outs, temps=None, scalars=(), raw=(), chunked=(), free=(), limit=22, ahead=1, micros=10):
    temps = temps or {}
    waits = [a for a in (Order.token,) if a is not None]
    names = list(inputs)
    loaded = [k for k in names if k not in scalars and k not in raw]
    buffers = {k: inputs[k] for k in loaded} | outs | temps
    is_sem = lambda v: not isinstance(v, (jax.Array, jax.ShapeDtypeStruct))
    kinds = [v if is_sem(v) else pltpu.VMEM(v.shape, v.dtype) for v in buffers.values()]
    sem_of, count = {}, 0
    for k in (*loaded, *outs):
        sem_of[k] = count
        count += buffers[k].shape[0] // CHUNK if k in chunked else 1
    first = {k: min(n for n, (_, used) in enumerate(steps) if k in used) for k in loaded}
    last = {k: max(n for n, (_, used) in enumerate(steps) if k in used) for k in outs}

    def body(*refs):
        given = dict(zip(names, refs))
        results = dict(zip(outs, refs[len(names) + len(waits) :]))
        token_ref = refs[len(names) + len(waits) + len(outs)]
        rest = refs[len(names) + len(waits) + len(outs) + 1 :]
        held, sems = dict(zip(buffers, rest)), rest[len(buffers)]
        token_ref[...] = jnp.zeros_like(token_ref)
        place = {k: given[k] for k in (*scalars, *raw)} | held

        def pieces(k, source, target):
            if k not in chunked:
                return [pltpu.make_async_copy(source, target, sems.at[sem_of[k]])]
            rows = [pl.ds(r, CHUNK) for r in range(0, buffers[k].shape[0], CHUNK)]
            return [
                pltpu.make_async_copy(source.at[at], target.at[at], sems.at[sem_of[k] + n]) for n, at in enumerate(rows)
            ]

        loads = {k: pieces(k, given[k], held[k]) for k in loaded}
        stores = {k: pieces(k, held[k], results[k]) for k in outs}

        def start(n):
            mine = [loads[k] for k in loaded if first[k] == n]
            for copies in [c for c in mine if len(c) == 1]:
                copies[0].start()
            for n in range(max([len(c) for c in mine], default=0)):
                for copies in mine:
                    if 1 < len(copies) and n < len(copies):
                        copies[n].start()

        def ready(r, *which):
            for k in which or loaded:
                if k in chunked:
                    loads[k][r // CHUNK].wait()

        def done(r):
            for k in outs:
                if k in chunked:
                    stores[k][r // CHUNK].start()

        for n in range(ahead):
            start(n)
        for n, (fn, used) in enumerate(steps):
            start(n + ahead)
            code = getattr(fn, "__code__", None)
            piecewise = chunked and code is not None and "ready" in code.co_varnames
            hooks = dict(ready=ready, done=done) if piecewise else {}
            for k in loaded:
                if first[k] == n and k not in chunked:
                    loads[k][0].wait()
            fn(*(place[k] for k in used), **hooks)
            for k in outs:
                if last[k] == n and k not in chunked:
                    stores[k][0].start()
        for k in outs:
            for copy in stores[k]:
                copy.wait()

    size = sum(nbytes(v) for v in buffers.values() if not is_sem(v))
    pad = sum(nbytes(v) * 128 for v in buffers.values() if not is_sem(v) and v.shape[-1] == 1)
    kernel = pl.pallas_call(
        body,
        in_specs=[SMEM if k in scalars else ANY if k in free else HBM for k in names] + [ANY] * len(waits),
        out_specs=[HBM] * len(outs) + [VMEM],
        out_shape=[*(pltpu.MemorySpace.HBM(v.shape, v.dtype) for v in outs.values()), shape_of((8, 128), F32)],
        scratch_shapes=[*kinds, pltpu.SemaphoreType.DMA((count,))],
        compiler_params=pltpu.CompilerParams(vmem_limit_bytes=(limit << 20) + size + pad),
        cost_estimate=pl.CostEstimate(flops=micros * FLOPS_A_MICRO + 1, bytes_accessed=1, transcendentals=0),
    )
    operands = [v if k in scalars or k in free else in_hbm(v) for k, v in inputs.items()]
    *results, Order.token = kernel(*operands, *waits)
    return results


def stream(body, args, outs, scalars=0, limit=22, chunked=()):
    named = {f"in{n}": a for n, a in enumerate(args)}
    made = {f"out{n}": a for n, a in enumerate(outs)}
    every = [*named, *made]
    return fused(
        [(body, every)],
        named,
        made,
        scalars=every[:scalars],
        chunked=[every[n] for n in chunked],
        limit=limit,
    )


def call(body, args, outs, scalars=0, limit=22, micros=0):
    outs = list(outs)
    waits = [a for a in (Order.token,) if a is not None]
    n_in, n_wait, n_out = len(args), len(waits), len(outs)

    def tied(*refs):
        token_ref = refs[n_in + n_wait + n_out]
        token_ref[...] = jnp.zeros_like(token_ref)
        body(*refs[:n_in], *refs[n_in + n_wait : n_in + n_wait + n_out])

    *results, Order.token = pl.pallas_call(
        tied,
        in_specs=[SMEM] * scalars + [VMEM] * (n_in - scalars) + [ANY] * n_wait,
        out_specs=[VMEM] * (n_out + 1),
        out_shape=outs + [shape_of((8, 128), F32)],
        compiler_params=pltpu.CompilerParams(vmem_limit_bytes=limit << 20),
        cost_estimate=pl.CostEstimate(
            flops=micros * FLOPS_A_MICRO + 1, bytes_accessed=sum(nbytes(a) for a in [*args, *outs]) // 64, transcendentals=0
        ),
    )(*args, *waits)
    return results


def norm_parts(values):
    center = values - jnp.mean(values, axis=-1, keepdims=True)
    rstd = lax.rsqrt(jnp.mean(center * center, axis=-1, keepdims=True) + EPS)
    return center * rstd, rstd


def norm_back(grad, unit, rstd, gain):
    scaled = grad * gain
    return rstd * (
        scaled
        - jnp.mean(scaled, axis=-1, keepdims=True)
        - unit * jnp.mean(scaled * unit, axis=-1, keepdims=True)
    )


def fold(a):
    return jnp.sum(a.astype(F32), axis=0, keepdims=True)


def prep_body(core_ref, lengths_ref, grad_ref, col_ref, row_ref, len_ref, low_ref):
    ext, own = col_ref.shape[0], len_ref.shape[0]
    slots = lengths_ref.shape[1]
    pad = jnp.zeros((1, 128 - slots), F32)
    lengths = jnp.concatenate([lengths_ref[...].astype(F32), pad], axis=1)
    before = lax.broadcasted_iota(jnp.int32, (128, 128), 0) <= lax.broadcasted_iota(jnp.int32, (128, 128), 1)
    ends = dot(jnp.broadcast_to(lengths, (8, 128)).astype(BF16), jnp.where(before, 1.0, 0.0).astype(BF16))[0:1]
    lane = lax.broadcasted_iota(jnp.int32, (1, 128), 1)
    ends = jnp.where(lane < slots, ends, 1e9)
    row = lax.broadcasted_iota(jnp.int32, (ext, 1), 0)
    core = core_ref[0]
    edge = jnp.where(core == 0, 0, -own - (ext - own))
    position = row + jnp.where(row < own, core * own, edge + core * own)
    past = jnp.where(position.astype(F32) >= ends, 1.0, 0.0)
    segment = jnp.sum(past, axis=1, keepdims=True)
    col_ref[...] = segment
    row_ref[...] = dot_nt(jnp.ones((8, 128), BF16), past.astype(BF16))[0:1]
    hit = jnp.where(segment[:own] == lane.astype(F32), lengths, 0.0)
    length = jnp.sum(hit, axis=1, keepdims=True)
    weight = jnp.where(length > 0, LEN_NORM / jnp.maximum(length, 1.0), 0.0)
    len_ref[...] = weight
    low_ref[...] = (grad_ref[...].astype(F32) * weight).astype(BF16)


def factor_body(group_ref, counts_ref, factor_ref):
    lane = lax.broadcasted_iota(jnp.int32, (1, 128), 1)
    counts = jnp.where(lane < GROUPS, fold(counts_ref[:, :128]) * 0.5, 0.0)
    roots = jnp.sqrt(counts)
    all_images = jnp.sum(counts, axis=1, keepdims=True)
    all_roots = jnp.sum(roots, axis=1, keepdims=True)
    root = jnp.sum(jnp.where(lane == group_ref[0], roots, 0.0), axis=1, keepdims=True)
    factor_ref[...] = jnp.broadcast_to(all_images / (root * all_roots), factor_ref.shape)


def factor_call(group, counts):
    return call(factor_body, (group, counts), [shape_of((8, 128), F32)], scalars=1)[0]


def edge_body(core_ref, other_ref, halo_ref, sem):
    rows = pl.ds(pl.multiple_of(core_ref[0] * (other_ref.shape[0] - TILE), TILE), TILE)
    load = pltpu.make_async_copy(other_ref.at[rows], halo_ref, sem)
    load.start()
    load.wait()


def qkv_body(tokens_ref, halo_ref, gains_ref, biases_ref, w_ref, w2_ref, b_ref, b2_ref, normed_ref, out_ref):
    own, width = tokens_ref.shape
    ext = normed_ref.shape[0]
    for r, ref in [(r, tokens_ref) for r in range(0, own, 256)] + [(own, halo_ref)]:
        n = min(256, ext - r)
        at = 0 if ref is halo_ref else r
        unit, _ = norm_parts(ref[at : at + n, :].astype(F32))
        normed = (unit * gains_ref[0:1, :] + biases_ref[0:1, :]).astype(BF16)
        normed_ref[r : r + n, :] = normed
        for t in range(3):
            weights = jnp.concatenate([w_ref[t], w2_ref[t]], axis=1)
            part = dot(normed, weights)
            if t != 1:
                row = t // 2
                part = part + jnp.concatenate([b_ref[row : row + 1, :], b2_ref[row : row + 1, :]], axis=1)
            out_ref[r : r + n, t * width : (t + 1) * width] = part.astype(BF16)


def out_norm_body(ctx_ref, tok_ref, w_ref, w2_ref, gains_ref, biases_ref, hid_ref, norm_ref):
    weights = jnp.concatenate([w_ref[...], w2_ref[...]], axis=0)
    own = tok_ref.shape[0]
    product = lambda r: dot(ctx_ref[r : r + 256, :], weights)
    ready = product(0)
    for r in range(0, own, 256):
        later = product(r + 256) if r + 256 < own else None
        rows = slice(r, r + 256)
        hidden = tok_ref[rows, :].astype(F32) + ready + biases_ref[2:3, :]
        hid_ref[rows, :] = hidden
        unit, _ = norm_parts(hidden)
        norm_ref[rows, :] = (unit * gains_ref[1:2, :] + biases_ref[1:2, :]).astype(BF16)
        ready = later


def ffn_body(x_ref, g_ref, w_ref, b_ref, v_ref, act_ref, gb_ref, sum_ref, *, ready=None, done=None):
    cols = 256
    hidden = w_ref.shape[1]

    def products(rows, j, first=False):
        if first and ready:
            ready(j, "v")
        v = dot(x_ref[rows, :], w_ref[:, j : j + cols]) + b_ref[:, j : j + cols]
        return v, dot_nt(g_ref[rows, :], v_ref[j : j + cols, :])

    def one(r, first):
        rows = pl.ds(r, 256)
        now = products(rows, 0, first)
        for j in range(0, hidden, cols):
            later = products(rows, j + cols, first) if j + cols < hidden else None
            v, grad = now
            u = v * v
            gate = 0.5 * jnp.tanh(v * (GELU_C + (GELU_C * 0.044715) * u)) + 0.5
            act = v * gate
            act_ref[rows, j : j + cols] = act.astype(BF16)
            slope = gate + act * (1.0 - gate) * (2 * GELU_C + (GELU_C * 6 * 0.044715) * u)
            low = (grad * slope).astype(BF16)
            gb_ref[rows, j : j + cols] = low
            sum_ref[:, j : j + cols] += fold(low)
            now = later

    sum_ref[...] = jnp.zeros_like(sum_ref)
    tiles = x_ref.shape[0] // 256
    start = 0
    if ready:
        ready(0, "x", "g")
        one(0, True)
        for r in range(256, x_ref.shape[0], 256):
            ready(r, "x", "g")
        start = 1

    def body(i, _):
        one(pl.multiple_of(i * 256, 256), False)
        return 0

    lax.fori_loop(start, tiles, body, 0)


def fc2_grad_body(act_ref, low_ref, out_ref):
    for r in range(0, out_ref.shape[0], 256):
        out_ref[r : r + 256, :] = dot_tn(act_ref[:, r : r + 256], low_ref[...]).astype(BF16)


def fc1_grad_body(x_ref, gb_ref, out_ref):
    for r in range(0, out_ref.shape[0], 256):
        out_ref[r : r + 256, :] = dot_tn(x_ref[:, r : r + 256], gb_ref[...]).astype(BF16)


def early_grad_body(ctx_ref, low_ref, norm_ref, ga_ref, own_ref, other_ref):
    half = own_ref.shape[1]
    own = low_ref.shape[0]
    for h in range(2):
        cols, at = slice(h * half, (h + 1) * half), 2 * h * half
        other_ref[at : at + half, :] = dot_tn(ctx_ref[:, half:], low_ref[:, cols]).astype(BF16)
        own_ref[at : at + half, :] = dot_tn(ctx_ref[:, :half], low_ref[:, cols]).astype(BF16)
        both = dot_tn(norm_ref[:own, cols], ga_ref[...]).astype(BF16)
        own_ref[at + half : at + 2 * half, :] = both[:, :half]
        other_ref[at + half : at + 2 * half, :] = both[:, half:]


def late_grad_body(norm_ref, gb_ref, gc_ref, own_ref, other_ref):
    own, half = gb_ref.shape[0], gb_ref.shape[1] // 2
    for r in range(0, own_ref.shape[0], 256):
        for n, ref in enumerate((gb_ref, gc_ref)):
            both = dot_tn(norm_ref[:own, r : r + 256], ref[...]).astype(BF16)
            own_ref[r : r + 256, n * half : (n + 1) * half] = both[:, :half]
            other_ref[r : r + 256, n * half : (n + 1) * half] = both[:, half:]


def edge_copies(core_ref, sources, targets, sems):
    at = (1 - core_ref[0]) * (sources[0].shape[0] - TILE)
    rows = pl.ds(pl.multiple_of(at, TILE), TILE)
    return [pltpu.make_async_copy(a.at[rows], b, sems.at[n]) for n, (a, b) in enumerate(zip(sources, targets))]


def edge_load_body(core_ref, a_ref, b_ref, c_ref, d_ref, a2_ref, b2_ref, c2_ref, d2_ref, sems):
    for copy in edge_copies(core_ref, (a_ref, b_ref, c_ref, d_ref), (a2_ref, b2_ref, c2_ref, d2_ref), sems):
        copy.start()


def edge_grad_body(
    core_ref, a_ref, b_ref, c_ref, d_ref, a2_ref, hid_ref, og_ref, wr_ref, sems, gb_ref, w_ref, w2_ref, gains_ref, out_ref
):
    for copy in edge_copies(core_ref, (a_ref, b_ref, c_ref, d_ref), (a2_ref, hid_ref, og_ref, wr_ref), sems):
        copy.wait()
    rows = pl.ds(pl.multiple_of((1 - core_ref[0]) * (gb_ref.shape[0] - TILE), TILE), TILE)
    grad = dot_nt(gb_ref[rows, :], w_ref[...]) + dot_nt(a2_ref[...], w2_ref[...])
    unit, rstd = norm_parts(hid_ref[...])
    back = norm_back(grad, unit, rstd, gains_ref[1:2, :])
    out_ref[...] = (back + og_ref[...].astype(F32) * wr_ref[...]).astype(BF16)


def grad_hidden_body(gb_ref, gb2_ref, w_ref, w2_ref, hid_ref, og_ref, wr_ref, gains_ref, gh_ref, low_ref, sums_ref, *, ready, done):
    def product(r):
        ready(r)
        rows = slice(r, r + 256)
        return dot_nt(gb_ref[rows, :], w_ref[...]) + dot_nt(gb2_ref[rows, :], w2_ref[...])

    own = hid_ref.shape[0]
    now, sums = product(0), [0.0] * 4
    for r in range(0, own, 256):
        later = product(r + 256) if r + 256 < own else None
        rows, grad = slice(r, r + 256), now
        unit, rstd = norm_parts(hid_ref[rows, :])
        cot = og_ref[rows, :].astype(F32) * wr_ref[rows, :]
        hidden = norm_back(grad, unit, rstd, gains_ref[1:2, :]) + cot
        gh_ref[rows, :] = hidden
        low_ref[rows, :] = hidden.astype(BF16)
        done(r)
        sums = [a + fold(b) for a, b in zip(sums, (grad * unit, grad, hidden, cot))]
        now = later
    for row, a in enumerate(sums):
        sums_ref[row : row + 1, :] = a


def grad_hidden_call(gb, gb2, w, w2, hidden, out_grad, weight_col, gains):
    rows, width = hidden.shape
    return stream(
        grad_hidden_body,
        (gb, gb2, w, w2, hidden, out_grad, weight_col, gains),
        [shape_of((rows, width), F32), shape_of((rows, width), BF16), shape_of((8, width), F32)],
        chunked=(0, 1, 4, 5, 6, 8, 9),
    )


def gctx_body(x_ref, h_ref, w_ref, w2_ref, out_ref):
    own = x_ref.shape[0]
    for r in range(0, own, 256):
        weights = jnp.concatenate([w_ref[...], w2_ref[...]], axis=0)
        out_ref[r : r + 256, :] = dot_nt(x_ref[r : r + 256, :], weights).astype(BF16)
    weights = jnp.concatenate([w_ref[...], w2_ref[...]], axis=0)
    out_ref[own:, :] = dot_nt(h_ref[...], weights).astype(BF16)


def grad_tokens_body(
    ga_ref, gb_ref, gc_ref, w_ref, w2_ref, tok_ref, gh_ref, gains_ref, two_ref, s_ref, s2_ref, factor_ref, out_ref, sums_ref
):
    factor = factor_ref[0:1, 0:1]
    width = tok_ref.shape[1]
    sums_ref[...] = jnp.zeros_like(sums_ref)
    sums_ref[2:6, :] = two_ref[0:4, :]
    for n, ref in enumerate((s_ref, s2_ref)):
        for r in range(2):
            row = 9 + 2 * n + r
            sums_ref[row : row + 1, :] = ref[:, r * width : (r + 1) * width]
    groups = (ga_ref, gb_ref, gc_ref)

    def product(r):
        grad = jnp.zeros((256, width), F32)
        for n, ref in enumerate(groups):
            cols = slice(n * TILE, (n + 1) * TILE)
            weights = [w[t, :, cols] for w in (w_ref, w2_ref) for t in range(3)]
            grad = grad + dot_nt(ref[r : r + 256, :], jnp.concatenate(weights, axis=1))
        return grad

    own = tok_ref.shape[0]
    now, sums = product(0), [0.0] * 5
    for r in range(0, own, 256):
        later = product(r + 256) if r + 256 < own else None
        rows, grad = slice(r, r + 256), now
        unit, rstd = norm_parts(tok_ref[rows, :].astype(F32))
        out_ref[rows, :] = (norm_back(grad, unit, rstd, gains_ref[0:1, :]) + gh_ref[rows, :]) * factor
        terms = (grad * unit, grad, *(ref[rows, :] for ref in groups))
        sums = [a + fold(b) for a, b in zip(sums, terms)]
        now = later
    for row, a in zip((0, 1, 6, 7, 8), sums):
        sums_ref[row : row + 1, :] = a
    sums_ref[...] = sums_ref[...] * factor


def vectors_body(core_ref, all_ref, gains_ref, shifts_ref, qv_ref, fc1_ref):
    blocks = all_ref.shape[0] // 32
    width = all_ref.shape[1]
    half = qv_ref.shape[1]
    total = all_ref[0:32, :]
    for b in range(1, blocks):
        total = total + all_ref[32 * b : 32 * (b + 1), :]
    mine = jnp.where(core_ref[0] == 0, total[:16], total[16:])
    peer = jnp.where(core_ref[0] == 0, total[16:], total[:16])
    both = mine + peer
    gains_ref[0:1, :] = both[0:1]
    gains_ref[1:2, :] = both[2:3]
    shifts_ref[0:1, :] = both[1:2]
    shifts_ref[1:4, :] = both[3:6]
    for n in range(3):
        both = mine[6 + n : 7 + n, :half] + peer[6 + n : 7 + n, half:]
        for row, t in ((0, 0), (1, 2)):
            qv_ref[row : row + 1, n * TILE : (n + 1) * TILE] = both[:, t * TILE : (t + 1) * TILE]
    for r in range(2):
        fc1_ref[:, r * width : (r + 1) * width] = mine[9 + r : 10 + r] + peer[11 + r : 12 + r]


def vectors_call(core, everything, half, hidden_half):
    width = everything.shape[1]
    return call(
        vectors_body,
        (core, everything),
        [shape_of((2, width), F32), shape_of((4, width), F32), shape_of((2, half), F32), shape_of((1, hidden_half), F32)],
        scalars=1,
    )


def output_body(a_ref, a2_ref, w_ref, w2_ref, hid_ref, biases_ref, out_ref, *, ready, done):
    for r in range(0, hid_ref.shape[0], 256):
        ready(r)
        rows = slice(r, r + 256)
        mlp = dot(a_ref[rows, :], w_ref[...]) + dot(a2_ref[rows, :], w2_ref[...])
        out_ref[rows, :] = (hid_ref[rows, :] + mlp + biases_ref[3:4, :]).astype(BF16)
        done(r)


def output_call(a, a2, w, w2, hidden, biases):
    return stream(
        output_body, (a, a2, w, w2, hidden, biases), [shape_of(hidden.shape, BF16)], chunked=(0, 1, 4, 6)
    )[0]


SCALE = HEAD_DIM ** (-0.5)


def attn_fwd_body(
    core_ref,
    lengths_ref,
    qkv_ref,
    seg_col_ref,
    seg_row_ref,
    normed_ref,
    other_ref,
    gains_ref,
    biases_ref,
    w_ref,
    w2_ref,
    b_ref,
    b2_ref,
    out_ref,
    far_ref,
    wide_ref,
    keys_ref,
    values_ref,
    sem,
):
    own, width = out_ref.shape
    tiles = qkv_ref.shape[0] // TILE

    pairs = width // TILE
    lane = lax.broadcasted_iota(jnp.int32, (TILE, TILE), 1)

    def one(i, _):
        starts = window(tiles, i)
        here = pl.ds(starts[1], TILE)
        bias = bias_of(starts, seg_col_ref, seg_row_ref[:, here])
        cols = lambda t, p: slice(t * width + p * TILE, t * width + (p + 1) * TILE)
        scores, probs = {}, {}
        for step in range(pairs + 2):
            if step < pairs:
                queries = pick_heads(qkv_ref[here, cols(0, step)] * jnp.asarray(SCALE, BF16))
                scores[step] = dot_nt(rows_of(qkv_ref, starts, cols(1, step)), queries) + bias
            p = step - 1
            if 0 <= p < pairs:
                expo = jnp.exp(scores[p] - jnp.max(scores[p], axis=0, keepdims=True))
                probs[p] = (expo * (1.0 / jnp.sum(expo, axis=0, keepdims=True))).astype(BF16)
            p = step - 2
            if 0 <= p < pairs:
                both = dot_tn(probs[p], rows_of(qkv_ref, starts, cols(2, p)))
                out_ref[here, cols(0, p)] = jnp.where(lane < HEAD_DIM, both[:TILE], both[TILE:]).astype(BF16)
        return 0

    lax.fori_loop(0, own // TILE, one, 0)
    total_rows = lax.fori_loop(0, lengths_ref.shape[1], lambda j, n: n + lengths_ref[0, j], jnp.int32(0))
    first_row = core_ref[0] * own

    @pl.when(total_rows < 2 * own - TILE)
    def _():
        load = pltpu.make_async_copy(other_ref, far_ref, sem)
        load.start()
        load.wait()

        @pl.loop(0, own // TILE)
        def _(i):
            rows = pl.ds(pl.multiple_of(i * TILE, TILE), TILE)
            unit, _ = norm_parts(far_ref[rows, :].astype(F32))
            far_ref[rows, :] = (unit * gains_ref[0:1, :] + biases_ref[0:1, :]).astype(BF16)

        key_row = lax.broadcasted_iota(jnp.int32, (2 * own, 1), 0) + first_row
        key_row = jnp.where(key_row >= 2 * own, key_row - 2 * own, key_row)
        wide_ref[...] = jnp.where(key_row >= total_rows, 0.0, MASKED)
        for side, (wide, bias_ref) in enumerate(((w_ref, b_ref), (w2_ref, b2_ref))):
            half = wide.shape[2]

            @pl.loop(0, half // TILE)
            def _(p):
                at = pl.multiple_of(p * TILE, TILE)
                base = pl.multiple_of(side * half + p * TILE, TILE)
                for t, ref in ((1, keys_ref), (2, values_ref)):
                    ref[:own, :] = qkv_ref[:own, pl.ds(pl.multiple_of(t * width + base, TILE), TILE)]
                    part = dot(far_ref[...], wide[t, :, pl.ds(at, TILE)])
                    if t == 2:
                        part = part + bias_ref[1:2, pl.ds(at, TILE)]
                    ref[own:, :] = part.astype(BF16)

                @pl.loop(0, own // TILE)
                def _(i):
                    rows = pl.ds(pl.multiple_of(i * TILE, TILE), TILE)
                    queries = pick_heads(qkv_ref[rows, pl.ds(base, TILE)] * jnp.asarray(SCALE, BF16))
                    scores = dot_nt(keys_ref[...], queries) + wide_ref[...]
                    top = jnp.max(scores, axis=0, keepdims=True)
                    expo = jnp.exp(scores - top)
                    probs = (expo * (1.0 / jnp.sum(expo, axis=0, keepdims=True))).astype(BF16)
                    full = join_heads(dot_tn(values_ref[...], probs)).astype(BF16)
                    row = lax.broadcasted_iota(jnp.int32, (TILE, TILE), 0) + i * TILE + first_row
                    out_ref[rows, pl.ds(base, TILE)] = jnp.where(row >= total_rows, full, out_ref[rows, pl.ds(base, TILE)])


def attn_bwd_body(qkv_ref, g_ref, seg_col_ref, seg_row_ref, out_ref, dq_ref, dk_ref, dv_ref, *, pairs, turns):
    tiles = qkv_ref.shape[0] // TILE
    own, width = out_ref.shape[0], qkv_ref.shape[1] // 3
    dk_ref[...] = jnp.zeros_like(dk_ref)
    dv_ref[...] = jnp.zeros_like(dv_ref)

    def load(starts, here, p):
        cols = lambda t: slice(t * width + p * TILE, t * width + (p + 1) * TILE)
        queries = pick_heads(qkv_ref[here, cols(0)] * jnp.asarray(SCALE, BF16))
        keys, values = rows_of(qkv_ref, starts, cols(1)), rows_of(qkv_ref, starts, cols(2))
        return queries, keys, values, pick_heads(g_ref[here, cols(0)])

    def products(arrays, bias):
        queries, keys, values, grads = arrays
        return dot_nt(keys, queries) + bias, dot_nt(values, grads)

    def softmax_back(scores, grad_probs):
        expo = jnp.exp(scores - jnp.max(scores, axis=0, keepdims=True))
        probs = expo * (1.0 / jnp.sum(expo, axis=0, keepdims=True))
        mean = jnp.sum(probs * grad_probs, axis=0, keepdims=True)
        return probs.astype(BF16), (probs * (grad_probs - mean)).astype(BF16)

    def finish(starts, here, at, arrays, probs, grad_scores):
        queries, keys, _, grads = arrays
        cols = slice(at * TILE, (at + 1) * TILE)
        dv, dk = dot(probs, grads), dot(grad_scores, queries)
        for k, s in enumerate(starts):
            part = slice(k * TILE, (k + 1) * TILE)
            dk_ref[pl.ds(s, TILE), cols] += dk[part]
            dv_ref[pl.ds(s, TILE), cols] += dv[part]
        dq_ref[here, cols] = (join_heads(dot_tn(keys, grad_scores)) * SCALE).astype(BF16)

    def one(i, _):
        work = []
        for turn in range(turns):
            starts = window(tiles, i * turns + turn)
            here = pl.ds(starts[1], TILE)
            bias = bias_of(starts, seg_col_ref, seg_row_ref[:, here])
            work += [(starts, here, bias, at, p) for at, p in enumerate(pairs)]
        first, second = {}, {}
        for step in range(len(work) + 2):
            if step < len(work):
                starts, here, bias, at, p = work[step]
                first[step] = products(load(starts, here, p), bias)
            if 0 <= step - 1 < len(work):
                second[step - 1] = softmax_back(*first.pop(step - 1))
            if 0 <= step - 2 < len(work):
                starts, here, bias, at, p = work[step - 2]
                finish(starts, here, at, load(starts, here, p), *second.pop(step - 2))
        return 0

    lax.fori_loop(0, tiles // turns, one, 0)
    half = len(pairs) * TILE // 2
    for side in range(2):
        cols = slice(side * half, (side + 1) * half)
        base = side * 3 * half
        out_ref[:, base : base + half] = dq_ref[:own, cols]
        out_ref[:, base + half : base + 2 * half] = dk_ref[:own, cols].astype(BF16)
        out_ref[:, base + 2 * half : base + 3 * half] = dv_ref[:own, cols].astype(BF16)


def half_of(side_ref, flip):
    return 1 - side_ref[0] if flip else side_ref[0]


def first_split_body(side_ref, kept_ref, got_ref, factor_ref, send_ref, keep_ref):
    half = keep_ref.shape[0]
    factor = factor_ref[0:1, 0:1]
    total = lambda at: (kept_ref[pl.ds(at, half), :].astype(F32) + got_ref[pl.ds(at, half), :].astype(F32)) * factor
    send_ref[...] = total(pl.multiple_of((1 - side_ref[0]) * half, 16)).astype(BF16)
    keep_ref[...] = total(pl.multiple_of(side_ref[0] * half, 16)).astype(BF16)


def first_split(side, kept, got, factor):
    half, cols = kept.shape[0] // 2, kept.shape[1]
    return call(
        first_split_body,
        (side, kept, got, factor),
        [shape_of((half, cols), BF16)] * 2,
        scalars=1,
    )


def split_two_body(side_ref, kept_ref, got_ref, send_ref, keep_ref):
    half = keep_ref.shape[0]
    total = lambda at: kept_ref[pl.ds(at, half), :].astype(F32) + got_ref[pl.ds(at, half), :].astype(F32)
    send_ref[...] = total(pl.multiple_of((1 - side_ref[0]) * half, 16)).astype(BF16)
    keep_ref[...] = total(pl.multiple_of(side_ref[0] * half, 16)).astype(BF16)


def split_two(side, kept, got, micros=0):
    half, cols = kept.shape[0] // 2, kept.shape[1]
    return call(
        split_two_body,
        (side, kept, got),
        [shape_of((half, cols), BF16)] * 2,
        scalars=1,
        micros=micros,
    )


def add_body(kept_ref, got_ref, out_ref):
    out_ref[...] = (kept_ref[...].astype(F32) + got_ref[...].astype(F32)).astype(BF16)


def add_two(kept, got):
    return call(add_body, (kept, got), [shape_of(kept.shape, BF16)])[0]


def join_body(side_ref, own_ref, got_ref, out_ref):
    half = own_ref.shape[0]
    out_ref[pl.ds(pl.multiple_of(side_ref[0] * half, 16), half), :] = own_ref[...]
    out_ref[pl.ds(pl.multiple_of((1 - side_ref[0]) * half, 16), half), :] = got_ref[...]


def join_two(side, own, got):
    half, cols = own.shape
    return call(join_body, (side, own, got), [shape_of((2 * half, cols), BF16)], scalars=1)[0]


def last_body(side_ref, own_ref, got_ref, out_ref):
    half = own_ref.shape[0]
    for flip, ref in ((False, own_ref), (True, got_ref)):
        out_ref[pl.ds(pl.multiple_of(half_of(side_ref, flip) * half, 16), half), :] = ref[...].astype(F32)


def last_rows(side, own, got):
    rows, cols = own.shape
    return call(last_body, (side, own, got), [shape_of((2 * rows, cols), F32)], scalars=1)[0]


def last_qkv_body(side_ref, a0_ref, a1_ref, b0_ref, b1_ref, wout_ref, wqkv_ref):
    half = wout_ref.shape[0]
    for flip, a_ref, b_ref in ((False, a0_ref, b0_ref), (True, a1_ref, b1_ref)):
        part = pl.ds(pl.multiple_of(half_of(side_ref, flip) * half, 128), half)
        wout_ref[:, part] = a_ref[:half, :].astype(F32)
        for t in range(3):
            wqkv_ref[t, part, :TILE] = a_ref[half:, t * TILE : (t + 1) * TILE].astype(F32)
            for n in range(2):
                at = n * half + t * TILE
                wqkv_ref[t, part, (1 + n) * TILE : (2 + n) * TILE] = b_ref[:, at : at + TILE].astype(F32)


def last_qkv(side, a0, a1, b0, b1):
    half = a0.shape[1]
    return call(
        last_qkv_body,
        (side, a0, a1, b0, b1),
        [shape_of((half, 2 * half), F32), shape_of((3, 2 * half, half), F32)],
        scalars=1,
    )


def swap(x):
    return lax.ppermute(x, "mp", [(0, 1), (1, 0)])


def exchange(x, bits, n):
    pairs = [(2 * d + m, 2 * (d ^ bits[m]) + m) for d in range(n) for m in range(2)]
    return lax.ppermute(x, ("dp", "mp"), pairs)


def sum_any(part):
    n = lax.axis_size("dp")
    shape = part.shape
    part = part.reshape(-1, shape[-1])
    if n & (n - 1) or part.shape[0] % n:
        return lax.psum(part, "dp").reshape(shape)
    d = lax.axis_index("dp")
    bits = [1 << k for k in range(n.bit_length() - 1)]
    for bit in bits:
        half = part.shape[0] // 2
        side = lax.rem(d // bit, 2)
        sent = lax.dynamic_slice_in_dim(part, (1 - side) * half, half).astype(BF16)
        kept = lax.dynamic_slice_in_dim(part, side * half, half)
        part = kept + exchange(sent, (bit, bit), n).astype(F32)
    total = part.astype(BF16)
    for bit in reversed(bits):
        side = lax.rem(d // bit, 2)
        got = exchange(total, (bit, bit), n)
        total = jnp.concatenate([jnp.where(side == 0, total, got), jnp.where(side == 0, got, total)], axis=0)
    return total.astype(F32).reshape(shape)


STAGES = ((1, 2), (2, 1), (4, 4), (8, 8))


class Bucket:
    def __init__(self, sides, sent, kept):
        self.sides, self.at, self.kept = sides, 0, kept
        self.got = exchange(sent, STAGES[0], 16)

    def step(self, micros=0):
        self.at += 1
        if self.at < 4:
            sent, self.kept = split_two(self.sides[self.at], self.kept, self.got, micros)
            self.got = exchange(sent, STAGES[self.at], 16)
        elif self.at == 4:
            self.kept = add_two(self.kept, self.got)
            self.got = exchange(self.kept, STAGES[3], 16)
        else:
            stage = 8 - self.at
            self.kept = join_two(self.sides[stage], self.kept, self.got)
            self.got = exchange(self.kept, STAGES[stage - 1], 16)


def local(
    tokens,
    out_grad,
    image_lengths,
    group_of_block,
    norm_gains,
    row_biases,
    w_qkv,
    qv_bias,
    w_out,
    w_fc1,
    b_fc1,
    w_fc2,
):
    own, width = tokens.shape
    half = w_qkv.shape[2]
    hidden_half = w_fc1.shape[1]
    row_count = own * 2
    n = lax.axis_size("dp")
    d, m = lax.axis_index("dp"), lax.axis_index("mp")
    Order.token = None

    tokens_other = swap(tokens)
    w_qkv2 = swap(w_qkv)
    qv_bias2 = swap(qv_bias)
    late_swap = lambda x: swap(lax.optimization_barrier((x, w_qkv2, tokens_other))[0])
    w_out2 = late_swap(w_out)
    w_fc12 = late_swap(w_fc1)
    w_fc22 = late_swap(w_fc2)
    b_fc12 = late_swap(b_fc1[None, :])

    core = m.astype(jnp.int32).reshape(1)
    ext = own + TILE
    images = jnp.sum((image_lengths > 0).astype(F32))
    lane = lax.broadcasted_iota(jnp.int32, (16, width), 1)
    row = lax.broadcasted_iota(jnp.int32, (16, width), 0)
    counts = jnp.where((row == 0) & (lane == group_of_block[0]), images, 0.0)
    counts = lax.all_gather(counts, ("dp", "mp"), axis=0, tiled=True)

    seg_col, seg_row, weight_col, out_low, normed, qkv, context = fused(
        [
            (prep_body, ["core", "lens", "og", "col", "row", "weight", "low"]),
            (edge_body, ["core", "other", "halo", "sem"]),
            (qkv_body, ["tokens", "halo", "gains", "biases", "w", "w2", "b", "b2", "normed", "qkv"]),
            (
                attn_fwd_body,
                ["core", "lengths", "qkv", "col", "row", "normed", "other", "gains", "biases"]
                + ["w", "w2", "b", "b2", "context", "far", "wide", "keys", "values", "sem"],
            ),
        ],
        dict(
            core=core,
            lengths=image_lengths,
            lens=image_lengths,
            og=out_grad,
            tokens=tokens,
            gains=norm_gains,
            biases=row_biases,
            w=w_qkv,
            w2=w_qkv2,
            b=qv_bias,
            b2=qv_bias2,
            other=tokens_other,
        ),
        dict(
            col=shape_of((ext, 1), F32),
            row=shape_of((1, ext), F32),
            weight=shape_of((own, 1), F32),
            low=shape_of((own, width), BF16),
            normed=shape_of((ext, width), BF16),
            qkv=shape_of((ext, 3 * width), BF16),
            context=shape_of((own, width), BF16),
        ),
        dict(
            halo=shape_of((TILE, width), BF16),
            far=shape_of((own, width), BF16),
            wide=shape_of((row_count, 1), F32),
            keys=shape_of((row_count, TILE), BF16),
            values=shape_of((row_count, TILE), BF16),
            sem=pltpu.SemaphoreType.DMA,
        ),
        scalars=("core", "lengths"),
        raw=("other",),
        free=("other", "w2", "b2"),
        ahead=3,
    )
    half_shapes = dict(
        act=shape_of((own, hidden_half), BF16),
        gb=shape_of((own, hidden_half), BF16),
        sums=shape_of((1, hidden_half), F32),
        grad2=shape_of((hidden_half, width), BF16),
        grad1=shape_of((width, hidden_half), BF16),
    )
    half_steps = [
        (ffn_body, ["x", "g", "w", "b", "v", "act", "gb", "sums"]),
        (fc2_grad_body, ["act", "g", "grad2"]),
        (fc1_grad_body, ["x", "gb", "grad1"]),
    ]
    hidden_one, normed_two, act2, gb2, sums2, fc2_got, fc1_got = fused(
        [(out_norm_body, ["context", "tokens", "wo", "wo2", "gains", "biases", "hidden", "x"]), *half_steps],
        dict(
            context=context,
            tokens=tokens,
            wo=w_out,
            wo2=w_out2,
            gains=norm_gains,
            biases=row_biases,
            g=out_low,
            w=w_fc12,
            b=b_fc12,
            v=w_fc22,
        ),
        dict(hidden=shape_of((own, width), F32), x=shape_of((own, width), BF16), **half_shapes),
    )
    fc2_got = swap(fc2_got)
    fc1_got = swap(fc1_got)
    edge_names = ["core", "gb2", "hidden", "og", "weight", "gb2e", "hiddene", "oge", "weighte", "sems"]
    act, gb, sums, fc2_own, fc1_own, edge_low = fused(
        [
            half_steps[0],
            (edge_load_body, edge_names),
            *half_steps[1:],
            (edge_grad_body, [*edge_names, "gb", "w", "w2", "gains", "edge"]),
        ],
        dict(
            core=core,
            w=w_fc1,
            b=b_fc1[None, :],
            x=normed_two,
            g=out_low,
            v=w_fc2,
            w2=w_fc12,
            gains=norm_gains,
            gb2=gb2,
            hidden=hidden_one,
            og=out_grad,
            weight=weight_col,
        ),
        half_shapes | dict(edge=shape_of((TILE, width), BF16)),
        dict(
            gb2e=shape_of((TILE, hidden_half), BF16),
            hiddene=shape_of((TILE, width), F32),
            oge=shape_of((TILE, width), BF16),
            weighte=shape_of((TILE, 1), F32),
            sems=pltpu.SemaphoreType.DMA((4,)),
        ),
        scalars=("core",),
        raw=("gb2", "hidden", "og", "weight"),
        chunked=("x", "g", "v"),
    )
    edge_low = swap(edge_low)
    factor = factor_call(group_of_block, counts)
    fast = n == 16
    if fast:
        both = lambda a, b: lax.rem(d // jnp.where(m == 0, a, b), 2).astype(jnp.int32)
        sides = jnp.stack([both(a, b) for a, b in STAGES])
        sides = [sides[k : k + 1] for k in range(4)]
    begin = lambda kept, got: Bucket(sides, *first_split(sides[0], kept, got, factor)) if fast else None
    step = lambda *buckets: [b.step() for b in buckets if fast]
    fc2 = begin(fc2_own, fc2_got)
    fc1 = begin(fc1_own, fc1_got)

    grad_hidden, hidden_low, sums_two = grad_hidden_call(
        gb, gb2, w_fc1, w_fc12, hidden_one, out_grad, weight_col, norm_gains
    )
    pairs = width // TILE // 2
    attn_back = lambda n: functools.partial(attn_bwd_body, pairs=(n, pairs + n), turns=3)
    attn_temps = dict(
        dq=shape_of((ext, 2 * TILE), BF16), dk=shape_of((ext, 2 * TILE), F32), dv=shape_of((ext, 2 * TILE), F32)
    )
    group_shape = shape_of((own, width), BF16)
    grad_context, grad_a, early_own, early_got = fused(
        [
            (gctx_body, ["low", "edge", "wo", "wo2", "g"]),
            (attn_back(0), ["qkv", "g", "col", "row", "out", "dq", "dk", "dv"]),
            (early_grad_body, ["context", "low", "normed", "out", "own", "other"]),
        ],
        dict(
            low=hidden_low,
            edge=edge_low,
            wo=w_out,
            wo2=w_out2,
            qkv=qkv,
            col=seg_col,
            row=seg_row,
            context=context,
            normed=normed,
        ),
        dict(
            g=shape_of((ext, width), BF16),
            out=group_shape,
            own=shape_of((2 * width, half), BF16),
            other=shape_of((2 * width, half), BF16),
        ),
        attn_temps,
    )
    early_got = swap(early_got)
    step(fc2, fc1)
    (grad_b,) = fused(
        [(attn_back(1), ["qkv", "g", "col", "row", "out", "dq", "dk", "dv"])],
        dict(qkv=qkv, g=grad_context, col=seg_col, row=seg_row),
        dict(out=group_shape),
        attn_temps,
    )
    early = begin(early_own, early_got)
    step(fc2, fc1)
    grad_input, vectors, late_own, late_got = fused(
        [
            (attn_back(2), ["qkv", "g", "col", "row", "gc", "dq", "dk", "dv"]),
            (
                grad_tokens_body,
                ["ga", "gb", "gc", "w", "w2", "tokens", "gh", "gains", "two", "s", "s2", "factor", "out", "sums"],
            ),
            (late_grad_body, ["normed", "gb", "gc", "own", "other"]),
        ],
        dict(
            qkv=qkv,
            g=grad_context,
            col=seg_col,
            row=seg_row,
            ga=grad_a,
            gb=grad_b,
            w=w_qkv,
            w2=w_qkv2,
            tokens=tokens,
            gh=grad_hidden,
            gains=norm_gains,
            two=sums_two,
            s=sums,
            s2=sums2,
            factor=factor,
            normed=normed,
        ),
        dict(
            out=shape_of((own, width), F32),
            sums=shape_of((16, width), F32),
            own=shape_of((width, width), BF16),
            other=shape_of((width, width), BF16),
        ),
        dict(gc=group_shape, **attn_temps),
    )
    late_got = swap(late_got)
    vectors = lax.all_gather(vectors, ("dp", "mp"), axis=0, tiled=True)
    step(fc2, fc1)
    if fast:
        early.step(20)
    late = begin(late_own, late_got)
    output = output_call(act, act2, w_fc2, w_fc22, hidden_one, row_biases)
    step(fc2, fc1)
    if fast:
        step(late, early, fc2, fc1)
        step(late, early, fc2, fc1)
        step(late, early, fc2, fc1)
        step(late, early)
        grad_fc2 = last_rows(sides[0], fc2.kept, fc2.got)
        step(late, early)
        grad_fc1 = last_rows(sides[0], fc1.kept, fc1.got)
        step(late, early)
        step(late)
        grad_out, grad_qkv = last_qkv(sides[0], early.kept, early.got, late.kept, late.got)
    else:
        total = lambda kept, got: (kept.astype(F32) + got.astype(F32)) * factor[0, 0]
        grad_fc2 = sum_any(total(fc2_own, fc2_got))
        grad_fc1 = sum_any(total(fc1_own, fc1_got))
        first = total(early_own, early_got).reshape(4, half, half)
        second = total(late_own, late_got)
        grad_out = sum_any(jnp.concatenate([first[0], first[2]], axis=1))
        first = jnp.concatenate([first[1], first[3]])
        part = lambda a, at: a[:, at : at + TILE]
        parts = [
            jnp.concatenate([part(first, t * TILE), part(second, t * TILE), part(second, half + t * TILE)], axis=1)
            for t in range(3)
        ]
        grad_qkv = sum_any(jnp.stack(parts))
    gains, shifts, grad_qv_bias, grad_b_fc1 = vectors_call(core, vectors, half, hidden_half)
    return (
        output,
        grad_input,
        gains,
        shifts,
        grad_qkv,
        grad_qv_bias,
        grad_out,
        grad_fc1,
        grad_b_fc1.reshape(hidden_half),
        grad_fc2,
    )


def solution(mesh):
    placed = (
        P(("dp", "mp"), None),
        P(("dp", "mp"), None),
        P("dp", None),
        P("dp"),
        P(),
        P(),
        P(None, None, "mp"),
        P(None, "mp"),
        P("mp", None),
        P(None, "mp"),
        P("mp"),
        P("mp", None),
    )
    return jax.shard_map(
        local,
        mesh=mesh,
        in_specs=placed,
        out_specs=(
            P(("dp", "mp"), None),
            P(("dp", "mp"), None),
            P(),
            P(),
            P(None, None, "mp"),
            P(None, "mp"),
            P("mp", None),
            P(None, "mp"),
            P("mp"),
            P("mp", None),
        ),
        check_vma=False,
    )
```

```python
import functools

import jax
import jax.numpy as jnp
from jax import lax
from jax.experimental import pallas as pl
from jax.experimental.pallas import tpu as pltpu
from jax.sharding import PartitionSpec as P

TILE = 128
MASKED = -3e38
F32 = jnp.float32
BF16 = jnp.bfloat16

def pick_heads(block):
    lane = lax.broadcasted_iota(jnp.int32, block.shape, 1)
    zero = jnp.zeros_like(block)
    return jnp.concatenate([jnp.where(lane < 64, block, zero), jnp.where(lane < 64, zero, block)], axis=0)

def join_heads(both):
    half = both.shape[1] // 2
    row = lax.broadcasted_iota(jnp.int32, (both.shape[0], half), 0)
    return jnp.where(row < 64, both[:, :half], both[:, half:]).T

def window(tiles, i):
    return [pl.multiple_of(lax.rem(i + step, tiles) * TILE, TILE) for step in (tiles - 1, 0, 1)]

def bias_of(starts, seg_col_ref, seg_row):
    keys = jnp.concatenate([seg_col_ref[pl.ds(s, TILE), :] for s in starts], axis=0)
    bias = jnp.where(keys == seg_row, 0.0, MASKED).astype(F32)
    return jnp.concatenate([bias, bias], axis=1)

def rows_of(ref, starts, cols):
    return jnp.concatenate([ref[pl.ds(s, TILE), cols] for s in starts], axis=0)


HEAD_DIM = 64
GROUPS = 3
LEN_NORM = 64
EPS = 1e-06
GELU_C = 0.7978845608028654
VMEM = pl.BlockSpec(memory_space=pltpu.VMEM)
SMEM = pl.BlockSpec(memory_space=pltpu.SMEM)
HBM = pl.BlockSpec(memory_space=pltpu.MemorySpace.HBM)
ANY = pl.BlockSpec(memory_space=pl.ANY)


def dot(a, b):
    return jnp.dot(a, b, preferred_element_type=F32)


def dot_nt(a, b):
    return lax.dot_general(a, b, (((1,), (1,)), ((), ())), preferred_element_type=F32)


def dot_tn(a, b):
    return lax.dot_general(a, b, (((0,), (0,)), ((), ())), preferred_element_type=F32)


def shape_of(shape, dtype):
    return jax.ShapeDtypeStruct(shape, dtype)


def nbytes(a):
    size = a.dtype.itemsize
    for n in a.shape:
        size *= n
    return size


class Order:
    token = None


CHUNK = 256
FLOPS_A_MICRO = 1_150_000_000


def in_hbm(x):
    return pltpu.with_memory_space_constraint(x, pltpu.MemorySpace.HBM)


def fused(steps, inputs, outs, temps=None, scalars=(), raw=(), chunked=(), free=(), limit=22, ahead=1, micros=10):
    temps = temps or {}
    waits = [a for a in (Order.token,) if a is not None]
    names = list(inputs)
    loaded = [k for k in names if k not in scalars and k not in raw]
    buffers = {k: inputs[k] for k in loaded} | outs | temps
    is_sem = lambda v: not isinstance(v, (jax.Array, jax.ShapeDtypeStruct))
    kinds = [v if is_sem(v) else pltpu.VMEM(v.shape, v.dtype) for v in buffers.values()]
    sem_of, count = {}, 0
    for k in (*loaded, *outs):
        sem_of[k] = count
        count += buffers[k].shape[0] // CHUNK if k in chunked else 1
    first = {k: min(n for n, (_, used) in enumerate(steps) if k in used) for k in loaded}
    last = {k: max(n for n, (_, used) in enumerate(steps) if k in used) for k in outs}

    def body(*refs):
        given = dict(zip(names, refs))
        results = dict(zip(outs, refs[len(names) + len(waits) :]))
        token_ref = refs[len(names) + len(waits) + len(outs)]
        rest = refs[len(names) + len(waits) + len(outs) + 1 :]
        held, sems = dict(zip(buffers, rest)), rest[len(buffers)]
        token_ref[...] = jnp.zeros_like(token_ref)
        place = {k: given[k] for k in (*scalars, *raw)} | held

        def pieces(k, source, target):
            if k not in chunked:
                return [pltpu.make_async_copy(source, target, sems.at[sem_of[k]])]
            rows = [pl.ds(r, CHUNK) for r in range(0, buffers[k].shape[0], CHUNK)]
            return [
                pltpu.make_async_copy(source.at[at], target.at[at], sems.at[sem_of[k] + n]) for n, at in enumerate(rows)
            ]

        loads = {k: pieces(k, given[k], held[k]) for k in loaded}
        stores = {k: pieces(k, held[k], results[k]) for k in outs}

        def start(n):
            mine = [loads[k] for k in loaded if first[k] == n]
            for copies in [c for c in mine if len(c) == 1]:
                copies[0].start()
            for n in range(max([len(c) for c in mine], default=0)):
                for copies in mine:
                    if 1 < len(copies) and n < len(copies):
                        copies[n].start()

        def ready(r, *which):
            for k in which or loaded:
                if k in chunked:
                    loads[k][r // CHUNK].wait()

        def done(r):
            for k in outs:
                if k in chunked:
                    stores[k][r // CHUNK].start()

        for n in range(ahead):
            start(n)
        for n, (fn, used) in enumerate(steps):
            start(n + ahead)
            code = getattr(fn, "__code__", None)
            piecewise = chunked and code is not None and "ready" in code.co_varnames
            hooks = dict(ready=ready, done=done) if piecewise else {}
            for k in loaded:
                if first[k] == n and k not in chunked:
                    loads[k][0].wait()
            fn(*(place[k] for k in used), **hooks)
            for k in outs:
                if last[k] == n and k not in chunked:
                    stores[k][0].start()
        for k in outs:
            for copy in stores[k]:
                copy.wait()

    size = sum(nbytes(v) for v in buffers.values() if not is_sem(v))
    pad = sum(nbytes(v) * 128 for v in buffers.values() if not is_sem(v) and v.shape[-1] == 1)
    kernel = pl.pallas_call(
        body,
        in_specs=[SMEM if k in scalars else ANY if k in free else HBM for k in names] + [ANY] * len(waits),
        out_specs=[HBM] * len(outs) + [VMEM],
        out_shape=[*(pltpu.MemorySpace.HBM(v.shape, v.dtype) for v in outs.values()), shape_of((8, 128), F32)],
        scratch_shapes=[*kinds, pltpu.SemaphoreType.DMA((count,))],
        compiler_params=pltpu.CompilerParams(vmem_limit_bytes=(limit << 20) + size + pad),
        cost_estimate=pl.CostEstimate(flops=micros * FLOPS_A_MICRO + 1, bytes_accessed=1, transcendentals=0),
    )
    operands = [v if k in scalars or k in free else in_hbm(v) for k, v in inputs.items()]
    *results, Order.token = kernel(*operands, *waits)
    return results


def stream(body, args, outs, scalars=0, limit=22, chunked=()):
    named = {f"in{n}": a for n, a in enumerate(args)}
    made = {f"out{n}": a for n, a in enumerate(outs)}
    every = [*named, *made]
    return fused(
        [(body, every)],
        named,
        made,
        scalars=every[:scalars],
        chunked=[every[n] for n in chunked],
        limit=limit,
    )


def call(body, args, outs, scalars=0, limit=22, micros=0):
    outs = list(outs)
    waits = [a for a in (Order.token,) if a is not None]
    n_in, n_wait, n_out = len(args), len(waits), len(outs)

    def tied(*refs):
        token_ref = refs[n_in + n_wait + n_out]
        token_ref[...] = jnp.zeros_like(token_ref)
        body(*refs[:n_in], *refs[n_in + n_wait : n_in + n_wait + n_out])

    *results, Order.token = pl.pallas_call(
        tied,
        in_specs=[SMEM] * scalars + [VMEM] * (n_in - scalars) + [ANY] * n_wait,
        out_specs=[VMEM] * (n_out + 1),
        out_shape=outs + [shape_of((8, 128), F32)],
        compiler_params=pltpu.CompilerParams(vmem_limit_bytes=limit << 20),
        cost_estimate=pl.CostEstimate(
            flops=micros * FLOPS_A_MICRO + 1, bytes_accessed=sum(nbytes(a) for a in [*args, *outs]) // 64, transcendentals=0
        ),
    )(*args, *waits)
    return results


def norm_parts(values):
    center = values - jnp.mean(values, axis=-1, keepdims=True)
    rstd = lax.rsqrt(jnp.mean(center * center, axis=-1, keepdims=True) + EPS)
    return center * rstd, rstd


def norm_back(grad, unit, rstd, gain):
    scaled = grad * gain
    return rstd * (
        scaled
        - jnp.mean(scaled, axis=-1, keepdims=True)
        - unit * jnp.mean(scaled * unit, axis=-1, keepdims=True)
    )


def fold(a):
    return jnp.sum(a.astype(F32), axis=0, keepdims=True)


def prep_body(core_ref, lengths_ref, grad_ref, col_ref, row_ref, len_ref, low_ref):
    ext, own = col_ref.shape[0], len_ref.shape[0]
    slots = lengths_ref.shape[1]
    pad = jnp.zeros((1, 128 - slots), F32)
    lengths = jnp.concatenate([lengths_ref[...].astype(F32), pad], axis=1)
    before = lax.broadcasted_iota(jnp.int32, (128, 128), 0) <= lax.broadcasted_iota(jnp.int32, (128, 128), 1)
    ends = dot(jnp.broadcast_to(lengths, (8, 128)).astype(BF16), jnp.where(before, 1.0, 0.0).astype(BF16))[0:1]
    lane = lax.broadcasted_iota(jnp.int32, (1, 128), 1)
    ends = jnp.where(lane < slots, ends, 1e9)
    row = lax.broadcasted_iota(jnp.int32, (ext, 1), 0)
    core = core_ref[0]
    edge = jnp.where(core == 0, 0, -own - (ext - own))
    position = row + jnp.where(row < own, core * own, edge + core * own)
    past = jnp.where(position.astype(F32) >= ends, 1.0, 0.0)
    segment = jnp.sum(past, axis=1, keepdims=True)
    col_ref[...] = segment
    row_ref[...] = dot_nt(jnp.ones((8, 128), BF16), past.astype(BF16))[0:1]
    hit = jnp.where(segment[:own] == lane.astype(F32), lengths, 0.0)
    length = jnp.sum(hit, axis=1, keepdims=True)
    weight = jnp.where(length > 0, LEN_NORM / jnp.maximum(length, 1.0), 0.0)
    len_ref[...] = weight
    low_ref[...] = (grad_ref[...].astype(F32) * weight).astype(BF16)


def factor_body(group_ref, counts_ref, factor_ref):
    lane = lax.broadcasted_iota(jnp.int32, (1, 128), 1)
    counts = jnp.where(lane < GROUPS, fold(counts_ref[:, :128]) * 0.5, 0.0)
    roots = jnp.sqrt(counts)
    all_images = jnp.sum(counts, axis=1, keepdims=True)
    all_roots = jnp.sum(roots, axis=1, keepdims=True)
    root = jnp.sum(jnp.where(lane == group_ref[0], roots, 0.0), axis=1, keepdims=True)
    factor_ref[...] = jnp.broadcast_to(all_images / (root * all_roots), factor_ref.shape)


def factor_call(group, counts):
    return call(factor_body, (group, counts), [shape_of((8, 128), F32)], scalars=1)[0]


def edge_body(core_ref, other_ref, halo_ref, sem):
    rows = pl.ds(pl.multiple_of(core_ref[0] * (other_ref.shape[0] - TILE), TILE), TILE)
    load = pltpu.make_async_copy(other_ref.at[rows], halo_ref, sem)
    load.start()
    load.wait()


def qkv_body(tokens_ref, halo_ref, gains_ref, biases_ref, w_ref, w2_ref, b_ref, b2_ref, normed_ref, out_ref):
    own, width = tokens_ref.shape
    ext = normed_ref.shape[0]
    for r, ref in [(r, tokens_ref) for r in range(0, own, 256)] + [(own, halo_ref)]:
        n = min(256, ext - r)
        at = 0 if ref is halo_ref else r
        unit, _ = norm_parts(ref[at : at + n, :].astype(F32))
        normed = (unit * gains_ref[0:1, :] + biases_ref[0:1, :]).astype(BF16)
        normed_ref[r : r + n, :] = normed
        for t in range(3):
            weights = jnp.concatenate([w_ref[t], w2_ref[t]], axis=1)
            part = dot(normed, weights)
            if t != 1:
                row = t // 2
                part = part + jnp.concatenate([b_ref[row : row + 1, :], b2_ref[row : row + 1, :]], axis=1)
            out_ref[r : r + n, t * width : (t + 1) * width] = part.astype(BF16)


def out_norm_body(ctx_ref, tok_ref, w_ref, w2_ref, gains_ref, biases_ref, hid_ref, norm_ref):
    weights = jnp.concatenate([w_ref[...], w2_ref[...]], axis=0)
    own = tok_ref.shape[0]
    product = lambda r: dot(ctx_ref[r : r + 256, :], weights)
    ready = product(0)
    for r in range(0, own, 256):
        later = product(r + 256) if r + 256 < own else None
        rows = slice(r, r + 256)
        hidden = tok_ref[rows, :].astype(F32) + ready + biases_ref[2:3, :]
        hid_ref[rows, :] = hidden
        unit, _ = norm_parts(hidden)
        norm_ref[rows, :] = (unit * gains_ref[1:2, :] + biases_ref[1:2, :]).astype(BF16)
        ready = later


def ffn_body(x_ref, g_ref, w_ref, b_ref, v_ref, act_ref, gb_ref, sum_ref, *, ready=None, done=None):
    cols = 256
    hidden = w_ref.shape[1]

    def products(rows, j, first=False):
        if first and ready:
            ready(j, "v")
        v = dot(x_ref[rows, :], w_ref[:, j : j + cols]) + b_ref[:, j : j + cols]
        return v, dot_nt(g_ref[rows, :], v_ref[j : j + cols, :])

    def one(r, first):
        rows = pl.ds(r, 256)
        now = products(rows, 0, first)
        for j in range(0, hidden, cols):
            later = products(rows, j + cols, first) if j + cols < hidden else None
            v, grad = now
            u = v * v
            gate = 0.5 * jnp.tanh(v * (GELU_C + (GELU_C * 0.044715) * u)) + 0.5
            act = v * gate
            act_ref[rows, j : j + cols] = act.astype(BF16)
            slope = gate + act * (1.0 - gate) * (2 * GELU_C + (GELU_C * 6 * 0.044715) * u)
            low = (grad * slope).astype(BF16)
            gb_ref[rows, j : j + cols] = low
            sum_ref[:, j : j + cols] += fold(low)
            now = later

    sum_ref[...] = jnp.zeros_like(sum_ref)
    tiles = x_ref.shape[0] // 256
    start = 0
    if ready:
        ready(0, "x", "g")
        one(0, True)
        for r in range(256, x_ref.shape[0], 256):
            ready(r, "x", "g")
        start = 1

    def body(i, _):
        one(pl.multiple_of(i * 256, 256), False)
        return 0

    lax.fori_loop(start, tiles, body, 0)


def fc2_grad_body(act_ref, low_ref, out_ref):
    def one(i, _):
        rows = pl.ds(pl.multiple_of(i * 256, 256), 256)
        out_ref[rows, :] = dot_tn(act_ref[:, rows], low_ref[...]).astype(BF16)
        return 0

    lax.fori_loop(0, out_ref.shape[0] // 256, one, 0)


def fc1_grad_body(x_ref, gb_ref, out_ref):
    def one(i, _):
        rows = pl.ds(pl.multiple_of(i * 256, 256), 256)
        out_ref[rows, :] = dot_tn(x_ref[:, rows], gb_ref[...]).astype(BF16)
        return 0

    lax.fori_loop(0, out_ref.shape[0] // 256, one, 0)


def early_grad_body(ctx_ref, low_ref, norm_ref, ga_ref, own_ref, other_ref):
    half = own_ref.shape[1]
    own = low_ref.shape[0]
    for h in range(2):
        cols, at = slice(h * half, (h + 1) * half), 2 * h * half
        other_ref[at : at + half, :] = dot_tn(ctx_ref[:, half:], low_ref[:, cols]).astype(BF16)
        own_ref[at : at + half, :] = dot_tn(ctx_ref[:, :half], low_ref[:, cols]).astype(BF16)
        both = dot_tn(norm_ref[:own, cols], ga_ref[...]).astype(BF16)
        own_ref[at + half : at + 2 * half, :] = both[:, :half]
        other_ref[at + half : at + 2 * half, :] = both[:, half:]


def late_grad_body(norm_ref, gb_ref, gc_ref, own_ref, other_ref):
    own, half = gb_ref.shape[0], gb_ref.shape[1] // 2
    for r in range(0, own_ref.shape[0], 256):
        for n, ref in enumerate((gb_ref, gc_ref)):
            both = dot_tn(norm_ref[:own, r : r + 256], ref[...]).astype(BF16)
            own_ref[r : r + 256, n * half : (n + 1) * half] = both[:, :half]
            other_ref[r : r + 256, n * half : (n + 1) * half] = both[:, half:]


def edge_copies(core_ref, sources, targets, sems):
    at = (1 - core_ref[0]) * (sources[0].shape[0] - TILE)
    rows = pl.ds(pl.multiple_of(at, TILE), TILE)
    return [pltpu.make_async_copy(a.at[rows], b, sems.at[n]) for n, (a, b) in enumerate(zip(sources, targets))]


def edge_load_body(core_ref, a_ref, b_ref, c_ref, d_ref, a2_ref, b2_ref, c2_ref, d2_ref, sems):
    for copy in edge_copies(core_ref, (a_ref, b_ref, c_ref, d_ref), (a2_ref, b2_ref, c2_ref, d2_ref), sems):
        copy.start()


def edge_grad_body(
    core_ref, a_ref, b_ref, c_ref, d_ref, a2_ref, hid_ref, og_ref, wr_ref, sems, gb_ref, w_ref, w2_ref, gains_ref, out_ref
):
    for copy in edge_copies(core_ref, (a_ref, b_ref, c_ref, d_ref), (a2_ref, hid_ref, og_ref, wr_ref), sems):
        copy.wait()
    rows = pl.ds(pl.multiple_of((1 - core_ref[0]) * (gb_ref.shape[0] - TILE), TILE), TILE)
    grad = dot_nt(gb_ref[rows, :], w_ref[...]) + dot_nt(a2_ref[...], w2_ref[...])
    unit, rstd = norm_parts(hid_ref[...])
    back = norm_back(grad, unit, rstd, gains_ref[1:2, :])
    out_ref[...] = (back + og_ref[...].astype(F32) * wr_ref[...]).astype(BF16)


def grad_hidden_body(gb_ref, gb2_ref, w_ref, w2_ref, hid_ref, og_ref, wr_ref, gains_ref, gh_ref, low_ref, sums_ref, *, ready, done):
    def product(r):
        ready(r)
        rows = slice(r, r + 256)
        return dot_nt(gb_ref[rows, :], w_ref[...]) + dot_nt(gb2_ref[rows, :], w2_ref[...])

    own = hid_ref.shape[0]
    now, sums = product(0), [0.0] * 4
    for r in range(0, own, 256):
        later = product(r + 256) if r + 256 < own else None
        rows, grad = slice(r, r + 256), now
        unit, rstd = norm_parts(hid_ref[rows, :])
        cot = og_ref[rows, :].astype(F32) * wr_ref[rows, :]
        hidden = norm_back(grad, unit, rstd, gains_ref[1:2, :]) + cot
        gh_ref[rows, :] = hidden
        low_ref[rows, :] = hidden.astype(BF16)
        done(r)
        sums = [a + fold(b) for a, b in zip(sums, (grad * unit, grad, hidden, cot))]
        now = later
    for row, a in enumerate(sums):
        sums_ref[row : row + 1, :] = a


def grad_hidden_call(gb, gb2, w, w2, hidden, out_grad, weight_col, gains):
    rows, width = hidden.shape
    return stream(
        grad_hidden_body,
        (gb, gb2, w, w2, hidden, out_grad, weight_col, gains),
        [shape_of((rows, width), F32), shape_of((rows, width), BF16), shape_of((8, width), F32)],
        chunked=(0, 1, 4, 5, 6, 8, 9),
    )


def gctx_body(x_ref, h_ref, w_ref, w2_ref, out_ref):
    own = x_ref.shape[0]
    for r in range(0, own, 256):
        weights = jnp.concatenate([w_ref[...], w2_ref[...]], axis=0)
        out_ref[r : r + 256, :] = dot_nt(x_ref[r : r + 256, :], weights).astype(BF16)
    weights = jnp.concatenate([w_ref[...], w2_ref[...]], axis=0)
    out_ref[own:, :] = dot_nt(h_ref[...], weights).astype(BF16)


def grad_tokens_body(
    ga_ref, gb_ref, gc_ref, w_ref, w2_ref, tok_ref, gh_ref, gains_ref, two_ref, s_ref, s2_ref, factor_ref, out_ref, sums_ref
):
    factor = factor_ref[0:1, 0:1]
    width = tok_ref.shape[1]
    sums_ref[...] = jnp.zeros_like(sums_ref)
    sums_ref[2:6, :] = two_ref[0:4, :]
    for n, ref in enumerate((s_ref, s2_ref)):
        for r in range(2):
            row = 9 + 2 * n + r
            sums_ref[row : row + 1, :] = ref[:, r * width : (r + 1) * width]
    groups = (ga_ref, gb_ref, gc_ref)

    def product(r):
        grad = jnp.zeros((256, width), F32)
        for n, ref in enumerate(groups):
            cols = slice(n * TILE, (n + 1) * TILE)
            weights = [w[t, :, cols] for w in (w_ref, w2_ref) for t in range(3)]
            grad = grad + dot_nt(ref[r : r + 256, :], jnp.concatenate(weights, axis=1))
        return grad

    own = tok_ref.shape[0]
    now, sums = product(0), [0.0] * 5
    for r in range(0, own, 256):
        later = product(r + 256) if r + 256 < own else None
        rows, grad = slice(r, r + 256), now
        unit, rstd = norm_parts(tok_ref[rows, :].astype(F32))
        out_ref[rows, :] = (norm_back(grad, unit, rstd, gains_ref[0:1, :]) + gh_ref[rows, :]) * factor
        terms = (grad * unit, grad, *(ref[rows, :] for ref in groups))
        sums = [a + fold(b) for a, b in zip(sums, terms)]
        now = later
    for row, a in zip((0, 1, 6, 7, 8), sums):
        sums_ref[row : row + 1, :] = a
    sums_ref[...] = sums_ref[...] * factor


def vectors_body(core_ref, all_ref, gains_ref, shifts_ref, qv_ref, fc1_ref):
    blocks = all_ref.shape[0] // 32
    width = all_ref.shape[1]
    half = qv_ref.shape[1]
    total = all_ref[0:32, :]
    for b in range(1, blocks):
        total = total + all_ref[32 * b : 32 * (b + 1), :]
    mine = jnp.where(core_ref[0] == 0, total[:16], total[16:])
    peer = jnp.where(core_ref[0] == 0, total[16:], total[:16])
    both = mine + peer
    gains_ref[0:1, :] = both[0:1]
    gains_ref[1:2, :] = both[2:3]
    shifts_ref[0:1, :] = both[1:2]
    shifts_ref[1:4, :] = both[3:6]
    for n in range(3):
        both = mine[6 + n : 7 + n, :half] + peer[6 + n : 7 + n, half:]
        for row, t in ((0, 0), (1, 2)):
            qv_ref[row : row + 1, n * TILE : (n + 1) * TILE] = both[:, t * TILE : (t + 1) * TILE]
    for r in range(2):
        fc1_ref[:, r * width : (r + 1) * width] = mine[9 + r : 10 + r] + peer[11 + r : 12 + r]


def vectors_call(core, everything, half, hidden_half):
    width = everything.shape[1]
    return call(
        vectors_body,
        (core, everything),
        [shape_of((2, width), F32), shape_of((4, width), F32), shape_of((2, half), F32), shape_of((1, hidden_half), F32)],
        scalars=1,
    )


def output_body(a_ref, a2_ref, w_ref, w2_ref, hid_ref, biases_ref, out_ref, *, ready, done):
    for r in range(0, hid_ref.shape[0], 256):
        ready(r)
        rows = slice(r, r + 256)
        mlp = dot(a_ref[rows, :], w_ref[...]) + dot(a2_ref[rows, :], w2_ref[...])
        out_ref[rows, :] = (hid_ref[rows, :] + mlp + biases_ref[3:4, :]).astype(BF16)
        done(r)


def output_call(a, a2, w, w2, hidden, biases):
    return stream(
        output_body, (a, a2, w, w2, hidden, biases), [shape_of(hidden.shape, BF16)], chunked=(0, 1, 4, 6)
    )[0]


SCALE = HEAD_DIM ** (-0.5)


def attn_fwd_body(
    core_ref,
    lengths_ref,
    qkv_ref,
    seg_col_ref,
    seg_row_ref,
    normed_ref,
    other_ref,
    gains_ref,
    biases_ref,
    w_ref,
    w2_ref,
    b_ref,
    b2_ref,
    out_ref,
    far_ref,
    wide_ref,
    keys_ref,
    values_ref,
    sem,
):
    own, width = out_ref.shape
    tiles = qkv_ref.shape[0] // TILE

    pairs = width // TILE
    lane = lax.broadcasted_iota(jnp.int32, (TILE, TILE), 1)

    def one(i, _):
        starts = window(tiles, i)
        here = pl.ds(starts[1], TILE)
        bias = bias_of(starts, seg_col_ref, seg_row_ref[:, here])
        cols = lambda t, p: slice(t * width + p * TILE, t * width + (p + 1) * TILE)
        scores, probs = {}, {}
        for step in range(pairs + 2):
            if step < pairs:
                queries = pick_heads(qkv_ref[here, cols(0, step)] * jnp.asarray(SCALE, BF16))
                scores[step] = dot_nt(rows_of(qkv_ref, starts, cols(1, step)), queries) + bias
            p = step - 1
            if 0 <= p < pairs:
                expo = jnp.exp(scores[p] - jnp.max(scores[p], axis=0, keepdims=True))
                probs[p] = (expo * (1.0 / jnp.sum(expo, axis=0, keepdims=True))).astype(BF16)
            p = step - 2
            if 0 <= p < pairs:
                both = dot_tn(probs[p], rows_of(qkv_ref, starts, cols(2, p)))
                out_ref[here, cols(0, p)] = jnp.where(lane < HEAD_DIM, both[:TILE], both[TILE:]).astype(BF16)
        return 0

    lax.fori_loop(0, own // TILE, one, 0)
    total_rows = lax.fori_loop(0, lengths_ref.shape[1], lambda j, n: n + lengths_ref[0, j], jnp.int32(0))
    first_row = core_ref[0] * own

    @pl.when(total_rows < 2 * own - TILE)
    def _():
        load = pltpu.make_async_copy(other_ref, far_ref, sem)
        load.start()
        load.wait()

        @pl.loop(0, own // TILE)
        def _(i):
            rows = pl.ds(pl.multiple_of(i * TILE, TILE), TILE)
            unit, _ = norm_parts(far_ref[rows, :].astype(F32))
            far_ref[rows, :] = (unit * gains_ref[0:1, :] + biases_ref[0:1, :]).astype(BF16)

        key_row = lax.broadcasted_iota(jnp.int32, (2 * own, 1), 0) + first_row
        key_row = jnp.where(key_row >= 2 * own, key_row - 2 * own, key_row)
        wide_ref[...] = jnp.where(key_row >= total_rows, 0.0, MASKED)
        for side, (wide, bias_ref) in enumerate(((w_ref, b_ref), (w2_ref, b2_ref))):
            half = wide.shape[2]

            @pl.loop(0, half // TILE)
            def _(p):
                at = pl.multiple_of(p * TILE, TILE)
                base = pl.multiple_of(side * half + p * TILE, TILE)
                for t, ref in ((1, keys_ref), (2, values_ref)):
                    ref[:own, :] = qkv_ref[:own, pl.ds(pl.multiple_of(t * width + base, TILE), TILE)]
                    part = dot(far_ref[...], wide[t, :, pl.ds(at, TILE)])
                    if t == 2:
                        part = part + bias_ref[1:2, pl.ds(at, TILE)]
                    ref[own:, :] = part.astype(BF16)

                @pl.loop(0, own // TILE)
                def _(i):
                    rows = pl.ds(pl.multiple_of(i * TILE, TILE), TILE)
                    queries = pick_heads(qkv_ref[rows, pl.ds(base, TILE)] * jnp.asarray(SCALE, BF16))
                    scores = dot_nt(keys_ref[...], queries) + wide_ref[...]
                    top = jnp.max(scores, axis=0, keepdims=True)
                    expo = jnp.exp(scores - top)
                    probs = (expo * (1.0 / jnp.sum(expo, axis=0, keepdims=True))).astype(BF16)
                    full = join_heads(dot_tn(values_ref[...], probs)).astype(BF16)
                    row = lax.broadcasted_iota(jnp.int32, (TILE, TILE), 0) + i * TILE + first_row
                    out_ref[rows, pl.ds(base, TILE)] = jnp.where(row >= total_rows, full, out_ref[rows, pl.ds(base, TILE)])


def attn_bwd_body(qkv_ref, g_ref, seg_col_ref, seg_row_ref, out_ref, dq_ref, dk_ref, dv_ref, *, pairs, turns):
    tiles = qkv_ref.shape[0] // TILE
    own, width = out_ref.shape[0], qkv_ref.shape[1] // 3
    dk_ref[...] = jnp.zeros_like(dk_ref)
    dv_ref[...] = jnp.zeros_like(dv_ref)

    def load(starts, here, p):
        cols = lambda t: slice(t * width + p * TILE, t * width + (p + 1) * TILE)
        queries = pick_heads(qkv_ref[here, cols(0)] * jnp.asarray(SCALE, BF16))
        keys, values = rows_of(qkv_ref, starts, cols(1)), rows_of(qkv_ref, starts, cols(2))
        return queries, keys, values, pick_heads(g_ref[here, cols(0)])

    def products(arrays, bias):
        queries, keys, values, grads = arrays
        return dot_nt(keys, queries) + bias, dot_nt(values, grads)

    def softmax_back(scores, grad_probs):
        expo = jnp.exp(scores - jnp.max(scores, axis=0, keepdims=True))
        probs = expo * (1.0 / jnp.sum(expo, axis=0, keepdims=True))
        mean = jnp.sum(probs * grad_probs, axis=0, keepdims=True)
        return probs.astype(BF16), (probs * (grad_probs - mean)).astype(BF16)

    def finish(starts, here, at, arrays, probs, grad_scores):
        queries, keys, _, grads = arrays
        cols = slice(at * TILE, (at + 1) * TILE)
        dv, dk = dot(probs, grads), dot(grad_scores, queries)
        for k, s in enumerate(starts):
            part = slice(k * TILE, (k + 1) * TILE)
            dk_ref[pl.ds(s, TILE), cols] += dk[part]
            dv_ref[pl.ds(s, TILE), cols] += dv[part]
        dq_ref[here, cols] = (join_heads(dot_tn(keys, grad_scores)) * SCALE).astype(BF16)

    def one(i, _):
        work = []
        for turn in range(turns):
            starts = window(tiles, i * turns + turn)
            here = pl.ds(starts[1], TILE)
            bias = bias_of(starts, seg_col_ref, seg_row_ref[:, here])
            work += [(starts, here, bias, at, p) for at, p in enumerate(pairs)]
        first, second = {}, {}
        for step in range(len(work) + 2):
            if step < len(work):
                starts, here, bias, at, p = work[step]
                first[step] = products(load(starts, here, p), bias)
            if 0 <= step - 1 < len(work):
                second[step - 1] = softmax_back(*first.pop(step - 1))
            if 0 <= step - 2 < len(work):
                starts, here, bias, at, p = work[step - 2]
                finish(starts, here, at, load(starts, here, p), *second.pop(step - 2))
        return 0

    lax.fori_loop(0, tiles // turns, one, 0)
    half = len(pairs) * TILE // 2
    for side in range(2):
        cols = slice(side * half, (side + 1) * half)
        base = side * 3 * half
        out_ref[:, base : base + half] = dq_ref[:own, cols]
        out_ref[:, base + half : base + 2 * half] = dk_ref[:own, cols].astype(BF16)
        out_ref[:, base + 2 * half : base + 3 * half] = dv_ref[:own, cols].astype(BF16)


def half_of(side_ref, flip):
    return 1 - side_ref[0] if flip else side_ref[0]


def first_split_body(side_ref, kept_ref, got_ref, factor_ref, send_ref, keep_ref):
    half = keep_ref.shape[0]
    factor = factor_ref[0:1, 0:1]
    total = lambda at: (kept_ref[pl.ds(at, half), :].astype(F32) + got_ref[pl.ds(at, half), :].astype(F32)) * factor
    send_ref[...] = total(pl.multiple_of((1 - side_ref[0]) * half, 16)).astype(BF16)
    keep_ref[...] = total(pl.multiple_of(side_ref[0] * half, 16)).astype(BF16)


def first_split(side, kept, got, factor):
    half, cols = kept.shape[0] // 2, kept.shape[1]
    return call(
        first_split_body,
        (side, kept, got, factor),
        [shape_of((half, cols), BF16)] * 2,
        scalars=1,
    )


def split_two_body(side_ref, kept_ref, got_ref, send_ref, keep_ref):
    half = keep_ref.shape[0]
    total = lambda at: kept_ref[pl.ds(at, half), :].astype(F32) + got_ref[pl.ds(at, half), :].astype(F32)
    send_ref[...] = total(pl.multiple_of((1 - side_ref[0]) * half, 16)).astype(BF16)
    keep_ref[...] = total(pl.multiple_of(side_ref[0] * half, 16)).astype(BF16)


def split_two(side, kept, got, micros=0):
    half, cols = kept.shape[0] // 2, kept.shape[1]
    return call(
        split_two_body,
        (side, kept, got),
        [shape_of((half, cols), BF16)] * 2,
        scalars=1,
        micros=micros,
    )


def add_body(kept_ref, got_ref, out_ref):
    out_ref[...] = (kept_ref[...].astype(F32) + got_ref[...].astype(F32)).astype(BF16)


def add_two(kept, got):
    return call(add_body, (kept, got), [shape_of(kept.shape, BF16)])[0]


def join_body(side_ref, own_ref, got_ref, out_ref):
    half = own_ref.shape[0]
    out_ref[pl.ds(pl.multiple_of(side_ref[0] * half, 16), half), :] = own_ref[...]
    out_ref[pl.ds(pl.multiple_of((1 - side_ref[0]) * half, 16), half), :] = got_ref[...]


def join_two(side, own, got):
    half, cols = own.shape
    return call(join_body, (side, own, got), [shape_of((2 * half, cols), BF16)], scalars=1)[0]


def last_body(side_ref, own_ref, got_ref, out_ref):
    half = own_ref.shape[0]
    for flip, ref in ((False, own_ref), (True, got_ref)):
        out_ref[pl.ds(pl.multiple_of(half_of(side_ref, flip) * half, 16), half), :] = ref[...].astype(F32)


def last_rows(side, own, got):
    rows, cols = own.shape
    return call(last_body, (side, own, got), [shape_of((2 * rows, cols), F32)], scalars=1)[0]


def last_qkv_body(side_ref, a0_ref, a1_ref, b0_ref, b1_ref, wout_ref, wqkv_ref):
    half = wout_ref.shape[0]
    for flip, a_ref, b_ref in ((False, a0_ref, b0_ref), (True, a1_ref, b1_ref)):
        part = pl.ds(pl.multiple_of(half_of(side_ref, flip) * half, 128), half)
        wout_ref[:, part] = a_ref[:half, :].astype(F32)
        for t in range(3):
            wqkv_ref[t, part, :TILE] = a_ref[half:, t * TILE : (t + 1) * TILE].astype(F32)
            for n in range(2):
                at = n * half + t * TILE
                wqkv_ref[t, part, (1 + n) * TILE : (2 + n) * TILE] = b_ref[:, at : at + TILE].astype(F32)


def last_qkv(side, a0, a1, b0, b1):
    half = a0.shape[1]
    return call(
        last_qkv_body,
        (side, a0, a1, b0, b1),
        [shape_of((half, 2 * half), F32), shape_of((3, 2 * half, half), F32)],
        scalars=1,
    )


def swap(x):
    return lax.ppermute(x, "mp", [(0, 1), (1, 0)])


def exchange(x, bits, n):
    pairs = [(2 * d + m, 2 * (d ^ bits[m]) + m) for d in range(n) for m in range(2)]
    return lax.ppermute(x, ("dp", "mp"), pairs)


def sum_any(part):
    n = lax.axis_size("dp")
    shape = part.shape
    part = part.reshape(-1, shape[-1])
    if n & (n - 1) or part.shape[0] % n:
        return lax.psum(part, "dp").reshape(shape)
    d = lax.axis_index("dp")
    bits = [1 << k for k in range(n.bit_length() - 1)]
    for bit in bits:
        half = part.shape[0] // 2
        side = lax.rem(d // bit, 2)
        sent = lax.dynamic_slice_in_dim(part, (1 - side) * half, half).astype(BF16)
        kept = lax.dynamic_slice_in_dim(part, side * half, half)
        part = kept + exchange(sent, (bit, bit), n).astype(F32)
    total = part.astype(BF16)
    for bit in reversed(bits):
        side = lax.rem(d // bit, 2)
        got = exchange(total, (bit, bit), n)
        total = jnp.concatenate([jnp.where(side == 0, total, got), jnp.where(side == 0, got, total)], axis=0)
    return total.astype(F32).reshape(shape)


STAGES = ((1, 2), (2, 1), (4, 4), (8, 8))


class Bucket:
    def __init__(self, sides, sent, kept):
        self.sides, self.at, self.kept = sides, 0, kept
        self.got = exchange(sent, STAGES[0], 16)

    def step(self, micros=0):
        self.at += 1
        if self.at < 4:
            sent, self.kept = split_two(self.sides[self.at], self.kept, self.got, micros)
            self.got = exchange(sent, STAGES[self.at], 16)
        elif self.at == 4:
            self.kept = add_two(self.kept, self.got)
            self.got = exchange(self.kept, STAGES[3], 16)
        else:
            stage = 8 - self.at
            self.kept = join_two(self.sides[stage], self.kept, self.got)
            self.got = exchange(self.kept, STAGES[stage - 1], 16)


def local(
    tokens,
    out_grad,
    image_lengths,
    group_of_block,
    norm_gains,
    row_biases,
    w_qkv,
    qv_bias,
    w_out,
    w_fc1,
    b_fc1,
    w_fc2,
):
    own, width = tokens.shape
    half = w_qkv.shape[2]
    hidden_half = w_fc1.shape[1]
    row_count = own * 2
    n = lax.axis_size("dp")
    d, m = lax.axis_index("dp"), lax.axis_index("mp")
    Order.token = None

    tokens_other = swap(tokens)
    w_qkv2 = swap(w_qkv)
    qv_bias2 = swap(qv_bias)
    late_swap = lambda x: swap(lax.optimization_barrier((x, w_qkv2, tokens_other))[0])
    w_out2 = late_swap(w_out)
    w_fc12 = late_swap(w_fc1)
    w_fc22 = late_swap(w_fc2)
    b_fc12 = late_swap(b_fc1[None, :])

    core = m.astype(jnp.int32).reshape(1)
    ext = own + TILE
    images = jnp.sum((image_lengths > 0).astype(F32))
    lane = lax.broadcasted_iota(jnp.int32, (16, width), 1)
    row = lax.broadcasted_iota(jnp.int32, (16, width), 0)
    counts = jnp.where((row == 0) & (lane == group_of_block[0]), images, 0.0)
    counts = lax.all_gather(counts, ("dp", "mp"), axis=0, tiled=True)

    seg_col, seg_row, weight_col, out_low, normed, qkv, context = fused(
        [
            (prep_body, ["core", "lens", "og", "col", "row", "weight", "low"]),
            (edge_body, ["core", "other", "halo", "sem"]),
            (qkv_body, ["tokens", "halo", "gains", "biases", "w", "w2", "b", "b2", "normed", "qkv"]),
            (
                attn_fwd_body,
                ["core", "lengths", "qkv", "col", "row", "normed", "other", "gains", "biases"]
                + ["w", "w2", "b", "b2", "context", "far", "wide", "keys", "values", "sem"],
            ),
        ],
        dict(
            core=core,
            lengths=image_lengths,
            lens=image_lengths,
            og=out_grad,
            tokens=tokens,
            gains=norm_gains,
            biases=row_biases,
            w=w_qkv,
            w2=w_qkv2,
            b=qv_bias,
            b2=qv_bias2,
            other=tokens_other,
        ),
        dict(
            col=shape_of((ext, 1), F32),
            row=shape_of((1, ext), F32),
            weight=shape_of((own, 1), F32),
            low=shape_of((own, width), BF16),
            normed=shape_of((ext, width), BF16),
            qkv=shape_of((ext, 3 * width), BF16),
            context=shape_of((own, width), BF16),
        ),
        dict(
            halo=shape_of((TILE, width), BF16),
            far=shape_of((own, width), BF16),
            wide=shape_of((row_count, 1), F32),
            keys=shape_of((row_count, TILE), BF16),
            values=shape_of((row_count, TILE), BF16),
            sem=pltpu.SemaphoreType.DMA,
        ),
        scalars=("core", "lengths"),
        raw=("other",),
        free=("other", "w2", "b2"),
        ahead=3,
    )
    half_shapes = dict(
        act=shape_of((own, hidden_half), BF16),
        gb=shape_of((own, hidden_half), BF16),
        sums=shape_of((1, hidden_half), F32),
        grad2=shape_of((hidden_half, width), BF16),
        grad1=shape_of((width, hidden_half), BF16),
    )
    half_steps = [
        (ffn_body, ["x", "g", "w", "b", "v", "act", "gb", "sums"]),
        (fc2_grad_body, ["act", "g", "grad2"]),
        (fc1_grad_body, ["x", "gb", "grad1"]),
    ]
    hidden_one, normed_two, act2, gb2, sums2, fc2_got, fc1_got = fused(
        [(out_norm_body, ["context", "tokens", "wo", "wo2", "gains", "biases", "hidden", "x"]), *half_steps],
        dict(
            context=context,
            tokens=tokens,
            wo=w_out,
            wo2=w_out2,
            gains=norm_gains,
            biases=row_biases,
            g=out_low,
            w=w_fc12,
            b=b_fc12,
            v=w_fc22,
        ),
        dict(hidden=shape_of((own, width), F32), x=shape_of((own, width), BF16), **half_shapes),
    )
    fc2_got = swap(fc2_got)
    fc1_got = swap(fc1_got)
    edge_names = ["core", "gb2", "hidden", "og", "weight", "gb2e", "hiddene", "oge", "weighte", "sems"]
    act, gb, sums, fc2_own, fc1_own, edge_low = fused(
        [
            half_steps[0],
            (edge_load_body, edge_names),
            *half_steps[1:],
            (edge_grad_body, [*edge_names, "gb", "w", "w2", "gains", "edge"]),
        ],
        dict(
            core=core,
            w=w_fc1,
            b=b_fc1[None, :],
            x=normed_two,
            g=out_low,
            v=w_fc2,
            w2=w_fc12,
            gains=norm_gains,
            gb2=gb2,
            hidden=hidden_one,
            og=out_grad,
            weight=weight_col,
        ),
        half_shapes | dict(edge=shape_of((TILE, width), BF16)),
        dict(
            gb2e=shape_of((TILE, hidden_half), BF16),
            hiddene=shape_of((TILE, width), F32),
            oge=shape_of((TILE, width), BF16),
            weighte=shape_of((TILE, 1), F32),
            sems=pltpu.SemaphoreType.DMA((4,)),
        ),
        scalars=("core",),
        raw=("gb2", "hidden", "og", "weight"),
        chunked=("x", "g", "v"),
    )
    edge_low = swap(edge_low)
    factor = factor_call(group_of_block, counts)
    fast = n == 16
    if fast:
        both = lambda a, b: lax.rem(d // jnp.where(m == 0, a, b), 2).astype(jnp.int32)
        sides = jnp.stack([both(a, b) for a, b in STAGES])
        sides = [sides[k : k + 1] for k in range(4)]
    begin = lambda kept, got: Bucket(sides, *first_split(sides[0], kept, got, factor)) if fast else None
    step = lambda *buckets: [b.step() for b in buckets if fast]
    fc2 = begin(fc2_own, fc2_got)
    fc1 = begin(fc1_own, fc1_got)

    grad_hidden, hidden_low, sums_two = grad_hidden_call(
        gb, gb2, w_fc1, w_fc12, hidden_one, out_grad, weight_col, norm_gains
    )
    pairs = width // TILE // 2
    attn_back = lambda n: functools.partial(attn_bwd_body, pairs=(n, pairs + n), turns=3)
    attn_temps = dict(
        dq=shape_of((ext, 2 * TILE), BF16), dk=shape_of((ext, 2 * TILE), F32), dv=shape_of((ext, 2 * TILE), F32)
    )
    group_shape = shape_of((own, width), BF16)
    grad_context, grad_a, early_own, early_got = fused(
        [
            (gctx_body, ["low", "edge", "wo", "wo2", "g"]),
            (attn_back(0), ["qkv", "g", "col", "row", "out", "dq", "dk", "dv"]),
            (early_grad_body, ["context", "low", "normed", "out", "own", "other"]),
        ],
        dict(
            low=hidden_low,
            edge=edge_low,
            wo=w_out,
            wo2=w_out2,
            qkv=qkv,
            col=seg_col,
            row=seg_row,
            context=context,
            normed=normed,
        ),
        dict(
            g=shape_of((ext, width), BF16),
            out=group_shape,
            own=shape_of((2 * width, half), BF16),
            other=shape_of((2 * width, half), BF16),
        ),
        attn_temps,
    )
    early_got = swap(early_got)
    step(fc2, fc1)
    (grad_b,) = fused(
        [(attn_back(1), ["qkv", "g", "col", "row", "out", "dq", "dk", "dv"])],
        dict(qkv=qkv, g=grad_context, col=seg_col, row=seg_row),
        dict(out=group_shape),
        attn_temps,
    )
    early = begin(early_own, early_got)
    step(fc2, fc1)
    grad_input, vectors, late_own, late_got = fused(
        [
            (attn_back(2), ["qkv", "g", "col", "row", "gc", "dq", "dk", "dv"]),
            (
                grad_tokens_body,
                ["ga", "gb", "gc", "w", "w2", "tokens", "gh", "gains", "two", "s", "s2", "factor", "out", "sums"],
            ),
            (late_grad_body, ["normed", "gb", "gc", "own", "other"]),
        ],
        dict(
            qkv=qkv,
            g=grad_context,
            col=seg_col,
            row=seg_row,
            ga=grad_a,
            gb=grad_b,
            w=w_qkv,
            w2=w_qkv2,
            tokens=tokens,
            gh=grad_hidden,
            gains=norm_gains,
            two=sums_two,
            s=sums,
            s2=sums2,
            factor=factor,
            normed=normed,
        ),
        dict(
            out=shape_of((own, width), F32),
            sums=shape_of((16, width), F32),
            own=shape_of((width, width), BF16),
            other=shape_of((width, width), BF16),
        ),
        dict(gc=group_shape, **attn_temps),
    )
    late_got = swap(late_got)
    vectors = lax.all_gather(vectors, ("dp", "mp"), axis=0, tiled=True)
    step(fc2, fc1)
    if fast:
        early.step(20)
    late = begin(late_own, late_got)
    output = output_call(act, act2, w_fc2, w_fc22, hidden_one, row_biases)
    step(fc2, fc1)
    if fast:
        step(late, early, fc2, fc1)
        step(late, early, fc2, fc1)
        step(late, early, fc2, fc1)
        step(late, early)
        grad_fc2 = last_rows(sides[0], fc2.kept, fc2.got)
        step(late, early)
        grad_fc1 = last_rows(sides[0], fc1.kept, fc1.got)
        step(late, early)
        step(late)
        grad_out, grad_qkv = last_qkv(sides[0], early.kept, early.got, late.kept, late.got)
    else:
        total = lambda kept, got: (kept.astype(F32) + got.astype(F32)) * factor[0, 0]
        grad_fc2 = sum_any(total(fc2_own, fc2_got))
        grad_fc1 = sum_any(total(fc1_own, fc1_got))
        first = total(early_own, early_got).reshape(4, half, half)
        second = total(late_own, late_got)
        grad_out = sum_any(jnp.concatenate([first[0], first[2]], axis=1))
        first = jnp.concatenate([first[1], first[3]])
        part = lambda a, at: a[:, at : at + TILE]
        parts = [
            jnp.concatenate([part(first, t * TILE), part(second, t * TILE), part(second, half + t * TILE)], axis=1)
            for t in range(3)
        ]
        grad_qkv = sum_any(jnp.stack(parts))
    gains, shifts, grad_qv_bias, grad_b_fc1 = vectors_call(core, vectors, half, hidden_half)
    return (
        output,
        grad_input,
        gains,
        shifts,
        grad_qkv,
        grad_qv_bias,
        grad_out,
        grad_fc1,
        grad_b_fc1.reshape(hidden_half),
        grad_fc2,
    )


def solution(mesh):
    placed = (
        P(("dp", "mp"), None),
        P(("dp", "mp"), None),
        P("dp", None),
        P("dp"),
        P(),
        P(),
        P(None, None, "mp"),
        P(None, "mp"),
        P("mp", None),
        P(None, "mp"),
        P("mp"),
        P("mp", None),
    )
    return jax.shard_map(
        local,
        mesh=mesh,
        in_specs=placed,
        out_specs=(
            P(("dp", "mp"), None),
            P(("dp", "mp"), None),
            P(),
            P(),
            P(None, None, "mp"),
            P(None, "mp"),
            P("mp", None),
            P(None, "mp"),
            P("mp"),
            P("mp", None),
        ),
        check_vma=False,
    )
```
